256 devices in a mesh: pair: 2 (over core), lat: 8 (over y, x_hi), lon: 16 (over z, x_lo).
Axes of the slice: x: 4 (x_hi: 2, x_lo: 2; x = x_hi * 2 + x_lo), y: 4, z: 8, core: 2. Of those that a mesh axis runs over, the one named last changes fastest.
Arguments:
- wave_states: bfloat16 [8, 4, 1536, 7168], P('pair', None, 'lat', 'lon'), may hold values from -6 to 6
- pair_list: int32 [8, 2], replicated, may hold values from 0 to 255
- pair_counts: int32 [2], replicated, may hold values from 0 to 4, as said below
- residuals: float32 [8, 4], replicated, may hold values from -6 to 6
- station_cell: int32 [256], replicated, may hold values from 0 to 11010047
- source_wavelet: float32 [4], replicated, may hold values from -6 to 6
- lat_faces: float32 [1536, 7168], P('lat', 'lon'), may hold values from 0.05 to 0.25
- lon_faces: float32 [1536, 7168], P('lat', 'lon'), may hold values from 0.05 to 0.25
Outputs:
- power_kernel: float32 [1536, 7168], P('lat', 'lon')
The draws below stay inside these ranges and needn't reach their ends.
Inputs may be any that keep to these rules, and one draw needn't show every extreme that they name: `pair_counts`: slots at and beyond an index's count are unused. One index of pair holds 4 live slots in every draw.
All inputs are finite; a program needn't handle non-finite values.
Results may differ from the reference program's by a relative error of at most 0.0003.
Values may be sent and summed in bfloat16 or wider, within the bound.
A program may use at most 64 MiB of HBM per device.

```python
import math
import jax
import jax.numpy as jnp
from jax import lax

SLOTS = 4
STEPS = 4
NSTAT = 256
NLAT = 1536
NLON = 7168
PAIRS = 8
N_PAIR = 2


def draw_pair_counts(key, part):
    low_key = jax.random.fold_in(key, 11)
    side_key = jax.random.fold_in(key, 23)
    lighter = jax.random.randint(low_key, (), 0, SLOTS // 4 + 1)
    busiest = jax.random.randint(side_key, (), 0, N_PAIR)
    indices = jnp.arange(N_PAIR, dtype=jnp.int32)
    return jnp.where(indices == busiest, jnp.int32(SLOTS), lighter.astype(jnp.int32)).astype(jnp.int32)


def with_ends(array, key, smallest, top_value):
    shape = array.shape
    place = [jax.random.randint(jax.random.fold_in(key, axis), (), 0, shape[axis]) for axis in range(len(shape))]
    array = array.at[tuple(place)].set(smallest)
    longest = shape.index(max(shape))
    place[longest] = (place[longest] + 1) % shape[longest]
    return array.at[tuple(place)].set(top_value)


def level_of(rng, shape, pieces, low, high):
    loudness, own = 1.0, jax.random.fold_in(rng, 6)
    for axis_at, parts in pieces:
        heights = jnp.exp(jax.random.uniform(jax.random.fold_in(own, axis_at), (parts,), jnp.float32, low / len(pieces), high / len(pieces)))
        loudness = loudness * jnp.repeat(heights, shape[axis_at] // parts).reshape([-1 if axis == axis_at else 1 for axis in range(len(shape))])
    return loudness


def normal_values(rng, shape, width, bound, pieces=(), kind=jnp.bfloat16):
    loudness = level_of(rng, shape, pieces, -0.22, 0.18) if pieces else 1.0
    result = jax.random.normal(rng, shape, jnp.float32) * width * loudness
    return jnp.minimum(jnp.maximum(result, -bound), bound).astype(kind)


def setup_inputs(seed: int = 0) -> dict:
    splits = jax.random.split(jax.random.key(seed), 9)
    return {
        "wave_states": normal_values(splits[0], (PAIRS, 4, NLAT, NLON), 1.0, 6.0, ((0, 2), (2, 8), (3, 16))),
        "pair_list": with_ends(jax.random.randint(splits[1], (PAIRS, 2), 0, NSTAT), jax.random.fold_in(splits[1], 1), 0, NSTAT - 1).astype(jnp.int32),
        "pair_counts": draw_pair_counts(jax.random.fold_in(splits[8], 71), 0),
        "residuals": normal_values(splits[3], (PAIRS, STEPS), 1.0, 6.0, (), jnp.float32),
        "station_cell": with_ends(jax.random.randint(splits[4], (NSTAT,), 0, NLAT * NLON), jax.random.fold_in(splits[4], 1), 0, (NLAT * NLON) - 1).astype(jnp.int32),
        "source_wavelet": normal_values(splits[5], (STEPS,), 1.0, 6.0, (), jnp.float32),
        "lat_faces": jnp.clip(jnp.exp(math.log(0.25) - 1.609438 * jax.random.uniform(splits[6], (NLAT, NLON), jnp.float32) ** level_of(splits[6], (NLAT, NLON), ((0, 8), (1, 16)), -0.2, 0.2)), 0.05, 0.25),
        "lon_faces": jnp.clip(jnp.exp(math.log(0.25) - 1.609438 * jax.random.uniform(splits[7], (NLAT, NLON), jnp.float32) ** level_of(splits[7], (NLAT, NLON), ((0, 8), (1, 16)), -0.2, 0.2)), 0.05, 0.25),
    }


def membrane(field, north, above, lon_faces, left):
    zero_row = jnp.zeros_like(field[:, :1])
    below_vals = jnp.concatenate([field[:, 1:], zero_row], axis=1)
    above_vals = jnp.concatenate([zero_row, field[:, :-1]], axis=1)
    right_vals = jnp.roll(field, -1, axis=2)
    left_vals = jnp.roll(field, 1, axis=2)
    return north * (below_vals - field) + above * (above_vals - field) + lon_faces * (right_vals - field) + left * (left_vals - field)


def reference(wave_states, pair_list, pair_counts, residuals, station_cell, source_wavelet, lat_faces, lon_faces):
    nlat, nlon = lat_faces.shape
    row_ids = jnp.arange(nlat, dtype=jnp.int32)
    north = jnp.where(row_ids[:, None] == nlat - 1, jnp.zeros_like(lat_faces), lat_faces)
    above = jnp.concatenate([jnp.zeros((1, nlon), lat_faces.dtype), north[:-1]], axis=0)
    left = jnp.roll(lon_faces, 1, axis=1)
    component = jnp.arange(2, dtype=jnp.int32)

    def one_slot(kernel, position):
        fields = lax.dynamic_index_in_dim(wave_states, position, 0, keepdims=False).astype(jnp.float32)
        active = ((position % SLOTS) < pair_counts[position // SLOTS]).astype(jnp.float32)
        station_cells = station_cell[pair_list[position]]
        earlier = fields[0:2]
        current = fields[2:4]
        for moment in range(STEPS):
            amplitudes = jnp.stack([source_wavelet[moment], residuals[position, STEPS - 1 - moment]])
            source = jnp.zeros((2, nlat * nlon), jnp.float32).at[component, station_cells].add(amplitudes).reshape(2, nlat, nlon)
            following = 2.0 * current - earlier + membrane(current, north, above, lon_faces, left) + source
            kernel = kernel + active * following[0] * following[1]
            earlier, current = current, following
        return kernel, None

    kernel, _ = lax.scan(one_slot, jnp.zeros((nlat, nlon), jnp.float32), jnp.arange(pair_list.shape[0], dtype=jnp.int32))
    return kernel
```

```python
import functools

import jax
import jax.numpy as jnp
from jax import lax
from jax.experimental import pallas as pl
from jax.experimental.pallas import tpu as pltpu
from jax.sharding import PartitionSpec as P

HALO = 4
TOP = 16
COLS = 512
STRIP = 8
MESH = pl.DeviceIdType.MESH


def exchange_kernel(send_l, send_r, top_rows, bot_rows, out_l, out_r, out_a, out_b, rl, rr, ra, rb, st, sb, send_sem, recv_sem):
    nlon = lax.axis_size("lon")
    nlat = lax.axis_size("lat")
    me_lat = lax.axis_index("lat")
    me_lon = lax.axis_index("lon")
    right = lax.rem(me_lon + 1, nlon)
    left = lax.rem(me_lon + nlon - 1, nlon)
    has_up = me_lat > 0
    has_down = me_lat < nlat - 1
    up = jnp.maximum(me_lat - 1, 0)
    down = jnp.minimum(me_lat + 1, nlat - 1)

    barrier = pltpu.get_barrier_semaphore()
    pl.semaphore_signal(barrier, 1, device_id={"lon": left}, device_id_type=MESH)
    pl.semaphore_signal(barrier, 1, device_id={"lon": right}, device_id_type=MESH)

    @pl.when(has_up)
    def _():
        pl.semaphore_signal(barrier, 1, device_id={"lat": up}, device_id_type=MESH)

    @pl.when(has_down)
    def _():
        pl.semaphore_signal(barrier, 1, device_id={"lat": down}, device_id_type=MESH)

    pl.semaphore_wait(barrier, 2 + has_up.astype(jnp.int32) + has_down.astype(jnp.int32))

    to_right = pltpu.make_async_remote_copy(send_r, rl, send_sem.at[0], recv_sem.at[0], device_id={"lon": right}, device_id_type=MESH)
    to_left = pltpu.make_async_remote_copy(send_l, rr, send_sem.at[1], recv_sem.at[1], device_id={"lon": left}, device_id_type=MESH)
    to_right.start()
    to_left.start()
    to_right.wait()
    to_left.wait()

    lane = lax.broadcasted_iota(jnp.int32, (STRIP, 128), 1)
    east_gap = (lane >= 64) & (lane < 64 + HALO)
    west_gap = lane >= 128 - HALO
    rows = rl.shape[0]
    for dst, src, first in ((st, top_rows, 0), (sb, bot_rows, rows - STRIP)):
        dst[...] = src[...]
        from_r = rr[pl.ds(first, STRIP), :]
        from_l = rl[pl.ds(first, STRIP), :]
        for a in range(src.shape[0]):
            hr = pltpu.roll(from_r, (64 - HALO * a) % 128, 1)
            hl = pltpu.roll(from_l, (128 - HALO - HALO * a) % 128, 1)
            tail = dst[a, :, pl.ds(384, 128)]
            dst[a, :, pl.ds(384, 128)] = jnp.where(east_gap, hr, jnp.where(west_gap, hl, tail))

    def upward():
        return pltpu.make_async_remote_copy(st, rb, send_sem.at[2], recv_sem.at[2], device_id={"lat": up}, device_id_type=MESH)

    def downward():
        return pltpu.make_async_remote_copy(sb, ra, send_sem.at[3], recv_sem.at[3], device_id={"lat": down}, device_id_type=MESH)

    @pl.when(has_up)
    def _():
        upward().start()

    @pl.when(has_down)
    def _():
        downward().start()

    @pl.when(has_up)
    def _():
        upward().wait_send()
        downward().wait_recv()

    @pl.when(has_down)
    def _():
        downward().wait_send()
        upward().wait_recv()

    @pl.when(jnp.logical_not(has_up))
    def _():
        ra[...] = jnp.zeros_like(ra)

    @pl.when(jnp.logical_not(has_down))
    def _():
        rb[...] = jnp.zeros_like(rb)

    out_l[...] = rl[...]
    out_r[...] = rr[...]
    out_a[...] = ra[...]
    out_b[...] = rb[...]


def exchange(send_l, send_r, top_rows, bot_rows):
    vmem = pl.BlockSpec(memory_space=pltpu.VMEM)
    shapes = [jax.ShapeDtypeStruct(x.shape, x.dtype) for x in (send_l, send_r, top_rows, bot_rows)]
    return pl.pallas_call(
        exchange_kernel,
        out_shape=shapes,
        in_specs=[vmem] * 4,
        out_specs=[vmem] * 4,
        scratch_shapes=[
            pltpu.VMEM(send_l.shape, jnp.float32),
            pltpu.VMEM(send_l.shape, jnp.float32),
            pltpu.VMEM(top_rows.shape, jnp.float32),
            pltpu.VMEM(top_rows.shape, jnp.float32),
            pltpu.VMEM(top_rows.shape, jnp.float32),
            pltpu.VMEM(top_rows.shape, jnp.float32),
            pltpu.SemaphoreType.DMA((4,)),
            pltpu.SemaphoreType.DMA((4,)),
        ],
        compiler_params=pltpu.CompilerParams(collective_id=0, has_side_effects=True),
    )(send_l, send_r, top_rows, bot_rows)


def wave_kernel(
    height,
    breadth,
    nlon,
    pl_ref,
    pc_ref,
    res_ref,
    sc_ref,
    wav_ref,
    f_ref,
    north_ref,
    east_ref,
    from_l,
    from_r,
    from_a,
    from_b,
    o_ref,
    cn,
    ca,
    ce,
    cw,
    cd,
    acc,
    bufs,
    halo,
):
    s = pl.program_id(0)
    rows = cn.shape[0]
    steps = wav_ref.shape[0]
    slots = pl.num_programs(0)
    fields = f_ref.shape[1]
    lane = lax.broadcasted_iota(jnp.int32, (height, 128), 1)

    def assemble(dst, raw, a):
        dst[pl.ds(TOP, height), pl.ds(0, breadth)] = raw
        tail = dst[pl.ds(TOP, height), pl.ds(384, 128)]
        dst[pl.ds(TOP, height), pl.ds(384, 128)] = jnp.where(lane < breadth - 384, tail, halo[a])
        dst[pl.ds(TOP - STRIP, STRIP), :] = from_a[a]
        dst[pl.ds(TOP + height, STRIP), :] = from_b[a]
        dst[pl.ds(0, TOP - STRIP), :] = jnp.zeros((TOP - STRIP, COLS), jnp.float32)
        dst[pl.ds(TOP + height + STRIP, rows - TOP - height - STRIP), :] = jnp.zeros(
            (rows - TOP - height - STRIP, COLS), jnp.float32
        )

    @pl.when(s == 0)
    def _():
        fr = from_r[...]
        fl = from_l[...]
        east_gap = (lane >= breadth - 384) & (lane < breadth - 384 + HALO)
        west_gap = lane >= 128 - HALO
        for a in range(halo.shape[0]):
            hr = pltpu.roll(fr, (breadth - 384 - HALO * a) % 128, 1)
            hl = pltpu.roll(fl, (128 - HALO - HALO * a) % 128, 1)
            halo[a] = jnp.where(east_gap, hr, jnp.where(west_gap, hl, jnp.float32(0.0)))
        coef_base = slots * fields
        assemble(cn, north_ref[...], coef_base)
        assemble(ce, east_ref[...], coef_base + 1)

        @pl.when(lax.axis_index("lat") == lax.axis_size("lat") - 1)
        def _():
            last = TOP + height - 8
            sub8 = lax.broadcasted_iota(jnp.int32, (8, COLS), 0)
            cn[pl.ds(last, 8), :] = jnp.where(sub8 == 7, jnp.float32(0.0), cn[pl.ds(last, 8), :])

        zero8 = jnp.zeros((8, COLS), jnp.float32)
        ca[pl.ds(8, rows - 16), :] = cn[pl.ds(7, rows - 16), :]
        ca[pl.ds(0, 8), :] = zero8
        ca[pl.ds(rows - 8, 8), :] = zero8
        cw[...] = pltpu.roll(ce[...], 1, 1)
        cd[...] = 2.0 - (cn[...] + ca[...] + ce[...] + cw[...])
        acc[...] = jnp.zeros_like(acc)

    member = lax.axis_index("pair")
    row_first = lax.axis_index("lat") * height
    col_first = lax.axis_index("lon") * breadth
    slot = member * slots + s
    act = jnp.where(s < pc_ref[member], jnp.float32(1.0), jnp.float32(0.0))

    places = []
    for comp in range(2):
        cell = sc_ref[pl_ref[slot * 2 + comp]]
        r = lax.div(cell, nlon)
        c = cell - r * nlon
        rb = r - row_first + TOP
        d = c - col_first
        d = jnp.where(d < 0, d + nlon, d)
        near = d < breadth + HALO
        wrap = d >= nlon - HALO
        cb = jnp.where(near, d, d - nlon + COLS)
        valid = (rb >= TOP - HALO) & (rb < TOP + height + HALO) & (near | wrap)
        places.append((rb, cb, valid))

    for comp in range(2):
        assemble(bufs.at[comp, 0], f_ref[0, comp].astype(jnp.float32), s * fields + comp)
        assemble(bufs.at[comp, 1], f_ref[0, 2 + comp].astype(jnp.float32), s * fields + 2 + comp)

    sub = lax.broadcasted_iota(jnp.int32, (8, COLS), 0)
    lane8 = lax.broadcasted_iota(jnp.int32, (8, COLS), 1)
    blocks = rows // 8

    for t in range(steps):
        ei, ci, ni = t % 3, (t + 1) % 3, (t + 2) % 3
        for comp in range(2):
            rb, cb, valid = places[comp]
            amp = wav_ref[t] if comp == 0 else res_ref[slot * steps + steps - 1 - t]

            @pl.when(valid)
            def _():
                r8 = pl.multiple_of(lax.div(rb, 8) * 8, 8)
                slab = bufs[comp, ei, pl.ds(r8, 8), :]
                hit = (sub == rb - r8) & (lane8 == cb)
                bufs[comp, ei, pl.ds(r8, 8), :] = slab - jnp.where(hit, amp, jnp.float32(0.0))

        last = t == steps - 1
        first_block, end_block = (2, blocks - 2) if last else (1, blocks - 1)
        for k in range(first_block, end_block):
            r0 = 8 * k
            dd = cd[pl.ds(r0, 8), :]
            nn = cn[pl.ds(r0, 8), :]
            aa = ca[pl.ds(r0, 8), :]
            ee = ce[pl.ds(r0, 8), :]
            ww = cw[pl.ds(r0, 8), :]
            outs = []
            for comp in range(2):
                cur = bufs[comp, ci, pl.ds(r0, 8), :]
                above = bufs[comp, ci, pl.ds(r0 - 1, 8), :]
                below = bufs[comp, ci, pl.ds(r0 + 1, 8), :]
                ear = bufs[comp, ei, pl.ds(r0, 8), :]
                west = pltpu.roll(cur, 1, 1)
                east = pltpu.roll(cur, COLS - 1, 1)
                nxt = dd * cur + nn * below + aa * above + ee * east + ww * west - ear
                bufs[comp, ni, pl.ds(r0, 8), :] = nxt
                outs.append(nxt)
            if 2 <= k < blocks - 2:
                acc[pl.ds(r0 - TOP, 8), :] += (outs[0] * act) * outs[1]

    @pl.when(s == slots - 1)
    def _():
        o_ref[...] = acc[:, pl.ds(0, breadth)]


def propagate(wave_states, lat_faces, lon_faces, halos, scalars, nlon):
    slots, fields, height, breadth = wave_states.shape
    rows = height + 2 * TOP
    smem = pl.BlockSpec(memory_space=pltpu.SMEM)
    whole2 = lambda x: pl.BlockSpec(x.shape, lambda s: (0,) * x.ndim)
    from_l, from_r, from_a, from_b = halos
    return pl.pallas_call(
        functools.partial(wave_kernel, height, breadth, nlon),
        out_shape=jax.ShapeDtypeStruct((height, breadth), jnp.float32),
        grid=(slots,),
        in_specs=[smem] * 5
        + [
            pl.BlockSpec((1, fields, height, breadth), lambda s: (s, 0, 0, 0)),
            whole2(lat_faces),
            whole2(lon_faces),
            whole2(from_l),
            whole2(from_r),
            whole2(from_a),
            whole2(from_b),
        ],
        out_specs=pl.BlockSpec((height, breadth), lambda s: (0, 0)),
        scratch_shapes=[
            pltpu.VMEM((rows, COLS), jnp.float32),
            pltpu.VMEM((rows, COLS), jnp.float32),
            pltpu.VMEM((rows, COLS), jnp.float32),
            pltpu.VMEM((rows, COLS), jnp.float32),
            pltpu.VMEM((rows, COLS), jnp.float32),
            pltpu.VMEM((height, COLS), jnp.float32),
            pltpu.VMEM((2, 3, rows, COLS), jnp.float32),
            pltpu.VMEM((from_a.shape[0], height, 128), jnp.float32),
        ],
        compiler_params=pltpu.CompilerParams(dimension_semantics=("arbitrary",)),
    )(*scalars, wave_states, lat_faces, lon_faces, from_l, from_r, from_a, from_b)


def edge_columns(fields, lat_faces, lon_faces, cols):
    x = jnp.concatenate(
        [fields[:, :, cols].astype(jnp.float32), jnp.stack([lat_faces[:, cols], lon_faces[:, cols]])]
    )
    x = jnp.transpose(x, (1, 0, 2)).reshape(x.shape[1], -1)
    return jnp.pad(x, ((0, 0), (0, 128 - x.shape[1])))


def edge_rows(fields, lat_faces, lon_faces, rows):
    x = jnp.concatenate(
        [fields[:, rows, :].astype(jnp.float32), jnp.stack([lat_faces[rows], lon_faces[rows]])]
    )
    return jnp.pad(x, ((0, 0), (0, 0), (0, COLS - x.shape[2])))


def body(
    wave_states,
    pair_list,
    pair_counts,
    residuals,
    station_cell,
    source_wavelet,
    lat_faces,
    lon_faces,
):
    height, breadth = lat_faces.shape
    nlon = breadth * lax.axis_size("lon")
    slots, fields = wave_states.shape[:2]
    flat = wave_states.reshape(slots * fields, height, breadth)
    send_l = edge_columns(flat, lat_faces, lon_faces, slice(0, HALO))
    send_r = edge_columns(flat, lat_faces, lon_faces, slice(breadth - HALO, breadth))
    top_rows = edge_rows(flat, lat_faces, lon_faces, slice(0, STRIP))
    bot_rows = edge_rows(flat, lat_faces, lon_faces, slice(height - STRIP, height))
    halos = exchange(send_l, send_r, top_rows, bot_rows)
    scalars = (pair_list.reshape(-1), pair_counts, residuals.reshape(-1), station_cell, source_wavelet)
    partial = propagate(wave_states, lat_faces, lon_faces, halos, scalars, nlon)
    other = lax.ppermute(partial, "pair", [(0, 1), (1, 0)])
    return partial + other


def solution(mesh):
    in_specs = (
        P("pair", None, "lat", "lon"),
        P(),
        P(),
        P(),
        P(),
        P(),
        P("lat", "lon"),
        P("lat", "lon"),
    )
    out_specs = P("lat", "lon")
    return jax.shard_map(body, mesh=mesh, in_specs=in_specs, out_specs=out_specs, check_vma=False)
```

```python
import functools

import jax
import jax.numpy as jnp
from jax import lax
from jax.experimental import pallas as pl
from jax.experimental.pallas import tpu as pltpu
from jax.sharding import PartitionSpec as P

HALO = 4
TOP = 16
COLS = 512
STRIP = 8
MESH = pl.DeviceIdType.MESH
TL, TR, BL, BR = 0, 1, 2, 3


def exchange_kernel(
    f_ref, lat_ref, lon_ref, out_l, out_r, out_a, out_b, out_c,
    pack_l, pack_r, strip_t, strip_b, tmp, tmp8, rl, rr, ra, rb, rc, send_sem, recv_sem,
):
    slots, fields, height, breadth = f_ref.shape
    count = slots * fields + 2
    nlon = lax.axis_size("lon")
    nlat = lax.axis_size("lat")
    me_lat = lax.axis_index("lat")
    me_lon = lax.axis_index("lon")
    right = lax.rem(me_lon + 1, nlon)
    left = lax.rem(me_lon + nlon - 1, nlon)
    has_up = me_lat > 0
    has_down = me_lat < nlat - 1
    up = jnp.maximum(me_lat - 1, 0)
    down = jnp.minimum(me_lat + 1, nlat - 1)

    def rows_of(a, first, size):
        if a < slots * fields:
            return f_ref[a // fields, a % fields, pl.ds(first, size), :].astype(jnp.float32)
        src = lat_ref if a == slots * fields else lon_ref
        return src[pl.ds(first, size), :]

    lane = lax.broadcasted_iota(jnp.int32, (height, 128), 1)
    quad = lane // HALO
    sub8 = lax.broadcasted_iota(jnp.int32, (STRIP, COLS), 0)
    pl_acc = jnp.zeros((height, 128), jnp.float32)
    pr_acc = jnp.zeros((height, 128), jnp.float32)
    tmp8[...] = jnp.zeros_like(tmp8)
    pending = {}
    for a in range(count):
        whole = rows_of(a, 0, height)
        tmp[:, pl.ds(0, breadth)] = whole
        head = tmp[:, pl.ds(0, 128)]
        tail = tmp[:, pl.ds(384, 128)]
        pl_acc = jnp.where(quad == a, pltpu.roll(head, (HALO * a) % 128, 1), pl_acc)
        pr_acc = jnp.where(quad == a, pltpu.roll(tail, (HALO * a - (breadth - 384 - HALO)) % 128, 1), pr_acc)
        tmp8[:, pl.ds(0, breadth)] = whole[0:STRIP]
        top = tmp8[...]
        tmp8[:, pl.ds(0, breadth)] = whole[height - STRIP : height]
        bottom = tmp8[...]
        if a % 2 == 0:
            pending = {"top": top, "bottom": bottom}
        else:
            b = a // 2
            strip_t[b] = jnp.where(sub8 < 4, pending["top"], pltpu.roll(top, 4, 0))
            strip_b[b] = jnp.where(sub8 < 4, pltpu.roll(pending["bottom"], 4, 0), bottom)
    pack_l[...] = pl_acc
    pack_r[...] = pr_acc

    barrier = pltpu.get_barrier_semaphore()
    for lon_to in (left, right):
        pl.semaphore_signal(barrier, 1, device_id={"lon": lon_to}, device_id_type=MESH)

    @pl.when(has_up)
    def _():
        for lon_to in (me_lon, left, right):
            pl.semaphore_signal(barrier, 1, device_id={"lat": up, "lon": lon_to}, device_id_type=MESH)

    @pl.when(has_down)
    def _():
        for lon_to in (me_lon, left, right):
            pl.semaphore_signal(barrier, 1, device_id={"lat": down, "lon": lon_to}, device_id_type=MESH)

    pl.semaphore_wait(barrier, 2 + 3 * has_up.astype(jnp.int32) + 3 * has_down.astype(jnp.int32))

    last8 = pl.ds(height - STRIP, STRIP)
    first8 = pl.ds(0, STRIP)
    copies = [
        (pack_r, rl, me_lat, right, None),
        (pack_l, rr, me_lat, left, None),
        (strip_t, rb, up, me_lon, "up"),
        (strip_b, ra, down, me_lon, "down"),
        (pack_r.at[last8], rc.at[TL], down, right, "down"),
        (pack_l.at[last8], rc.at[TR], down, left, "down"),
        (pack_r.at[first8], rc.at[BL], up, right, "up"),
        (pack_l.at[first8], rc.at[BR], up, left, "up"),
    ]

    def descriptor(i):
        src, dst, lat_to, lon_to, _ = copies[i]
        return pltpu.make_async_remote_copy(
            src, dst, send_sem.at[i], recv_sem.at[i], device_id={"lat": lat_to, "lon": lon_to}, device_id_type=MESH
        )

    def when(cond, fn):
        if cond is None:
            fn()
        else:
            pl.when(has_up if cond == "up" else has_down)(fn)

    for i, copy in enumerate(copies):
        when(copy[4], lambda i=i: descriptor(i).start())
    for i, copy in enumerate(copies):
        when(copy[4], lambda i=i: descriptor(i).wait_send())
        mirror = {None: None, "up": "down", "down": "up"}[copy[4]]
        when(mirror, lambda i=i: descriptor(i).wait_recv())

    @pl.when(jnp.logical_not(has_up))
    def _():
        ra[...] = jnp.zeros_like(ra)
        rc[TL] = jnp.zeros((STRIP, 128), jnp.float32)
        rc[TR] = jnp.zeros((STRIP, 128), jnp.float32)

    @pl.when(jnp.logical_not(has_down))
    def _():
        rb[...] = jnp.zeros_like(rb)
        rc[BL] = jnp.zeros((STRIP, 128), jnp.float32)
        rc[BR] = jnp.zeros((STRIP, 128), jnp.float32)

    out_l[...] = rl[...]
    out_r[...] = rr[...]
    out_a[...] = ra[...]
    out_b[...] = rb[...]
    out_c[...] = rc[...]


def exchange(wave_states, lat_faces, lon_faces):
    slots, fields, height, breadth = wave_states.shape
    count = slots * fields + 2
    vmem = pl.BlockSpec(memory_space=pltpu.VMEM)
    pack = jax.ShapeDtypeStruct((height, 128), jnp.float32)
    strip = jax.ShapeDtypeStruct((count // 2, STRIP, COLS), jnp.float32)
    corners = jax.ShapeDtypeStruct((4, STRIP, 128), jnp.float32)
    return pl.pallas_call(
        exchange_kernel,
        out_shape=[pack, pack, strip, strip, corners],
        in_specs=[vmem] * 3,
        out_specs=[vmem] * 5,
        scratch_shapes=[
            pltpu.VMEM(pack.shape, jnp.float32),
            pltpu.VMEM(pack.shape, jnp.float32),
            pltpu.VMEM(strip.shape, jnp.float32),
            pltpu.VMEM(strip.shape, jnp.float32),
            pltpu.VMEM((height, COLS), jnp.float32),
            pltpu.VMEM((STRIP, COLS), jnp.float32),
            pltpu.VMEM(pack.shape, jnp.float32),
            pltpu.VMEM(pack.shape, jnp.float32),
            pltpu.VMEM(strip.shape, jnp.float32),
            pltpu.VMEM(strip.shape, jnp.float32),
            pltpu.VMEM(corners.shape, jnp.float32),
            pltpu.SemaphoreType.DMA((8,)),
            pltpu.SemaphoreType.DMA((8,)),
        ],
        compiler_params=pltpu.CompilerParams(collective_id=0, has_side_effects=True),
    )(wave_states, lat_faces, lon_faces)


def wave_kernel(
    height,
    breadth,
    nlon,
    pl_ref,
    pc_ref,
    res_ref,
    sc_ref,
    wav_ref,
    f_ref,
    north_ref,
    east_ref,
    from_l,
    from_r,
    strip_a,
    strip_b,
    corner,
    o_ref,
    cn,
    ca,
    ce,
    cw,
    cd,
    acc,
    bufs,
    halo,
    from_a,
    from_b,
):
    s = pl.program_id(0)
    rows = cn.shape[0]
    steps = wav_ref.shape[0]
    slots = pl.num_programs(0)
    fields = f_ref.shape[1]
    lane = lax.broadcasted_iota(jnp.int32, (height, 128), 1)

    def assemble(dst, raw, a):
        dst[pl.ds(TOP, height), pl.ds(0, breadth)] = raw
        tail = dst[pl.ds(TOP, height), pl.ds(384, 128)]
        dst[pl.ds(TOP, height), pl.ds(384, 128)] = jnp.where(lane < breadth - 384, tail, halo[a])
        dst[pl.ds(TOP - STRIP, STRIP), :] = from_a[a]
        dst[pl.ds(TOP + height, STRIP), :] = from_b[a]
        dst[pl.ds(0, TOP - STRIP), :] = jnp.zeros((TOP - STRIP, COLS), jnp.float32)
        dst[pl.ds(TOP + height + STRIP, rows - TOP - height - STRIP), :] = jnp.zeros(
            (rows - TOP - height - STRIP, COLS), jnp.float32
        )

    @pl.when(s == 0)
    def _():
        fr = from_r[...]
        fl = from_l[...]
        east_gap = (lane >= breadth - 384) & (lane < breadth - 384 + HALO)
        west_gap = lane >= 128 - HALO
        sub8 = lax.broadcasted_iota(jnp.int32, (STRIP, COLS), 0)
        sub_c = lax.broadcasted_iota(jnp.int32, (STRIP, 128), 0)
        lane_c = lax.broadcasted_iota(jnp.int32, (STRIP, 128), 1)
        east_c = (lane_c >= breadth - 384) & (lane_c < breadth - 384 + HALO)
        west_c = lane_c >= 128 - HALO
        for a in range(halo.shape[0]):
            east_shift = (breadth - 384 - HALO * a) % 128
            west_shift = (128 - HALO - HALO * a) % 128
            hr = pltpu.roll(fr, east_shift, 1)
            hl = pltpu.roll(fl, west_shift, 1)
            halo[a] = jnp.where(east_gap, hr, jnp.where(west_gap, hl, jnp.float32(0.0)))
            b = a // 2
            blk = strip_a[b]
            blk = pltpu.roll(blk, 4, 0) if a % 2 == 0 else blk
            from_a[a] = jnp.where(sub8 >= 4, blk, jnp.float32(0.0))
            tail = from_a[a, :, pl.ds(384, 128)]
            low = sub_c >= 4
            tail = jnp.where(low & east_c, pltpu.roll(corner[TR], east_shift, 1), tail)
            tail = jnp.where(low & west_c, pltpu.roll(corner[TL], west_shift, 1), tail)
            from_a[a, :, pl.ds(384, 128)] = tail
            blk = strip_b[b]
            blk = blk if a % 2 == 0 else pltpu.roll(blk, 4, 0)
            from_b[a] = jnp.where(sub8 < 4, blk, jnp.float32(0.0))
            tail = from_b[a, :, pl.ds(384, 128)]
            high = sub_c < 4
            tail = jnp.where(high & east_c, pltpu.roll(corner[BR], east_shift, 1), tail)
            tail = jnp.where(high & west_c, pltpu.roll(corner[BL], west_shift, 1), tail)
            from_b[a, :, pl.ds(384, 128)] = tail
        coef_base = slots * fields
        assemble(cn, north_ref[...], coef_base)
        assemble(ce, east_ref[...], coef_base + 1)

        @pl.when(lax.axis_index("lat") == lax.axis_size("lat") - 1)
        def _():
            last = TOP + height - 8
            sub8 = lax.broadcasted_iota(jnp.int32, (8, COLS), 0)
            cn[pl.ds(last, 8), :] = jnp.where(sub8 == 7, jnp.float32(0.0), cn[pl.ds(last, 8), :])

        zero8 = jnp.zeros((8, COLS), jnp.float32)
        ca[pl.ds(8, rows - 16), :] = cn[pl.ds(7, rows - 16), :]
        ca[pl.ds(0, 8), :] = zero8
        ca[pl.ds(rows - 8, 8), :] = zero8
        cw[...] = pltpu.roll(ce[...], 1, 1)
        cd[...] = 2.0 - (cn[...] + ca[...] + ce[...] + cw[...])
        acc[...] = jnp.zeros_like(acc)

    member = lax.axis_index("pair")
    row_first = lax.axis_index("lat") * height
    col_first = lax.axis_index("lon") * breadth
    slot = member * slots + s
    act = jnp.where(s < pc_ref[member], jnp.float32(1.0), jnp.float32(0.0))

    places = []
    for comp in range(2):
        cell = sc_ref[pl_ref[slot, comp]]
        r = lax.div(cell, nlon)
        c = cell - r * nlon
        rb = r - row_first + TOP
        d = c - col_first
        d = jnp.where(d < 0, d + nlon, d)
        near = d < breadth + HALO
        wrap = d >= nlon - HALO
        cb = jnp.where(near, d, d - nlon + COLS)
        valid = (rb >= TOP - HALO) & (rb < TOP + height + HALO) & (near | wrap)
        places.append((rb, cb, valid))

    for comp in range(2):
        assemble(bufs.at[comp, 0], f_ref[0, comp].astype(jnp.float32), s * fields + comp)
        assemble(bufs.at[comp, 1], f_ref[0, 2 + comp].astype(jnp.float32), s * fields + 2 + comp)

    sub = lax.broadcasted_iota(jnp.int32, (8, COLS), 0)
    lane8 = lax.broadcasted_iota(jnp.int32, (8, COLS), 1)
    blocks = rows // 8

    for t in range(steps):
        ei, ci, ni = t % 3, (t + 1) % 3, (t + 2) % 3
        for comp in range(2):
            rb, cb, valid = places[comp]
            amp = wav_ref[t] if comp == 0 else res_ref[slot, steps - 1 - t]

            @pl.when(valid)
            def _():
                r8 = pl.multiple_of(lax.div(rb, 8) * 8, 8)
                slab = bufs[comp, ei, pl.ds(r8, 8), :]
                hit = (sub == rb - r8) & (lane8 == cb)
                bufs[comp, ei, pl.ds(r8, 8), :] = slab - jnp.where(hit, amp, jnp.float32(0.0))

        last = t == steps - 1
        first_block, end_block = (2, blocks - 2) if last else (1, blocks - 1)
        for k in range(first_block, end_block):
            r0 = 8 * k
            dd = cd[pl.ds(r0, 8), :]
            nn = cn[pl.ds(r0, 8), :]
            aa = ca[pl.ds(r0, 8), :]
            ee = ce[pl.ds(r0, 8), :]
            ww = cw[pl.ds(r0, 8), :]
            outs = []
            for comp in range(2):
                cur = bufs[comp, ci, pl.ds(r0, 8), :]
                above = bufs[comp, ci, pl.ds(r0 - 1, 8), :]
                below = bufs[comp, ci, pl.ds(r0 + 1, 8), :]
                ear = bufs[comp, ei, pl.ds(r0, 8), :]
                west = pltpu.roll(cur, 1, 1)
                east = pltpu.roll(cur, COLS - 1, 1)
                nxt = dd * cur + nn * below + aa * above + ee * east + ww * west - ear
                bufs[comp, ni, pl.ds(r0, 8), :] = nxt
                outs.append(nxt)
            if 2 <= k < blocks - 2:
                acc[pl.ds(r0 - TOP, 8), :] += (outs[0] * act) * outs[1]

    @pl.when(s == slots - 1)
    def _():
        o_ref[...] = acc[:, pl.ds(0, breadth)]


def propagate(wave_states, lat_faces, lon_faces, halos, scalars, nlon):
    slots, fields, height, breadth = wave_states.shape
    rows = height + 2 * TOP
    count = slots * fields + 2
    smem = pl.BlockSpec(memory_space=pltpu.SMEM)
    whole2 = lambda x: pl.BlockSpec(x.shape, lambda s: (0,) * x.ndim)
    return pl.pallas_call(
        functools.partial(wave_kernel, height, breadth, nlon),
        out_shape=jax.ShapeDtypeStruct((height, breadth), jnp.float32),
        grid=(slots,),
        in_specs=[smem] * 5
        + [
            pl.BlockSpec((1, fields, height, breadth), lambda s: (s, 0, 0, 0)),
            whole2(lat_faces),
            whole2(lon_faces),
        ]
        + [whole2(x) for x in halos],
        out_specs=pl.BlockSpec((height, breadth), lambda s: (0, 0)),
        scratch_shapes=[
            pltpu.VMEM((rows, COLS), jnp.float32),
            pltpu.VMEM((rows, COLS), jnp.float32),
            pltpu.VMEM((rows, COLS), jnp.float32),
            pltpu.VMEM((rows, COLS), jnp.float32),
            pltpu.VMEM((rows, COLS), jnp.float32),
            pltpu.VMEM((height, COLS), jnp.float32),
            pltpu.VMEM((2, 3, rows, COLS), jnp.float32),
            pltpu.VMEM((count, height, 128), jnp.float32),
            pltpu.VMEM((count, STRIP, COLS), jnp.float32),
            pltpu.VMEM((count, STRIP, COLS), jnp.float32),
        ],
        compiler_params=pltpu.CompilerParams(dimension_semantics=("arbitrary",)),
    )(*scalars, wave_states, lat_faces, lon_faces, *halos)


def body(
    wave_states,
    pair_list,
    pair_counts,
    residuals,
    station_cell,
    source_wavelet,
    lat_faces,
    lon_faces,
):
    height, breadth = lat_faces.shape
    nlon = breadth * lax.axis_size("lon")
    halos = exchange(wave_states, lat_faces, lon_faces)
    scalars = (pair_list, pair_counts, residuals, station_cell, source_wavelet)
    partial = propagate(wave_states, lat_faces, lon_faces, halos, scalars, nlon)
    other = lax.ppermute(partial, "pair", [(0, 1), (1, 0)])
    return partial + other


def solution(mesh):
    in_specs = (
        P("pair", None, "lat", "lon"),
        P(),
        P(),
        P(),
        P(),
        P(),
        P("lat", "lon"),
        P("lat", "lon"),
    )
    out_specs = P("lat", "lon")
    return jax.shard_map(body, mesh=mesh, in_specs=in_specs, out_specs=out_specs, check_vma=False)
```

```python
import functools

import jax
import jax.numpy as jnp
from jax import lax
from jax.experimental import pallas as pl
from jax.experimental.pallas import tpu as pltpu
from jax.sharding import PartitionSpec as P

HALO = 4
TOP = 16
COLS = 512
STRIP = 8
MESH = pl.DeviceIdType.MESH
TL, TR, BL, BR = 0, 1, 2, 3


def exchange_kernel(
    f_ref, lat_ref, lon_ref, out_l, out_r, out_a, out_b, out_c,
    pack_l, pack_r, strip_t, strip_b, tmp, tmp8, rl, rr, ra, rb, rc, send_sem, recv_sem,
):
    slots, fields, height, breadth = f_ref.shape
    count = slots * fields + 2
    nlon = lax.axis_size("lon")
    nlat = lax.axis_size("lat")
    me_lat = lax.axis_index("lat")
    me_lon = lax.axis_index("lon")
    right = lax.rem(me_lon + 1, nlon)
    left = lax.rem(me_lon + nlon - 1, nlon)
    has_up = me_lat > 0
    has_down = me_lat < nlat - 1
    up = jnp.maximum(me_lat - 1, 0)
    down = jnp.minimum(me_lat + 1, nlat - 1)

    barrier = pltpu.get_barrier_semaphore()
    for lon_to in (left, right):
        pl.semaphore_signal(barrier, 1, device_id={"lon": lon_to}, device_id_type=MESH)

    @pl.when(has_up)
    def _():
        for lon_to in (me_lon, left, right):
            pl.semaphore_signal(barrier, 1, device_id={"lat": up, "lon": lon_to}, device_id_type=MESH)

    @pl.when(has_down)
    def _():
        for lon_to in (me_lon, left, right):
            pl.semaphore_signal(barrier, 1, device_id={"lat": down, "lon": lon_to}, device_id_type=MESH)

    def rows_of(a, first, size):
        if a < slots * fields:
            return f_ref[a // fields, a % fields, pl.ds(first, size), :].astype(jnp.float32)
        src = lat_ref if a == slots * fields else lon_ref
        return src[pl.ds(first, size), :]

    lane = lax.broadcasted_iota(jnp.int32, (height, 128), 1)
    quad = lane // HALO
    sub8 = lax.broadcasted_iota(jnp.int32, (STRIP, COLS), 0)
    pl_acc = jnp.zeros((height, 128), jnp.float32)
    pr_acc = jnp.zeros((height, 128), jnp.float32)
    tmp8[...] = jnp.zeros_like(tmp8)
    pending = {}
    for a in range(count):
        whole = rows_of(a, 0, height)
        tmp[:, pl.ds(0, breadth)] = whole
        head = tmp[:, pl.ds(0, 128)]
        tail = tmp[:, pl.ds(384, 128)]
        pl_acc = jnp.where(quad == a, pltpu.roll(head, (HALO * a) % 128, 1), pl_acc)
        pr_acc = jnp.where(quad == a, pltpu.roll(tail, (HALO * a - (breadth - 384 - HALO)) % 128, 1), pr_acc)
        tmp8[:, pl.ds(0, breadth)] = whole[0:STRIP]
        top = tmp8[...]
        tmp8[:, pl.ds(0, breadth)] = whole[height - STRIP : height]
        bottom = tmp8[...]
        if a % 2 == 0:
            pending = {"top": top, "bottom": bottom}
        else:
            b = a // 2
            strip_t[b] = jnp.where(sub8 < 4, pending["top"], pltpu.roll(top, 4, 0))
            strip_b[b] = jnp.where(sub8 < 4, pltpu.roll(pending["bottom"], 4, 0), bottom)
    pack_l[...] = pl_acc
    pack_r[...] = pr_acc

    pl.semaphore_wait(barrier, 2 + 3 * has_up.astype(jnp.int32) + 3 * has_down.astype(jnp.int32))

    last8 = pl.ds(height - STRIP, STRIP)
    first8 = pl.ds(0, STRIP)
    copies = [
        (pack_r, rl, me_lat, right, None),
        (pack_l, rr, me_lat, left, None),
        (strip_t, rb, up, me_lon, "up"),
        (strip_b, ra, down, me_lon, "down"),
        (pack_r.at[last8], rc.at[TL], down, right, "down"),
        (pack_l.at[last8], rc.at[TR], down, left, "down"),
        (pack_r.at[first8], rc.at[BL], up, right, "up"),
        (pack_l.at[first8], rc.at[BR], up, left, "up"),
    ]

    def descriptor(i):
        src, dst, lat_to, lon_to, _ = copies[i]
        return pltpu.make_async_remote_copy(
            src, dst, send_sem.at[i], recv_sem.at[i], device_id={"lat": lat_to, "lon": lon_to}, device_id_type=MESH
        )

    def when(cond, fn):
        if cond is None:
            fn()
        else:
            pl.when(has_up if cond == "up" else has_down)(fn)

    for i, copy in enumerate(copies):
        when(copy[4], lambda i=i: descriptor(i).start())
    for i, copy in enumerate(copies):
        when(copy[4], lambda i=i: descriptor(i).wait_send())
        mirror = {None: None, "up": "down", "down": "up"}[copy[4]]
        when(mirror, lambda i=i: descriptor(i).wait_recv())

    @pl.when(jnp.logical_not(has_up))
    def _():
        ra[...] = jnp.zeros_like(ra)
        rc[TL] = jnp.zeros((STRIP, 128), jnp.float32)
        rc[TR] = jnp.zeros((STRIP, 128), jnp.float32)

    @pl.when(jnp.logical_not(has_down))
    def _():
        rb[...] = jnp.zeros_like(rb)
        rc[BL] = jnp.zeros((STRIP, 128), jnp.float32)
        rc[BR] = jnp.zeros((STRIP, 128), jnp.float32)

    out_l[...] = rl[...]
    out_r[...] = rr[...]
    out_a[...] = ra[...]
    out_b[...] = rb[...]
    out_c[...] = rc[...]


def exchange(wave_states, lat_faces, lon_faces):
    slots, fields, height, breadth = wave_states.shape
    count = slots * fields + 2
    vmem = pl.BlockSpec(memory_space=pltpu.VMEM)
    pack = jax.ShapeDtypeStruct((height, 128), jnp.float32)
    strip = jax.ShapeDtypeStruct((count // 2, STRIP, COLS), jnp.float32)
    corners = jax.ShapeDtypeStruct((4, STRIP, 128), jnp.float32)
    return pl.pallas_call(
        exchange_kernel,
        out_shape=[pack, pack, strip, strip, corners],
        in_specs=[vmem] * 3,
        out_specs=[vmem] * 5,
        scratch_shapes=[
            pltpu.VMEM(pack.shape, jnp.float32),
            pltpu.VMEM(pack.shape, jnp.float32),
            pltpu.VMEM(strip.shape, jnp.float32),
            pltpu.VMEM(strip.shape, jnp.float32),
            pltpu.VMEM((height, COLS), jnp.float32),
            pltpu.VMEM((STRIP, COLS), jnp.float32),
            pltpu.VMEM(pack.shape, jnp.float32),
            pltpu.VMEM(pack.shape, jnp.float32),
            pltpu.VMEM(strip.shape, jnp.float32),
            pltpu.VMEM(strip.shape, jnp.float32),
            pltpu.VMEM(corners.shape, jnp.float32),
            pltpu.SemaphoreType.DMA((8,)),
            pltpu.SemaphoreType.DMA((8,)),
        ],
        compiler_params=pltpu.CompilerParams(collective_id=0, has_side_effects=True),
    )(wave_states, lat_faces, lon_faces)


def wave_kernel(
    height,
    breadth,
    nlon,
    pl_ref,
    pc_ref,
    res_ref,
    sc_ref,
    wav_ref,
    f_ref,
    north_ref,
    east_ref,
    from_l,
    from_r,
    strip_a,
    strip_b,
    corner,
    o_ref,
    cn,
    ca,
    ce,
    cw,
    cd,
    acc,
    bufs,
    halo,
    from_a,
    from_b,
):
    s = pl.program_id(0)
    rows = cn.shape[0]
    steps = wav_ref.shape[0]
    slots = pl.num_programs(0)
    fields = f_ref.shape[1]
    lane = lax.broadcasted_iota(jnp.int32, (height, 128), 1)

    def assemble(dst, raw, a):
        dst[pl.ds(TOP, height), pl.ds(0, breadth)] = raw
        tail = dst[pl.ds(TOP, height), pl.ds(384, 128)]
        dst[pl.ds(TOP, height), pl.ds(384, 128)] = jnp.where(lane < breadth - 384, tail, halo[a])
        dst[pl.ds(TOP - STRIP, STRIP), :] = from_a[a]
        dst[pl.ds(TOP + height, STRIP), :] = from_b[a]
        dst[pl.ds(0, TOP - STRIP), :] = jnp.zeros((TOP - STRIP, COLS), jnp.float32)
        dst[pl.ds(TOP + height + STRIP, rows - TOP - height - STRIP), :] = jnp.zeros(
            (rows - TOP - height - STRIP, COLS), jnp.float32
        )

    @pl.when(s == 0)
    def _():
        fr = from_r[...]
        fl = from_l[...]
        east_gap = (lane >= breadth - 384) & (lane < breadth - 384 + HALO)
        west_gap = lane >= 128 - HALO
        sub8 = lax.broadcasted_iota(jnp.int32, (STRIP, COLS), 0)
        sub_c = lax.broadcasted_iota(jnp.int32, (STRIP, 128), 0)
        lane_c = lax.broadcasted_iota(jnp.int32, (STRIP, 128), 1)
        east_c = (lane_c >= breadth - 384) & (lane_c < breadth - 384 + HALO)
        west_c = lane_c >= 128 - HALO
        for a in range(halo.shape[0]):
            east_shift = (breadth - 384 - HALO * a) % 128
            west_shift = (128 - HALO - HALO * a) % 128
            hr = pltpu.roll(fr, east_shift, 1)
            hl = pltpu.roll(fl, west_shift, 1)
            halo[a] = jnp.where(east_gap, hr, jnp.where(west_gap, hl, jnp.float32(0.0)))
            b = a // 2
            blk = strip_a[b]
            blk = pltpu.roll(blk, 4, 0) if a % 2 == 0 else blk
            from_a[a] = jnp.where(sub8 >= 4, blk, jnp.float32(0.0))
            tail = from_a[a, :, pl.ds(384, 128)]
            low = sub_c >= 4
            tail = jnp.where(low & east_c, pltpu.roll(corner[TR], east_shift, 1), tail)
            tail = jnp.where(low & west_c, pltpu.roll(corner[TL], west_shift, 1), tail)
            from_a[a, :, pl.ds(384, 128)] = tail
            blk = strip_b[b]
            blk = blk if a % 2 == 0 else pltpu.roll(blk, 4, 0)
            from_b[a] = jnp.where(sub8 < 4, blk, jnp.float32(0.0))
            tail = from_b[a, :, pl.ds(384, 128)]
            high = sub_c < 4
            tail = jnp.where(high & east_c, pltpu.roll(corner[BR], east_shift, 1), tail)
            tail = jnp.where(high & west_c, pltpu.roll(corner[BL], west_shift, 1), tail)
            from_b[a, :, pl.ds(384, 128)] = tail
        coef_base = slots * fields
        assemble(cn, north_ref[...], coef_base)
        assemble(ce, east_ref[...], coef_base + 1)

        @pl.when(lax.axis_index("lat") == lax.axis_size("lat") - 1)
        def _():
            last = TOP + height - 8
            sub8 = lax.broadcasted_iota(jnp.int32, (8, COLS), 0)
            cn[pl.ds(last, 8), :] = jnp.where(sub8 == 7, jnp.float32(0.0), cn[pl.ds(last, 8), :])

        zero8 = jnp.zeros((8, COLS), jnp.float32)
        ca[pl.ds(8, rows - 16), :] = cn[pl.ds(7, rows - 16), :]
        ca[pl.ds(0, 8), :] = zero8
        ca[pl.ds(rows - 8, 8), :] = zero8
        cw[...] = pltpu.roll(ce[...], 1, 1)
        cd[...] = 2.0 - (cn[...] + ca[...] + ce[...] + cw[...])
        acc[...] = jnp.zeros_like(acc)

    member = lax.axis_index("pair")
    row_first = lax.axis_index("lat") * height
    col_first = lax.axis_index("lon") * breadth
    slot = member * slots + s
    act = jnp.where(s < pc_ref[member], jnp.float32(1.0), jnp.float32(0.0))

    places = []
    for comp in range(2):
        cell = sc_ref[pl_ref[comp, slot]]
        r = lax.div(cell, nlon)
        c = cell - r * nlon
        rb = r - row_first + TOP
        d = c - col_first
        d = jnp.where(d < 0, d + nlon, d)
        near = d < breadth + HALO
        wrap = d >= nlon - HALO
        cb = jnp.where(near, d, d - nlon + COLS)
        valid = (rb >= TOP - HALO) & (rb < TOP + height + HALO) & (near | wrap)
        places.append((rb, cb, valid))

    for comp in range(2):
        assemble(bufs.at[comp, 0], f_ref[0, comp].astype(jnp.float32), s * fields + comp)
        assemble(bufs.at[comp, 1], f_ref[0, 2 + comp].astype(jnp.float32), s * fields + 2 + comp)

    sub = lax.broadcasted_iota(jnp.int32, (8, COLS), 0)
    lane8 = lax.broadcasted_iota(jnp.int32, (8, COLS), 1)
    blocks = rows // 8

    for t in range(steps):
        ei, ci, ni = t % 3, (t + 1) % 3, (t + 2) % 3
        for comp in range(2):
            rb, cb, valid = places[comp]
            amp = wav_ref[t] if comp == 0 else res_ref[steps - 1 - t, slot]

            @pl.when(valid)
            def _():
                r8 = pl.multiple_of(lax.div(rb, 8) * 8, 8)
                slab = bufs[comp, ei, pl.ds(r8, 8), :]
                hit = (sub == rb - r8) & (lane8 == cb)
                bufs[comp, ei, pl.ds(r8, 8), :] = slab - jnp.where(hit, amp, jnp.float32(0.0))

        last = t == steps - 1
        first_block, end_block = (2, blocks - 2) if last else (1, blocks - 1)
        for k in range(first_block, end_block):
            r0 = 8 * k
            dd = cd[pl.ds(r0, 8), :]
            nn = cn[pl.ds(r0, 8), :]
            aa = ca[pl.ds(r0, 8), :]
            ee = ce[pl.ds(r0, 8), :]
            ww = cw[pl.ds(r0, 8), :]
            outs = []
            for comp in range(2):
                cur = bufs[comp, ci, pl.ds(r0, 8), :]
                above = bufs[comp, ci, pl.ds(r0 - 1, 8), :]
                below = bufs[comp, ci, pl.ds(r0 + 1, 8), :]
                ear = bufs[comp, ei, pl.ds(r0, 8), :]
                west = pltpu.roll(cur, 1, 1)
                east = pltpu.roll(cur, COLS - 1, 1)
                nxt = dd * cur + nn * below + aa * above + ee * east + ww * west - ear
                bufs[comp, ni, pl.ds(r0, 8), :] = nxt
                outs.append(nxt)
            if 2 <= k < blocks - 2:
                acc[pl.ds(r0 - TOP, 8), :] += (outs[0] * act) * outs[1]

    @pl.when(s == slots - 1)
    def _():
        o_ref[...] = acc[:, pl.ds(0, breadth)]


def propagate(wave_states, lat_faces, lon_faces, halos, scalars, nlon):
    slots, fields, height, breadth = wave_states.shape
    rows = height + 2 * TOP
    count = slots * fields + 2
    smem = pl.BlockSpec(memory_space=pltpu.SMEM)
    whole2 = lambda x: pl.BlockSpec(x.shape, lambda s: (0,) * x.ndim)
    return pl.pallas_call(
        functools.partial(wave_kernel, height, breadth, nlon),
        out_shape=jax.ShapeDtypeStruct((height, breadth), jnp.float32),
        grid=(slots,),
        in_specs=[smem] * 5
        + [
            pl.BlockSpec((1, fields, height, breadth), lambda s: (s, 0, 0, 0)),
            whole2(lat_faces),
            whole2(lon_faces),
        ]
        + [whole2(x) for x in halos],
        out_specs=pl.BlockSpec((height, breadth), lambda s: (0, 0)),
        scratch_shapes=[
            pltpu.VMEM((rows, COLS), jnp.float32),
            pltpu.VMEM((rows, COLS), jnp.float32),
            pltpu.VMEM((rows, COLS), jnp.float32),
            pltpu.VMEM((rows, COLS), jnp.float32),
            pltpu.VMEM((rows, COLS), jnp.float32),
            pltpu.VMEM((height, COLS), jnp.float32),
            pltpu.VMEM((2, 3, rows, COLS), jnp.float32),
            pltpu.VMEM((count, height, 128), jnp.float32),
            pltpu.VMEM((count, STRIP, COLS), jnp.float32),
            pltpu.VMEM((count, STRIP, COLS), jnp.float32),
        ],
        compiler_params=pltpu.CompilerParams(dimension_semantics=("arbitrary",)),
    )(*scalars, wave_states, lat_faces, lon_faces, *halos)


def body(
    wave_states,
    pair_list,
    pair_counts,
    residuals,
    station_cell,
    source_wavelet,
    lat_faces,
    lon_faces,
):
    height, breadth = lat_faces.shape
    nlon = breadth * lax.axis_size("lon")
    halos = exchange(wave_states, lat_faces, lon_faces)
    scalars = (pair_list.T, pair_counts, residuals.T, station_cell, source_wavelet)
    partial = propagate(wave_states, lat_faces, lon_faces, halos, scalars, nlon)
    other = lax.ppermute(partial, "pair", [(0, 1), (1, 0)])
    return partial + other


def solution(mesh):
    in_specs = (
        P("pair", None, "lat", "lon"),
        P(),
        P(),
        P(),
        P(),
        P(),
        P("lat", "lon"),
        P("lat", "lon"),
    )
    out_specs = P("lat", "lon")
    return jax.shard_map(body, mesh=mesh, in_specs=in_specs, out_specs=out_specs, check_vma=False)
```

```python
import functools

import jax
import jax.numpy as jnp
from jax import lax
from jax.experimental import pallas as pl
from jax.experimental.pallas import tpu as pltpu
from jax.sharding import PartitionSpec as P

HALO = 4
TOP = 16
COLS = 512
STRIP = 8
MESH = pl.DeviceIdType.MESH
TL, TR, BL, BR = 0, 1, 2, 3


def exchange_kernel(
    f_ref, lat_ref, lon_ref, out_l, out_r, out_a, out_b, out_c,
    pack_l, pack_r, strip_t, strip_b, tmp, tmp8,
    send_lb, send_rb, send_lc, send_rc, send_tb, send_bb, send_tc, send_bc,
    rlb, rrb, rlc, rrc, rab, rbb, rac, rbc, rc, send_sem, recv_sem,
):
    slots, fields, height, breadth = f_ref.shape
    count = slots * fields + 2
    nfield = slots * fields
    nlon = lax.axis_size("lon")
    nlat = lax.axis_size("lat")
    me_lat = lax.axis_index("lat")
    me_lon = lax.axis_index("lon")
    right = lax.rem(me_lon + 1, nlon)
    left = lax.rem(me_lon + nlon - 1, nlon)
    has_up = me_lat > 0
    has_down = me_lat < nlat - 1
    up = jnp.maximum(me_lat - 1, 0)
    down = jnp.minimum(me_lat + 1, nlat - 1)

    barrier = pltpu.get_barrier_semaphore()
    for lon_to in (left, right):
        pl.semaphore_signal(barrier, 1, device_id={"lon": lon_to}, device_id_type=MESH)

    @pl.when(has_up)
    def _():
        for lon_to in (me_lon, left, right):
            pl.semaphore_signal(barrier, 1, device_id={"lat": up, "lon": lon_to}, device_id_type=MESH)

    @pl.when(has_down)
    def _():
        for lon_to in (me_lon, left, right):
            pl.semaphore_signal(barrier, 1, device_id={"lat": down, "lon": lon_to}, device_id_type=MESH)

    def rows_of(a, first, size):
        if a < nfield:
            return f_ref[a // fields, a % fields, pl.ds(first, size), :].astype(jnp.float32)
        src = lat_ref if a == nfield else lon_ref
        return src[pl.ds(first, size), :]

    lane = lax.broadcasted_iota(jnp.int32, (height, 128), 1)
    quad = lane // HALO
    sub8 = lax.broadcasted_iota(jnp.int32, (STRIP, COLS), 0)
    lane8 = lax.broadcasted_iota(jnp.int32, (STRIP, 128), 1)
    pl_acc = jnp.zeros((height, 128), jnp.float32)
    pr_acc = jnp.zeros((height, 128), jnp.float32)
    tmp8[...] = jnp.zeros_like(tmp8)
    pending = {}
    for a in range(count):
        whole = rows_of(a, 0, height)
        tmp[:, pl.ds(0, breadth)] = whole
        head = tmp[:, pl.ds(0, 128)]
        tail = tmp[:, pl.ds(384, 128)]
        pl_acc = jnp.where(quad == a, pltpu.roll(head, (HALO * a) % 128, 1), pl_acc)
        pr_acc = jnp.where(quad == a, pltpu.roll(tail, (HALO * a - (breadth - 384 - HALO)) % 128, 1), pr_acc)
        tmp8[:, pl.ds(0, breadth)] = whole[0:STRIP]
        top = tmp8[...]
        tmp8[:, pl.ds(0, breadth)] = whole[height - STRIP : height]
        bottom = tmp8[...]
        if a % 2 == 0:
            pending = {"top": top, "bottom": bottom}
        else:
            b = a // 2
            strip_t[b] = jnp.where(sub8 < 4, pending["top"], pltpu.roll(top, 4, 0))
            strip_b[b] = jnp.where(sub8 < 4, pltpu.roll(pending["bottom"], 4, 0), bottom)
    pack_l[...] = pl_acc
    pack_r[...] = pr_acc

    coef_lane = HALO * nfield
    width = 2 * HALO
    per_row = 128 // width
    send_lb[...] = pl_acc.astype(jnp.bfloat16)
    send_rb[...] = pr_acc.astype(jnp.bfloat16)
    for src, dst in ((pl_acc, send_lc), (pr_acc, send_rc)):
        for h in range(dst.shape[0] // STRIP):
            packed = jnp.zeros((STRIP, 128), jnp.float32)
            for g in range(per_row):
                i = h * per_row + g
                if i * STRIP >= height:
                    break
                blk = src[i * STRIP : (i + 1) * STRIP]
                packed = jnp.where(lane8 // width == g, pltpu.roll(blk, (width * g - coef_lane) % 128, 1), packed)
            dst[pl.ds(h * STRIP, STRIP), :] = packed
    for src, dst_b, dst_c in ((strip_t, send_tb, send_tc), (strip_b, send_bb, send_bc)):
        for j in range(dst_b.shape[0]):
            dst_b[j] = jnp.concatenate([src[2 * j], src[2 * j + 1]], axis=0).astype(jnp.bfloat16)
        dst_c[...] = src[nfield // 2]

    pl.semaphore_wait(barrier, 2 + 3 * has_up.astype(jnp.int32) + 3 * has_down.astype(jnp.int32))

    last8 = pl.ds(height - STRIP, STRIP)
    first8 = pl.ds(0, STRIP)
    copies = [
        (send_rb, rlb, me_lat, right, None),
        (send_rc, rlc, me_lat, right, None),
        (send_lb, rrb, me_lat, left, None),
        (send_lc, rrc, me_lat, left, None),
        (send_tb, rbb, up, me_lon, "up"),
        (send_tc, rbc, up, me_lon, "up"),
        (send_bb, rab, down, me_lon, "down"),
        (send_bc, rac, down, me_lon, "down"),
        (pack_r.at[last8], rc.at[TL], down, right, "down"),
        (pack_l.at[last8], rc.at[TR], down, left, "down"),
        (pack_r.at[first8], rc.at[BL], up, right, "up"),
        (pack_l.at[first8], rc.at[BR], up, left, "up"),
    ]

    def descriptor(i):
        src, dst, lat_to, lon_to, _ = copies[i]
        return pltpu.make_async_remote_copy(
            src, dst, send_sem.at[i], recv_sem.at[i], device_id={"lat": lat_to, "lon": lon_to}, device_id_type=MESH
        )

    def when(cond, fn):
        if cond is None:
            fn()
        else:
            pl.when(has_up if cond == "up" else has_down)(fn)

    for i, copy in enumerate(copies):
        when(copy[4], lambda i=i: descriptor(i).start())
    for i, copy in enumerate(copies):
        when(copy[4], lambda i=i: descriptor(i).wait_send())
        mirror = {None: None, "up": "down", "down": "up"}[copy[4]]
        when(mirror, lambda i=i: descriptor(i).wait_recv())

    @pl.when(jnp.logical_not(has_up))
    def _():
        rab[...] = jnp.zeros_like(rab)
        rac[...] = jnp.zeros_like(rac)
        rc[TL] = jnp.zeros((STRIP, 128), jnp.float32)
        rc[TR] = jnp.zeros((STRIP, 128), jnp.float32)

    @pl.when(jnp.logical_not(has_down))
    def _():
        rbb[...] = jnp.zeros_like(rbb)
        rbc[...] = jnp.zeros_like(rbc)
        rc[BL] = jnp.zeros((STRIP, 128), jnp.float32)
        rc[BR] = jnp.zeros((STRIP, 128), jnp.float32)

    for src_b, src_c, dst in ((rlb, rlc, out_l), (rrb, rrc, out_r)):
        fields_part = src_b[...].astype(jnp.float32)
        for i in range(height // STRIP):
            h, g = divmod(i, per_row)
            blk_c = pltpu.roll(src_c[pl.ds(h * STRIP, STRIP), :], (coef_lane - width * g) % 128, 1)
            blk_f = fields_part[i * STRIP : (i + 1) * STRIP]
            dst[pl.ds(i * STRIP, STRIP), :] = jnp.where(
                lane8 < coef_lane, blk_f, jnp.where(lane8 < coef_lane + width, blk_c, jnp.float32(0.0))
            )
    for src_b, src_c, dst in ((rab, rac, out_a), (rbb, rbc, out_b)):
        for j in range(src_b.shape[0]):
            both = src_b[j].astype(jnp.float32)
            dst[2 * j] = both[0:STRIP]
            dst[2 * j + 1] = both[STRIP : 2 * STRIP]
        dst[nfield // 2] = src_c[...]
    out_c[...] = rc[...]


def exchange(wave_states, lat_faces, lon_faces):
    slots, fields, height, breadth = wave_states.shape
    count = slots * fields + 2
    nfield = slots * fields
    vmem = pl.BlockSpec(memory_space=pltpu.VMEM)
    pack = jax.ShapeDtypeStruct((height, 128), jnp.float32)
    strip = jax.ShapeDtypeStruct((count // 2, STRIP, COLS), jnp.float32)
    corners = jax.ShapeDtypeStruct((4, STRIP, 128), jnp.float32)
    per_row = 128 // (2 * HALO)
    coef_rows = STRIP * ((height // STRIP + per_row - 1) // per_row)
    packed_b = pltpu.VMEM((height, 128), jnp.bfloat16)
    packed_c = pltpu.VMEM((coef_rows, 128), jnp.float32)
    strip_b16 = pltpu.VMEM((nfield // 4, 2 * STRIP, COLS), jnp.bfloat16)
    strip_c = pltpu.VMEM((STRIP, COLS), jnp.float32)
    return pl.pallas_call(
        exchange_kernel,
        out_shape=[pack, pack, strip, strip, corners],
        in_specs=[vmem] * 3,
        out_specs=[vmem] * 5,
        scratch_shapes=[
            pltpu.VMEM(pack.shape, jnp.float32),
            pltpu.VMEM(pack.shape, jnp.float32),
            pltpu.VMEM(strip.shape, jnp.float32),
            pltpu.VMEM(strip.shape, jnp.float32),
            pltpu.VMEM((height, COLS), jnp.float32),
            pltpu.VMEM((STRIP, COLS), jnp.float32),
        ]
        + [packed_b, packed_b, packed_c, packed_c, strip_b16, strip_b16, strip_c, strip_c] * 2
        + [
            pltpu.VMEM(corners.shape, jnp.float32),
            pltpu.SemaphoreType.DMA((12,)),
            pltpu.SemaphoreType.DMA((12,)),
        ],
        compiler_params=pltpu.CompilerParams(collective_id=0, has_side_effects=True),
    )(wave_states, lat_faces, lon_faces)


def wave_kernel(
    height,
    breadth,
    nlon,
    pl_ref,
    pc_ref,
    res_ref,
    sc_ref,
    wav_ref,
    f_ref,
    north_ref,
    east_ref,
    from_l,
    from_r,
    strip_a,
    strip_b,
    corner,
    o_ref,
    cn,
    ca,
    ce,
    cw,
    cd,
    acc,
    bufs,
    halo,
    from_a,
    from_b,
):
    s = pl.program_id(0)
    rows = cn.shape[0]
    steps = wav_ref.shape[0]
    slots = pl.num_programs(0)
    fields = f_ref.shape[1]
    lane = lax.broadcasted_iota(jnp.int32, (height, 128), 1)

    def assemble(dst, raw, a):
        dst[pl.ds(TOP, height), pl.ds(0, breadth)] = raw
        tail = dst[pl.ds(TOP, height), pl.ds(384, 128)]
        dst[pl.ds(TOP, height), pl.ds(384, 128)] = jnp.where(lane < breadth - 384, tail, halo[a])
        dst[pl.ds(TOP - STRIP, STRIP), :] = from_a[a]
        dst[pl.ds(TOP + height, STRIP), :] = from_b[a]
        dst[pl.ds(0, TOP - STRIP), :] = jnp.zeros((TOP - STRIP, COLS), jnp.float32)
        dst[pl.ds(TOP + height + STRIP, rows - TOP - height - STRIP), :] = jnp.zeros(
            (rows - TOP - height - STRIP, COLS), jnp.float32
        )

    @pl.when(s == 0)
    def _():
        fr = from_r[...]
        fl = from_l[...]
        east_gap = (lane >= breadth - 384) & (lane < breadth - 384 + HALO)
        west_gap = lane >= 128 - HALO
        sub8 = lax.broadcasted_iota(jnp.int32, (STRIP, COLS), 0)
        sub_c = lax.broadcasted_iota(jnp.int32, (STRIP, 128), 0)
        lane_c = lax.broadcasted_iota(jnp.int32, (STRIP, 128), 1)
        east_c = (lane_c >= breadth - 384) & (lane_c < breadth - 384 + HALO)
        west_c = lane_c >= 128 - HALO
        for a in range(halo.shape[0]):
            east_shift = (breadth - 384 - HALO * a) % 128
            west_shift = (128 - HALO - HALO * a) % 128
            hr = pltpu.roll(fr, east_shift, 1)
            hl = pltpu.roll(fl, west_shift, 1)
            halo[a] = jnp.where(east_gap, hr, jnp.where(west_gap, hl, jnp.float32(0.0)))
            b = a // 2
            blk = strip_a[b]
            blk = pltpu.roll(blk, 4, 0) if a % 2 == 0 else blk
            from_a[a] = jnp.where(sub8 >= 4, blk, jnp.float32(0.0))
            tail = from_a[a, :, pl.ds(384, 128)]
            low = sub_c >= 4
            tail = jnp.where(low & east_c, pltpu.roll(corner[TR], east_shift, 1), tail)
            tail = jnp.where(low & west_c, pltpu.roll(corner[TL], west_shift, 1), tail)
            from_a[a, :, pl.ds(384, 128)] = tail
            blk = strip_b[b]
            blk = blk if a % 2 == 0 else pltpu.roll(blk, 4, 0)
            from_b[a] = jnp.where(sub8 < 4, blk, jnp.float32(0.0))
            tail = from_b[a, :, pl.ds(384, 128)]
            high = sub_c < 4
            tail = jnp.where(high & east_c, pltpu.roll(corner[BR], east_shift, 1), tail)
            tail = jnp.where(high & west_c, pltpu.roll(corner[BL], west_shift, 1), tail)
            from_b[a, :, pl.ds(384, 128)] = tail
        coef_base = slots * fields
        assemble(cn, north_ref[...], coef_base)
        assemble(ce, east_ref[...], coef_base + 1)

        @pl.when(lax.axis_index("lat") == lax.axis_size("lat") - 1)
        def _():
            last = TOP + height - 8
            sub8 = lax.broadcasted_iota(jnp.int32, (8, COLS), 0)
            cn[pl.ds(last, 8), :] = jnp.where(sub8 == 7, jnp.float32(0.0), cn[pl.ds(last, 8), :])

        zero8 = jnp.zeros((8, COLS), jnp.float32)
        ca[pl.ds(8, rows - 16), :] = cn[pl.ds(7, rows - 16), :]
        ca[pl.ds(0, 8), :] = zero8
        ca[pl.ds(rows - 8, 8), :] = zero8
        cw[...] = pltpu.roll(ce[...], 1, 1)
        cd[...] = 2.0 - (cn[...] + ca[...] + ce[...] + cw[...])
        acc[...] = jnp.zeros_like(acc)

    member = lax.axis_index("pair")
    row_first = lax.axis_index("lat") * height
    col_first = lax.axis_index("lon") * breadth
    slot = member * slots + s
    act = jnp.where(s < pc_ref[member], jnp.float32(1.0), jnp.float32(0.0))

    places = []
    for comp in range(2):
        cell = sc_ref[pl_ref[comp, slot]]
        r = lax.div(cell, nlon)
        c = cell - r * nlon
        rb = r - row_first + TOP
        d = c - col_first
        d = jnp.where(d < 0, d + nlon, d)
        near = d < breadth + HALO
        wrap = d >= nlon - HALO
        cb = jnp.where(near, d, d - nlon + COLS)
        valid = (rb >= TOP - HALO) & (rb < TOP + height + HALO) & (near | wrap)
        places.append((rb, cb, valid))

    for comp in range(2):
        assemble(bufs.at[comp, 0], f_ref[0, comp].astype(jnp.float32), s * fields + comp)
        assemble(bufs.at[comp, 1], f_ref[0, 2 + comp].astype(jnp.float32), s * fields + 2 + comp)

    sub = lax.broadcasted_iota(jnp.int32, (8, COLS), 0)
    lane8 = lax.broadcasted_iota(jnp.int32, (8, COLS), 1)
    blocks = rows // 8

    for t in range(steps):
        ei, ci, ni = t % 3, (t + 1) % 3, (t + 2) % 3
        for comp in range(2):
            rb, cb, valid = places[comp]
            amp = wav_ref[t] if comp == 0 else res_ref[steps - 1 - t, slot]

            @pl.when(valid)
            def _():
                r8 = pl.multiple_of(lax.div(rb, 8) * 8, 8)
                slab = bufs[comp, ei, pl.ds(r8, 8), :]
                hit = (sub == rb - r8) & (lane8 == cb)
                bufs[comp, ei, pl.ds(r8, 8), :] = slab - jnp.where(hit, amp, jnp.float32(0.0))

        last = t == steps - 1
        first_block, end_block = (2, blocks - 2) if last else (1, blocks - 1)
        for k in range(first_block, end_block):
            r0 = 8 * k
            dd = cd[pl.ds(r0, 8), :]
            nn = cn[pl.ds(r0, 8), :]
            aa = ca[pl.ds(r0, 8), :]
            ee = ce[pl.ds(r0, 8), :]
            ww = cw[pl.ds(r0, 8), :]
            outs = []
            for comp in range(2):
                cur = bufs[comp, ci, pl.ds(r0, 8), :]
                above = bufs[comp, ci, pl.ds(r0 - 1, 8), :]
                below = bufs[comp, ci, pl.ds(r0 + 1, 8), :]
                ear = bufs[comp, ei, pl.ds(r0, 8), :]
                west = pltpu.roll(cur, 1, 1)
                east = pltpu.roll(cur, COLS - 1, 1)
                nxt = dd * cur + nn * below + aa * above + ee * east + ww * west - ear
                bufs[comp, ni, pl.ds(r0, 8), :] = nxt
                outs.append(nxt)
            if 2 <= k < blocks - 2:
                acc[pl.ds(r0 - TOP, 8), :] += (outs[0] * act) * outs[1]

    @pl.when(s == slots - 1)
    def _():
        o_ref[...] = acc[:, pl.ds(0, breadth)]


def propagate(wave_states, lat_faces, lon_faces, halos, scalars, nlon):
    slots, fields, height, breadth = wave_states.shape
    rows = height + 2 * TOP
    count = slots * fields + 2
    smem = pl.BlockSpec(memory_space=pltpu.SMEM)
    whole2 = lambda x: pl.BlockSpec(x.shape, lambda s: (0,) * x.ndim)
    return pl.pallas_call(
        functools.partial(wave_kernel, height, breadth, nlon),
        out_shape=jax.ShapeDtypeStruct((height, breadth), jnp.float32),
        grid=(slots,),
        in_specs=[smem] * 5
        + [
            pl.BlockSpec((1, fields, height, breadth), lambda s: (s, 0, 0, 0)),
            whole2(lat_faces),
            whole2(lon_faces),
        ]
        + [whole2(x) for x in halos],
        out_specs=pl.BlockSpec((height, breadth), lambda s: (0, 0)),
        scratch_shapes=[
            pltpu.VMEM((rows, COLS), jnp.float32),
            pltpu.VMEM((rows, COLS), jnp.float32),
            pltpu.VMEM((rows, COLS), jnp.float32),
            pltpu.VMEM((rows, COLS), jnp.float32),
            pltpu.VMEM((rows, COLS), jnp.float32),
            pltpu.VMEM((height, COLS), jnp.float32),
            pltpu.VMEM((2, 3, rows, COLS), jnp.float32),
            pltpu.VMEM((count, height, 128), jnp.float32),
            pltpu.VMEM((count, STRIP, COLS), jnp.float32),
            pltpu.VMEM((count, STRIP, COLS), jnp.float32),
        ],
        compiler_params=pltpu.CompilerParams(dimension_semantics=("arbitrary",)),
    )(*scalars, wave_states, lat_faces, lon_faces, *halos)


def body(
    wave_states,
    pair_list,
    pair_counts,
    residuals,
    station_cell,
    source_wavelet,
    lat_faces,
    lon_faces,
):
    height, breadth = lat_faces.shape
    nlon = breadth * lax.axis_size("lon")
    halos = exchange(wave_states, lat_faces, lon_faces)
    scalars = (pair_list.T, pair_counts, residuals.T, station_cell, source_wavelet)
    partial = propagate(wave_states, lat_faces, lon_faces, halos, scalars, nlon)
    other = lax.ppermute(partial, "pair", [(0, 1), (1, 0)])
    return partial + other


def solution(mesh):
    in_specs = (
        P("pair", None, "lat", "lon"),
        P(),
        P(),
        P(),
        P(),
        P(),
        P("lat", "lon"),
        P("lat", "lon"),
    )
    out_specs = P("lat", "lon")
    return jax.shard_map(body, mesh=mesh, in_specs=in_specs, out_specs=out_specs, check_vma=False)
```

```python
import functools

import jax
import jax.numpy as jnp
from jax import lax
from jax.experimental import pallas as pl
from jax.experimental.pallas import tpu as pltpu
from jax.sharding import PartitionSpec as P

HALO = 4
TOP = 16
COLS = 512
STRIP = 8
MESH = pl.DeviceIdType.MESH
TL, TR, BL, BR = 0, 1, 2, 3


def fused_kernel(
    nlon_cells,
    pl_ref, pc_ref, res_ref, sc_ref, wav_ref,
    f_ref, lat_ref, lon_ref,
    o_ref,
    X, work, ca, cw, cd, acc, pacc,
    pack_l, pack_r,
    send_lb, send_rb, send_lc, send_rc, send_tb, send_bb, send_tc, send_bc,
    rlb, rrb, rlc, rrc, rab, rbb, rac, rbc, rc,
    send_sem, recv_sem,
):
    slots, fields, height, breadth = f_ref.shape
    nfield = slots * fields
    count = nfield + 2
    rows = X.shape[1]
    blocks = rows // 8
    steps = wav_ref.shape[0]
    nlon = lax.axis_size("lon")
    nlat = lax.axis_size("lat")
    me_lat = lax.axis_index("lat")
    me_lon = lax.axis_index("lon")
    member = lax.axis_index("pair")
    partner = 1 - member
    right = lax.rem(me_lon + 1, nlon)
    left = lax.rem(me_lon + nlon - 1, nlon)
    has_up = me_lat > 0
    has_down = me_lat < nlat - 1
    up = jnp.maximum(me_lat - 1, 0)
    down = jnp.minimum(me_lat + 1, nlat - 1)
    cn = X.at[nfield]
    ce = X.at[nfield + 1]

    barrier = pltpu.get_barrier_semaphore()
    pl.semaphore_signal(barrier, 1, device_id={"pair": partner}, device_id_type=MESH)
    for lon_to in (left, right):
        pl.semaphore_signal(barrier, 1, device_id={"lon": lon_to}, device_id_type=MESH)

    @pl.when(has_up)
    def _():
        for lon_to in (me_lon, left, right):
            pl.semaphore_signal(barrier, 1, device_id={"lat": up, "lon": lon_to}, device_id_type=MESH)

    @pl.when(has_down)
    def _():
        for lon_to in (me_lon, left, right):
            pl.semaphore_signal(barrier, 1, device_id={"lat": down, "lon": lon_to}, device_id_type=MESH)

    lane = lax.broadcasted_iota(jnp.int32, (height, 128), 1)
    quad = lane // HALO
    sub8 = lax.broadcasted_iota(jnp.int32, (STRIP, COLS), 0)
    lane8 = lax.broadcasted_iota(jnp.int32, (STRIP, 128), 1)
    sub_c = lax.broadcasted_iota(jnp.int32, (STRIP, 128), 0)
    lane_w = lax.broadcasted_iota(jnp.int32, (STRIP, COLS), 1)
    zero_rows = jnp.zeros((TOP, COLS), jnp.float32)

    for a in range(count):
        if a < nfield:
            raw = f_ref[a // fields, a % fields].astype(jnp.float32)
        else:
            raw = (lat_ref if a == nfield else lon_ref)[...]
        X[a, pl.ds(TOP, height), pl.ds(0, breadth)] = raw
        tail = X[a, pl.ds(TOP, height), pl.ds(384, 128)]
        X[a, pl.ds(TOP, height), pl.ds(384, 128)] = jnp.where(lane < breadth - 384, tail, jnp.float32(0.0))
        X[a, pl.ds(0, TOP), :] = zero_rows
        X[a, pl.ds(TOP + height, rows - TOP - height), :] = zero_rows

    @pl.when(me_lat == nlat - 1)
    def _():
        last = TOP + height - 8
        cn[pl.ds(last, 8), :] = jnp.where(sub8 == 7, jnp.float32(0.0), cn[pl.ds(last, 8), :])

    pl_acc = jnp.zeros((height, 128), jnp.float32)
    pr_acc = jnp.zeros((height, 128), jnp.float32)
    for a in range(count):
        head = X[a, pl.ds(TOP, height), pl.ds(0, 128)]
        tail = X[a, pl.ds(TOP, height), pl.ds(384, 128)]
        pl_acc = jnp.where(quad == a, pltpu.roll(head, (HALO * a) % 128, 1), pl_acc)
        pr_acc = jnp.where(quad == a, pltpu.roll(tail, (HALO * a - (breadth - 384 - HALO)) % 128, 1), pr_acc)
    pack_l[...] = pl_acc
    pack_r[...] = pr_acc

    coef_lane = HALO * nfield
    width = 2 * HALO
    per_row = 128 // width
    send_lb[...] = pl_acc.astype(jnp.bfloat16)
    send_rb[...] = pr_acc.astype(jnp.bfloat16)
    for src, dst in ((pl_acc, send_lc), (pr_acc, send_rc)):
        for h in range(dst.shape[0] // STRIP):
            packed = jnp.zeros((STRIP, 128), jnp.float32)
            for g in range(per_row):
                i = h * per_row + g
                if i * STRIP >= height:
                    break
                blk = src[i * STRIP : (i + 1) * STRIP]
                packed = jnp.where(lane8 // width == g, pltpu.roll(blk, (width * g - coef_lane) % 128, 1), packed)
            dst[pl.ds(h * STRIP, STRIP), :] = packed

    def strip_pair(a, first, keep_low):
        lo = X[a, pl.ds(first, STRIP), :]
        hi = X[a + 1, pl.ds(first, STRIP), :]
        if keep_low:
            return jnp.where(sub8 < 4, lo, pltpu.roll(hi, 4, 0))
        return jnp.where(sub8 < 4, pltpu.roll(lo, 4, 0), hi)

    for dst_b, dst_c, first, keep_low in (
        (send_tb, send_tc, TOP, True),
        (send_bb, send_bc, TOP + height - STRIP, False),
    ):
        for j in range(dst_b.shape[0]):
            both = [strip_pair(4 * j, first, keep_low), strip_pair(4 * j + 2, first, keep_low)]
            dst_b[j] = jnp.concatenate(both, axis=0).astype(jnp.bfloat16)
        dst_c[...] = strip_pair(nfield, first, keep_low)

    pl.semaphore_wait(barrier, 3 + 3 * has_up.astype(jnp.int32) + 3 * has_down.astype(jnp.int32))

    last8 = pl.ds(height - STRIP, STRIP)
    first8 = pl.ds(0, STRIP)
    copies = [
        (send_rb, rlb, me_lat, right, None),
        (send_rc, rlc, me_lat, right, None),
        (send_lb, rrb, me_lat, left, None),
        (send_lc, rrc, me_lat, left, None),
        (send_tb, rbb, up, me_lon, "up"),
        (send_tc, rbc, up, me_lon, "up"),
        (send_bb, rab, down, me_lon, "down"),
        (send_bc, rac, down, me_lon, "down"),
        (pack_r.at[last8], rc.at[TL], down, right, "down"),
        (pack_l.at[last8], rc.at[TR], down, left, "down"),
        (pack_r.at[first8], rc.at[BL], up, right, "up"),
        (pack_l.at[first8], rc.at[BR], up, left, "up"),
    ]

    def descriptor(i):
        src, dst, lat_to, lon_to, _ = copies[i]
        return pltpu.make_async_remote_copy(
            src, dst, send_sem.at[i], recv_sem.at[i], device_id={"lat": lat_to, "lon": lon_to}, device_id_type=MESH
        )

    def when(cond, fn):
        if cond is None:
            fn()
        else:
            pl.when(has_up if cond == "up" else has_down)(fn)

    def finish(i):
        cond = copies[i][4]
        when(cond, lambda: descriptor(i).wait_send())
        mirror = {None: None, "up": "down", "down": "up"}[cond]
        when(mirror, lambda: descriptor(i).wait_recv())

    for i, copy in enumerate(copies):
        when(copy[4], lambda i=i: descriptor(i).start())

    for i in range(4):
        finish(i)
    east_gap = (lane >= breadth - 384) & (lane < breadth - 384 + HALO)
    west_gap = lane >= 128 - HALO
    unpacked = []
    for src_b, src_c in ((rlb, rlc), (rrb, rrc)):
        fields_part = src_b[...].astype(jnp.float32)
        parts = []
        for i in range(height // STRIP):
            h, g = divmod(i, per_row)
            blk_c = pltpu.roll(src_c[pl.ds(h * STRIP, STRIP), :], (coef_lane - width * g) % 128, 1)
            blk_f = fields_part[i * STRIP : (i + 1) * STRIP]
            parts.append(jnp.where(lane8 < coef_lane, blk_f, blk_c))
        unpacked.append(jnp.concatenate(parts, axis=0))
    from_l, from_r = unpacked
    for a in range(count):
        east_shift = (breadth - 384 - HALO * a) % 128
        west_shift = (128 - HALO - HALO * a) % 128
        tail = X[a, pl.ds(TOP, height), pl.ds(384, 128)]
        tail = jnp.where(east_gap, pltpu.roll(from_r, east_shift, 1), tail)
        tail = jnp.where(west_gap, pltpu.roll(from_l, west_shift, 1), tail)
        X[a, pl.ds(TOP, height), pl.ds(384, 128)] = tail

    def derive(first, size):
        ca[pl.ds(first, size), :] = cn[pl.ds(first - 1, size), :]
        cw[pl.ds(first, size), :] = pltpu.roll(ce[pl.ds(first, size), :], 1, 1)
        cd[pl.ds(first, size), :] = 2.0 - (
            cn[pl.ds(first, size), :] + ca[pl.ds(first, size), :] + ce[pl.ds(first, size), :] + cw[pl.ds(first, size), :]
        )

    derive(8, rows - 16)
    acc[...] = jnp.zeros_like(acc)

    def slot_places(s):
        slot = member * slots + s
        act = jnp.where(s < pc_ref[member], jnp.float32(1.0), jnp.float32(0.0))
        row_first = me_lat * height
        col_first = me_lon * breadth
        places = []
        for comp in range(2):
            cell = sc_ref[pl_ref[comp, slot]]
            r = lax.div(cell, nlon_cells)
            c = cell - r * nlon_cells
            rb = r - row_first + TOP
            d = c - col_first
            d = jnp.where(d < 0, d + nlon_cells, d)
            near = d < breadth + HALO
            wrap = d >= nlon_cells - HALO
            cb = jnp.where(near, d, d - nlon_cells + COLS)
            valid = (rb >= TOP - HALO) & (rb < TOP + height + HALO) & (near | wrap)
            hit = (sub8 == lax.rem(jnp.maximum(rb, 0), 8)) & (lane_w == cb)
            amps = [wav_ref[t] if comp == 0 else res_ref[steps - 1 - t, slot] for t in range(steps)]
            places.append((rb, valid, hit, amps))
        return act, places

    def run_blocks(s, t, block_list, act, places):
        bufs = [(X.at[s * fields + comp], X.at[s * fields + 2 + comp], work.at[s, comp]) for comp in range(2)]
        ei, ci, ni = t % 3, (t + 1) % 3, (t + 2) % 3
        for k in block_list:
            r0 = 8 * k
            dd = cd[pl.ds(r0, 8), :]
            nn = cn[pl.ds(r0, 8), :]
            aa = ca[pl.ds(r0, 8), :]
            ee = ce[pl.ds(r0, 8), :]
            ww = cw[pl.ds(r0, 8), :]
            outs = []
            for comp in range(2):
                rb, valid, hit, amps = places[comp]
                amp = jnp.where(valid & (rb >= r0) & (rb < r0 + 8), amps[t], jnp.float32(0.0))
                cur_ref, ear_ref, nxt_ref = bufs[comp][ci], bufs[comp][ei], bufs[comp][ni]
                cur = cur_ref[pl.ds(r0, 8), :]
                above = cur_ref[pl.ds(r0 - 1, 8), :]
                below = cur_ref[pl.ds(r0 + 1, 8), :]
                ear = ear_ref[pl.ds(r0, 8), :]
                west = pltpu.roll(cur, 1, 1)
                east = pltpu.roll(cur, COLS - 1, 1)
                nxt = dd * cur + nn * below + aa * above + ee * east + ww * west - ear
                nxt = nxt + jnp.where(hit, amp, jnp.float32(0.0))
                nxt_ref[pl.ds(r0, 8), :] = nxt
                outs.append(nxt)
            if 2 <= k < blocks - 2:
                acc[pl.ds(r0 - TOP, 8), :] += (outs[0] * act) * outs[1]

    def phase(ranges):
        def body(s, carry):
            act, places = slot_places(s)
            for t in range(steps):
                run_blocks(s, t, ranges(t), act, places)
            return carry

        lax.fori_loop(0, slots, body, 0)

    inner = lambda t: list(range(3 + t, blocks - 3 - t))
    phase(inner)

    for i in range(4, len(copies)):
        finish(i)

    @pl.when(jnp.logical_not(has_up))
    def _():
        rab[...] = jnp.zeros_like(rab)
        rac[...] = jnp.zeros_like(rac)
        rc[TL] = jnp.zeros((STRIP, 128), jnp.float32)
        rc[TR] = jnp.zeros((STRIP, 128), jnp.float32)

    @pl.when(jnp.logical_not(has_down))
    def _():
        rbb[...] = jnp.zeros_like(rbb)
        rbc[...] = jnp.zeros_like(rbc)
        rc[BL] = jnp.zeros((STRIP, 128), jnp.float32)
        rc[BR] = jnp.zeros((STRIP, 128), jnp.float32)

    east_c = (lane8 >= breadth - 384) & (lane8 < breadth - 384 + HALO)
    west_c = lane8 >= 128 - HALO
    for src_b, src_c, first, low_half, (c_east, c_west) in (
        (rab, rac, TOP - STRIP, False, (TR, TL)),
        (rbb, rbc, TOP + height, True, (BR, BL)),
    ):
        for a in range(count):
            b = a // 2
            if a < nfield:
                both = src_b[b // 2].astype(jnp.float32)
                blk = both[STRIP * (b % 2) : STRIP * (b % 2 + 1)]
            else:
                blk = src_c[...]
            even = a % 2 == 0
            if low_half:
                blk = blk if even else pltpu.roll(blk, 4, 0)
                blk = jnp.where(sub8 < 4, blk, jnp.float32(0.0))
                band = sub_c < 4
            else:
                blk = pltpu.roll(blk, 4, 0) if even else blk
                blk = jnp.where(sub8 >= 4, blk, jnp.float32(0.0))
                band = sub_c >= 4
            X[a, pl.ds(first, STRIP), :] = blk
            east_shift = (breadth - 384 - HALO * a) % 128
            west_shift = (128 - HALO - HALO * a) % 128
            tail = X[a, pl.ds(first, STRIP), pl.ds(384, 128)]
            tail = jnp.where(band & east_c, pltpu.roll(rc[c_east], east_shift, 1), tail)
            tail = jnp.where(band & west_c, pltpu.roll(rc[c_west], west_shift, 1), tail)
            X[a, pl.ds(first, STRIP), pl.ds(384, 128)] = tail

    derive(8, 24)
    derive(rows - 32, 24)

    def outer(t):
        if t < steps - 1:
            return list(range(1, 3 + t)) + list(range(blocks - 3 - t, blocks - 1))
        return list(range(2, 3 + t)) + list(range(blocks - 3 - t, blocks - 2))

    phase(outer)

    to_partner = pltpu.make_async_remote_copy(
        acc, pacc, send_sem.at[len(copies)], recv_sem.at[len(copies)], device_id={"pair": partner}, device_id_type=MESH
    )
    to_partner.start()
    to_partner.wait()
    o_ref[...] = (acc[...] + pacc[...])[:, 0:breadth]


def fused(wave_states, lat_faces, lon_faces, scalars, nlon_cells):
    slots, fields, height, breadth = wave_states.shape
    nfield = slots * fields
    count = nfield + 2
    rows = height + 2 * TOP
    smem = pl.BlockSpec(memory_space=pltpu.SMEM)
    vmem = pl.BlockSpec(memory_space=pltpu.VMEM)
    per_row = 128 // (2 * HALO)
    coef_rows = STRIP * ((height // STRIP + per_row - 1) // per_row)
    packed_b = pltpu.VMEM((height, 128), jnp.bfloat16)
    packed_c = pltpu.VMEM((coef_rows, 128), jnp.float32)
    strip_b16 = pltpu.VMEM((nfield // 4, 2 * STRIP, COLS), jnp.bfloat16)
    strip_c = pltpu.VMEM((STRIP, COLS), jnp.float32)
    plane = pltpu.VMEM((rows, COLS), jnp.float32)
    return pl.pallas_call(
        functools.partial(fused_kernel, nlon_cells),
        out_shape=jax.ShapeDtypeStruct((height, breadth), jnp.float32),
        in_specs=[smem] * 5 + [vmem] * 3,
        out_specs=vmem,
        scratch_shapes=[
            pltpu.VMEM((count, rows, COLS), jnp.float32),
            pltpu.VMEM((slots, 2, rows, COLS), jnp.float32),
            plane,
            plane,
            plane,
            pltpu.VMEM((height, COLS), jnp.float32),
            pltpu.VMEM((height, COLS), jnp.float32),
            pltpu.VMEM((height, 128), jnp.float32),
            pltpu.VMEM((height, 128), jnp.float32),
        ]
        + [packed_b, packed_b, packed_c, packed_c, strip_b16, strip_b16, strip_c, strip_c] * 2
        + [
            pltpu.VMEM((4, STRIP, 128), jnp.float32),
            pltpu.SemaphoreType.DMA((13,)),
            pltpu.SemaphoreType.DMA((13,)),
        ],
        compiler_params=pltpu.CompilerParams(collective_id=0, has_side_effects=True, vmem_limit_bytes=60 * 1024 * 1024),
    )(*scalars, wave_states, lat_faces, lon_faces)


def body(
    wave_states,
    pair_list,
    pair_counts,
    residuals,
    station_cell,
    source_wavelet,
    lat_faces,
    lon_faces,
):
    height, breadth = lat_faces.shape
    nlon_cells = breadth * lax.axis_size("lon")
    scalars = (pair_list.T, pair_counts, residuals.T, station_cell, source_wavelet)
    return fused(wave_states, lat_faces, lon_faces, scalars, nlon_cells)


def solution(mesh):
    in_specs = (
        P("pair", None, "lat", "lon"),
        P(),
        P(),
        P(),
        P(),
        P(),
        P("lat", "lon"),
        P("lat", "lon"),
    )
    out_specs = P("lat", "lon")
    return jax.shard_map(body, mesh=mesh, in_specs=in_specs, out_specs=out_specs, check_vma=False)
```

```python
import functools

import jax
import jax.numpy as jnp
from jax import lax
from jax.experimental import pallas as pl
from jax.experimental.pallas import tpu as pltpu
from jax.sharding import PartitionSpec as P

HALO = 4
TOP = 16
COLS = 512
STRIP = 8
MESH = pl.DeviceIdType.MESH
TL, TR, BL, BR = 0, 1, 2, 3


def fused_kernel(
    nlon_cells,
    pl_ref, pc_ref, res_ref, sc_ref, wav_ref,
    f_hbm, lat_hbm, lon_hbm,
    o_ref,
    f_ref, lat_ref, lon_ref, in_sem, src_tiles,
    X, work, ca, cw, cd, acc, pacc,
    pack_l, pack_r,
    send_lb, send_rb, send_lc, send_rc, send_tb, send_bb, send_tc, send_bc,
    rlb, rrb, rlc, rrc, rab, rbb, rac, rbc, rc,
    send_sem, recv_sem,
):
    slots, fields, height, breadth = f_ref.shape
    nfield = slots * fields
    count = nfield + 2
    rows = X.shape[1]
    blocks = rows // 8
    steps = wav_ref.shape[0]
    nlon = lax.axis_size("lon")
    nlat = lax.axis_size("lat")
    me_lat = lax.axis_index("lat")
    me_lon = lax.axis_index("lon")
    member = lax.axis_index("pair")
    partner = 1 - member
    right = lax.rem(me_lon + 1, nlon)
    left = lax.rem(me_lon + nlon - 1, nlon)
    has_up = me_lat > 0
    has_down = me_lat < nlat - 1
    up = jnp.maximum(me_lat - 1, 0)
    down = jnp.minimum(me_lat + 1, nlat - 1)
    cn = X.at[nfield]
    ce = X.at[nfield + 1]

    barrier = pltpu.get_barrier_semaphore()
    pl.semaphore_signal(barrier, 1, device_id={"pair": partner}, device_id_type=MESH)
    for lon_to in (left, right):
        pl.semaphore_signal(barrier, 1, device_id={"lon": lon_to}, device_id_type=MESH)

    @pl.when(has_up)
    def _():
        for lon_to in (me_lon, left, right):
            pl.semaphore_signal(barrier, 1, device_id={"lat": up, "lon": lon_to}, device_id_type=MESH)

    @pl.when(has_down)
    def _():
        for lon_to in (me_lon, left, right):
            pl.semaphore_signal(barrier, 1, device_id={"lat": down, "lon": lon_to}, device_id_type=MESH)

    loads = [pltpu.make_async_copy(f_hbm.at[i], f_ref.at[i], in_sem.at[i]) for i in range(slots)]
    loads.append(pltpu.make_async_copy(lat_hbm, lat_ref, in_sem.at[slots]))
    loads.append(pltpu.make_async_copy(lon_hbm, lon_ref, in_sem.at[slots + 1]))
    for copy in loads:
        copy.start()

    lane = lax.broadcasted_iota(jnp.int32, (height, 128), 1)
    quad = lane // HALO
    sub8 = lax.broadcasted_iota(jnp.int32, (STRIP, COLS), 0)
    lane8 = lax.broadcasted_iota(jnp.int32, (STRIP, 128), 1)
    sub_c = lax.broadcasted_iota(jnp.int32, (STRIP, 128), 0)
    lane_w = lax.broadcasted_iota(jnp.int32, (STRIP, COLS), 1)
    zero_rows = jnp.zeros((TOP, COLS), jnp.float32)

    for a in range(count):
        if a % fields == 0 and a < nfield:
            loads[a // fields].wait()
        if a == nfield:
            loads[slots].wait()
            loads[slots + 1].wait()
        if a < nfield:
            raw = f_ref[a // fields, a % fields].astype(jnp.float32)
        else:
            raw = (lat_ref if a == nfield else lon_ref)[...]
        X[a, pl.ds(TOP, height), pl.ds(0, breadth)] = raw
        tail = X[a, pl.ds(TOP, height), pl.ds(384, 128)]
        X[a, pl.ds(TOP, height), pl.ds(384, 128)] = jnp.where(lane < breadth - 384, tail, jnp.float32(0.0))
        X[a, pl.ds(0, TOP), :] = zero_rows
        X[a, pl.ds(TOP + height, rows - TOP - height), :] = zero_rows

    @pl.when(me_lat == nlat - 1)
    def _():
        last = TOP + height - 8
        cn[pl.ds(last, 8), :] = jnp.where(sub8 == 7, jnp.float32(0.0), cn[pl.ds(last, 8), :])

    pl_acc = jnp.zeros((height, 128), jnp.float32)
    pr_acc = jnp.zeros((height, 128), jnp.float32)
    for a in range(count):
        head = X[a, pl.ds(TOP, height), pl.ds(0, 128)]
        tail = X[a, pl.ds(TOP, height), pl.ds(384, 128)]
        pl_acc = jnp.where(quad == a, pltpu.roll(head, (HALO * a) % 128, 1), pl_acc)
        pr_acc = jnp.where(quad == a, pltpu.roll(tail, (HALO * a - (breadth - 384 - HALO)) % 128, 1), pr_acc)
    pack_l[...] = pl_acc
    pack_r[...] = pr_acc

    coef_lane = HALO * nfield
    width = 2 * HALO
    per_row = 128 // width
    send_lb[...] = pl_acc.astype(jnp.bfloat16)
    send_rb[...] = pr_acc.astype(jnp.bfloat16)
    for src, dst in ((pl_acc, send_lc), (pr_acc, send_rc)):
        for h in range(dst.shape[0] // STRIP):
            packed = jnp.zeros((STRIP, 128), jnp.float32)
            for g in range(per_row):
                i = h * per_row + g
                if i * STRIP >= height:
                    break
                blk = src[i * STRIP : (i + 1) * STRIP]
                packed = jnp.where(lane8 // width == g, pltpu.roll(blk, (width * g - coef_lane) % 128, 1), packed)
            dst[pl.ds(h * STRIP, STRIP), :] = packed

    def strip_pair(a, first, keep_low):
        lo = X[a, pl.ds(first, STRIP), :]
        hi = X[a + 1, pl.ds(first, STRIP), :]
        if keep_low:
            return jnp.where(sub8 < 4, lo, pltpu.roll(hi, 4, 0))
        return jnp.where(sub8 < 4, pltpu.roll(lo, 4, 0), hi)

    for dst_b, dst_c, first, keep_low in (
        (send_tb, send_tc, TOP, True),
        (send_bb, send_bc, TOP + height - STRIP, False),
    ):
        for j in range(dst_b.shape[0]):
            both = [strip_pair(4 * j, first, keep_low), strip_pair(4 * j + 2, first, keep_low)]
            dst_b[j] = jnp.concatenate(both, axis=0).astype(jnp.bfloat16)
        dst_c[...] = strip_pair(nfield, first, keep_low)

    pl.semaphore_wait(barrier, 3 + 3 * has_up.astype(jnp.int32) + 3 * has_down.astype(jnp.int32))

    last8 = pl.ds(height - STRIP, STRIP)
    first8 = pl.ds(0, STRIP)
    copies = [
        (send_rb, rlb, me_lat, right, None),
        (send_rc, rlc, me_lat, right, None),
        (send_lb, rrb, me_lat, left, None),
        (send_lc, rrc, me_lat, left, None),
        (send_tb, rbb, up, me_lon, "up"),
        (send_tc, rbc, up, me_lon, "up"),
        (send_bb, rab, down, me_lon, "down"),
        (send_bc, rac, down, me_lon, "down"),
        (pack_r.at[last8], rc.at[TL], down, right, "down"),
        (pack_l.at[last8], rc.at[TR], down, left, "down"),
        (pack_r.at[first8], rc.at[BL], up, right, "up"),
        (pack_l.at[first8], rc.at[BR], up, left, "up"),
    ]

    def descriptor(i):
        src, dst, lat_to, lon_to, _ = copies[i]
        return pltpu.make_async_remote_copy(
            src, dst, send_sem.at[i], recv_sem.at[i], device_id={"lat": lat_to, "lon": lon_to}, device_id_type=MESH
        )

    def when(cond, fn):
        if cond is None:
            fn()
        else:
            pl.when(has_up if cond == "up" else has_down)(fn)

    def finish(i):
        cond = copies[i][4]
        when(cond, lambda: descriptor(i).wait_send())
        mirror = {None: None, "up": "down", "down": "up"}[cond]
        when(mirror, lambda: descriptor(i).wait_recv())

    for i, copy in enumerate(copies):
        when(copy[4], lambda i=i: descriptor(i).start())

    for i in range(4):
        finish(i)
    east_gap = (lane >= breadth - 384) & (lane < breadth - 384 + HALO)
    west_gap = lane >= 128 - HALO
    unpacked = []
    for src_b, src_c in ((rlb, rlc), (rrb, rrc)):
        fields_part = src_b[...].astype(jnp.float32)
        parts = []
        for i in range(height // STRIP):
            h, g = divmod(i, per_row)
            blk_c = pltpu.roll(src_c[pl.ds(h * STRIP, STRIP), :], (coef_lane - width * g) % 128, 1)
            blk_f = fields_part[i * STRIP : (i + 1) * STRIP]
            parts.append(jnp.where(lane8 < coef_lane, blk_f, blk_c))
        unpacked.append(jnp.concatenate(parts, axis=0))
    from_l, from_r = unpacked
    for a in range(count):
        east_shift = (breadth - 384 - HALO * a) % 128
        west_shift = (128 - HALO - HALO * a) % 128
        tail = X[a, pl.ds(TOP, height), pl.ds(384, 128)]
        tail = jnp.where(east_gap, pltpu.roll(from_r, east_shift, 1), tail)
        tail = jnp.where(west_gap, pltpu.roll(from_l, west_shift, 1), tail)
        X[a, pl.ds(TOP, height), pl.ds(384, 128)] = tail

    def derive(first, size):
        ca[pl.ds(first, size), :] = cn[pl.ds(first - 1, size), :]
        cw[pl.ds(first, size), :] = pltpu.roll(ce[pl.ds(first, size), :], 1, 1)
        cd[pl.ds(first, size), :] = 2.0 - (
            cn[pl.ds(first, size), :] + ca[pl.ds(first, size), :] + ce[pl.ds(first, size), :] + cw[pl.ds(first, size), :]
        )

    derive(8, rows - 16)
    acc[...] = jnp.zeros_like(acc)
    src_tiles[:, :, 0] = jnp.zeros((2, steps, STRIP, COLS), jnp.float32)

    def slot_places(s):
        slot = member * slots + s
        act = jnp.where(s < pc_ref[member], jnp.float32(1.0), jnp.float32(0.0))
        row_first = me_lat * height
        col_first = me_lon * breadth
        places = []
        for comp in range(2):
            cell = sc_ref[pl_ref[comp, slot]]
            r = lax.div(cell, nlon_cells)
            c = cell - r * nlon_cells
            rb = r - row_first + TOP
            d = c - col_first
            d = jnp.where(d < 0, d + nlon_cells, d)
            near = d < breadth + HALO
            wrap = d >= nlon_cells - HALO
            cb = jnp.where(near, d, d - nlon_cells + COLS)
            valid = (rb >= TOP - HALO) & (rb < TOP + height + HALO) & (near | wrap)
            hit = (sub8 == lax.rem(jnp.maximum(rb, 0), 8)) & (lane_w == cb)
            for t in range(steps):
                amp = wav_ref[t] if comp == 0 else res_ref[steps - 1 - t, slot]
                src_tiles[comp, t, 1] = jnp.where(hit, amp, jnp.float32(0.0))
            places.append((rb, valid))
        return act, places

    def run_blocks(s, t, block_list, act, places):
        bufs = [(X.at[s * fields + comp], X.at[s * fields + 2 + comp], work.at[s, comp]) for comp in range(2)]
        ei, ci, ni = t % 3, (t + 1) % 3, (t + 2) % 3
        for k in block_list:
            r0 = 8 * k
            dd = cd[pl.ds(r0, 8), :]
            nn = cn[pl.ds(r0, 8), :]
            aa = ca[pl.ds(r0, 8), :]
            ee = ce[pl.ds(r0, 8), :]
            ww = cw[pl.ds(r0, 8), :]
            outs = []
            for comp in range(2):
                rb, valid = places[comp]
                pick = (valid & (rb >= r0) & (rb < r0 + 8)).astype(jnp.int32)
                cur_ref, ear_ref, nxt_ref = bufs[comp][ci], bufs[comp][ei], bufs[comp][ni]
                cur = cur_ref[pl.ds(r0, 8), :]
                above = cur_ref[pl.ds(r0 - 1, 8), :]
                below = cur_ref[pl.ds(r0 + 1, 8), :]
                ear = ear_ref[pl.ds(r0, 8), :]
                west = pltpu.roll(cur, 1, 1)
                east = pltpu.roll(cur, COLS - 1, 1)
                nxt = dd * cur + nn * below + aa * above + ee * east + ww * west - ear
                nxt = nxt + src_tiles[comp, t, pick]
                nxt_ref[pl.ds(r0, 8), :] = nxt
                outs.append(nxt)
            if 2 <= k < blocks - 2:
                acc[pl.ds(r0 - TOP, 8), :] += (outs[0] * act) * outs[1]

    def phase(ranges):
        def body(s, carry):
            act, places = slot_places(s)
            for t in range(steps):
                run_blocks(s, t, ranges(t), act, places)
            return carry

        lax.fori_loop(0, slots, body, 0)

    inner = lambda t: list(range(3 + t, blocks - 3 - t))
    phase(inner)

    for i in range(4, len(copies)):
        finish(i)

    @pl.when(jnp.logical_not(has_up))
    def _():
        rab[...] = jnp.zeros_like(rab)
        rac[...] = jnp.zeros_like(rac)
        rc[TL] = jnp.zeros((STRIP, 128), jnp.float32)
        rc[TR] = jnp.zeros((STRIP, 128), jnp.float32)

    @pl.when(jnp.logical_not(has_down))
    def _():
        rbb[...] = jnp.zeros_like(rbb)
        rbc[...] = jnp.zeros_like(rbc)
        rc[BL] = jnp.zeros((STRIP, 128), jnp.float32)
        rc[BR] = jnp.zeros((STRIP, 128), jnp.float32)

    east_c = (lane8 >= breadth - 384) & (lane8 < breadth - 384 + HALO)
    west_c = lane8 >= 128 - HALO
    for src_b, src_c, first, low_half, (c_east, c_west) in (
        (rab, rac, TOP - STRIP, False, (TR, TL)),
        (rbb, rbc, TOP + height, True, (BR, BL)),
    ):
        for a in range(count):
            b = a // 2
            if a < nfield:
                both = src_b[b // 2].astype(jnp.float32)
                blk = both[STRIP * (b % 2) : STRIP * (b % 2 + 1)]
            else:
                blk = src_c[...]
            even = a % 2 == 0
            if low_half:
                blk = blk if even else pltpu.roll(blk, 4, 0)
                blk = jnp.where(sub8 < 4, blk, jnp.float32(0.0))
                band = sub_c < 4
            else:
                blk = pltpu.roll(blk, 4, 0) if even else blk
                blk = jnp.where(sub8 >= 4, blk, jnp.float32(0.0))
                band = sub_c >= 4
            X[a, pl.ds(first, STRIP), :] = blk
            east_shift = (breadth - 384 - HALO * a) % 128
            west_shift = (128 - HALO - HALO * a) % 128
            tail = X[a, pl.ds(first, STRIP), pl.ds(384, 128)]
            tail = jnp.where(band & east_c, pltpu.roll(rc[c_east], east_shift, 1), tail)
            tail = jnp.where(band & west_c, pltpu.roll(rc[c_west], west_shift, 1), tail)
            X[a, pl.ds(first, STRIP), pl.ds(384, 128)] = tail

    derive(8, 24)
    derive(rows - 32, 24)

    def outer(t):
        if t < steps - 1:
            return list(range(1, 3 + t)) + list(range(blocks - 3 - t, blocks - 1))
        return list(range(2, 3 + t)) + list(range(blocks - 3 - t, blocks - 2))

    phase(outer)

    to_partner = pltpu.make_async_remote_copy(
        acc, pacc, send_sem.at[len(copies)], recv_sem.at[len(copies)], device_id={"pair": partner}, device_id_type=MESH
    )
    to_partner.start()
    to_partner.wait()
    o_ref[...] = (acc[...] + pacc[...])[:, 0:breadth]


def fused(wave_states, lat_faces, lon_faces, scalars, nlon_cells):
    slots, fields, height, breadth = wave_states.shape
    nfield = slots * fields
    count = nfield + 2
    rows = height + 2 * TOP
    smem = pl.BlockSpec(memory_space=pltpu.SMEM)
    vmem = pl.BlockSpec(memory_space=pltpu.VMEM)
    per_row = 128 // (2 * HALO)
    coef_rows = STRIP * ((height // STRIP + per_row - 1) // per_row)
    packed_b = pltpu.VMEM((height, 128), jnp.bfloat16)
    packed_c = pltpu.VMEM((coef_rows, 128), jnp.float32)
    strip_b16 = pltpu.VMEM((nfield // 4, 2 * STRIP, COLS), jnp.bfloat16)
    strip_c = pltpu.VMEM((STRIP, COLS), jnp.float32)
    plane = pltpu.VMEM((rows, COLS), jnp.float32)
    return pl.pallas_call(
        functools.partial(fused_kernel, nlon_cells),
        out_shape=jax.ShapeDtypeStruct((height, breadth), jnp.float32),
        in_specs=[smem] * 5 + [pl.BlockSpec(memory_space=pl.ANY)] * 3,
        out_specs=vmem,
        scratch_shapes=[
            pltpu.VMEM(wave_states.shape, wave_states.dtype),
            pltpu.VMEM(lat_faces.shape, jnp.float32),
            pltpu.VMEM(lon_faces.shape, jnp.float32),
            pltpu.SemaphoreType.DMA((slots + 2,)),
            pltpu.VMEM((2, 4, 2, STRIP, COLS), jnp.float32),
            pltpu.VMEM((count, rows, COLS), jnp.float32),
            pltpu.VMEM((slots, 2, rows, COLS), jnp.float32),
            plane,
            plane,
            plane,
            pltpu.VMEM((height, COLS), jnp.float32),
            pltpu.VMEM((height, COLS), jnp.float32),
            pltpu.VMEM((height, 128), jnp.float32),
            pltpu.VMEM((height, 128), jnp.float32),
        ]
        + [packed_b, packed_b, packed_c, packed_c, strip_b16, strip_b16, strip_c, strip_c] * 2
        + [
            pltpu.VMEM((4, STRIP, 128), jnp.float32),
            pltpu.SemaphoreType.DMA((13,)),
            pltpu.SemaphoreType.DMA((13,)),
        ],
        compiler_params=pltpu.CompilerParams(collective_id=0, has_side_effects=True, vmem_limit_bytes=60 * 1024 * 1024),
    )(*scalars, wave_states, lat_faces, lon_faces)


def body(
    wave_states,
    pair_list,
    pair_counts,
    residuals,
    station_cell,
    source_wavelet,
    lat_faces,
    lon_faces,
):
    height, breadth = lat_faces.shape
    nlon_cells = breadth * lax.axis_size("lon")
    scalars = (pair_list.T, pair_counts, residuals.T, station_cell, source_wavelet)
    return fused(wave_states, lat_faces, lon_faces, scalars, nlon_cells)


def solution(mesh):
    in_specs = (
        P("pair", None, "lat", "lon"),
        P(),
        P(),
        P(),
        P(),
        P(),
        P("lat", "lon"),
        P("lat", "lon"),
    )
    out_specs = P("lat", "lon")
    return jax.shard_map(body, mesh=mesh, in_specs=in_specs, out_specs=out_specs, check_vma=False)
```

```python
import functools

import jax
import jax.numpy as jnp
from jax import lax
from jax.experimental import pallas as pl
from jax.experimental.pallas import tpu as pltpu
from jax.sharding import PartitionSpec as P

HALO = 4
TOP = 16
COLS = 512
STRIP = 8
MESH = pl.DeviceIdType.MESH
TL, TR, BL, BR = 0, 1, 2, 3
SPLIT = 80


def fused_kernel(
    nlon_cells,
    pl_ref, pc_ref, res_ref, sc_ref, wav_ref,
    f_hbm, lat_hbm, lon_hbm,
    o_ref,
    f_ref, lat_ref, lon_ref, in_sem, src_tiles,
    X, work, ca, cw, cd, acc, pacc, SX, swork, sa, sw, sd, seam_src,
    pack_l, pack_r,
    send_lb, send_rb, send_lc, send_rc, send_tb, send_bb, send_tc, send_bc,
    rlb, rrb, rlc, rrc, rab, rbb, rac, rbc, rc,
    send_sem, recv_sem,
):
    slots, fields, height, breadth = f_ref.shape
    nfield = slots * fields
    count = nfield + 2
    rows = X.shape[1]
    blocks = rows // 8
    steps = wav_ref.shape[0]
    nlon = lax.axis_size("lon")
    nlat = lax.axis_size("lat")
    me_lat = lax.axis_index("lat")
    me_lon = lax.axis_index("lon")
    member = lax.axis_index("pair")
    partner = 1 - member
    right = lax.rem(me_lon + 1, nlon)
    left = lax.rem(me_lon + nlon - 1, nlon)
    has_up = me_lat > 0
    has_down = me_lat < nlat - 1
    up = jnp.maximum(me_lat - 1, 0)
    down = jnp.minimum(me_lat + 1, nlat - 1)
    cn = X.at[nfield]
    ce = X.at[nfield + 1]

    barrier = pltpu.get_barrier_semaphore()
    pl.semaphore_signal(barrier, 1, device_id={"pair": partner}, device_id_type=MESH)
    for lon_to in (left, right):
        pl.semaphore_signal(barrier, 1, device_id={"lon": lon_to}, device_id_type=MESH)

    @pl.when(has_up)
    def _():
        for lon_to in (me_lon, left, right):
            pl.semaphore_signal(barrier, 1, device_id={"lat": up, "lon": lon_to}, device_id_type=MESH)

    @pl.when(has_down)
    def _():
        for lon_to in (me_lon, left, right):
            pl.semaphore_signal(barrier, 1, device_id={"lat": down, "lon": lon_to}, device_id_type=MESH)

    loads = [pltpu.make_async_copy(f_hbm.at[i], f_ref.at[i], in_sem.at[i]) for i in range(slots)]
    loads.append(pltpu.make_async_copy(lat_hbm, lat_ref, in_sem.at[slots]))
    loads.append(pltpu.make_async_copy(lon_hbm, lon_ref, in_sem.at[slots + 1]))
    for copy in loads:
        copy.start()

    lane = lax.broadcasted_iota(jnp.int32, (height, 128), 1)
    quad = lane // HALO
    sub8 = lax.broadcasted_iota(jnp.int32, (STRIP, COLS), 0)
    lane8 = lax.broadcasted_iota(jnp.int32, (STRIP, 128), 1)
    sub_c = lax.broadcasted_iota(jnp.int32, (STRIP, 128), 0)
    lane_w = lax.broadcasted_iota(jnp.int32, (STRIP, COLS), 1)
    zero_rows = jnp.zeros((TOP, COLS), jnp.float32)

    for a in range(count):
        if a % fields == 0 and a < nfield:
            loads[a // fields].wait()
        if a == nfield:
            loads[slots].wait()
            loads[slots + 1].wait()
        if a < nfield:
            raw = f_ref[a // fields, a % fields].astype(jnp.float32)
        else:
            raw = (lat_ref if a == nfield else lon_ref)[...]
        X[a, pl.ds(TOP, height), pl.ds(0, breadth)] = raw
        tail = X[a, pl.ds(TOP, height), pl.ds(384, 128)]
        X[a, pl.ds(TOP, height), pl.ds(384, 128)] = jnp.where(lane < breadth - 384, tail, jnp.float32(0.0))
        X[a, pl.ds(0, TOP), :] = zero_rows
        X[a, pl.ds(TOP + height, rows - TOP - height), :] = zero_rows

    @pl.when(me_lat == nlat - 1)
    def _():
        last = TOP + height - 8
        cn[pl.ds(last, 8), :] = jnp.where(sub8 == 7, jnp.float32(0.0), cn[pl.ds(last, 8), :])

    pl_acc = jnp.zeros((height, 128), jnp.float32)
    pr_acc = jnp.zeros((height, 128), jnp.float32)
    for a in range(count):
        head = X[a, pl.ds(TOP, height), pl.ds(0, 128)]
        tail = X[a, pl.ds(TOP, height), pl.ds(384, 128)]
        pl_acc = jnp.where(quad == a, pltpu.roll(head, (HALO * a) % 128, 1), pl_acc)
        pr_acc = jnp.where(quad == a, pltpu.roll(tail, (HALO * a - (breadth - 384 - HALO)) % 128, 1), pr_acc)
    pack_l[...] = pl_acc
    pack_r[...] = pr_acc

    coef_lane = HALO * nfield
    width = 2 * HALO
    per_row = 128 // width
    send_lb[...] = pl_acc.astype(jnp.bfloat16)
    send_rb[...] = pr_acc.astype(jnp.bfloat16)
    for src, dst in ((pl_acc, send_lc), (pr_acc, send_rc)):
        for h in range(dst.shape[0] // STRIP):
            packed = jnp.zeros((STRIP, 128), jnp.float32)
            for g in range(per_row):
                i = h * per_row + g
                if i * STRIP >= height:
                    break
                blk = src[i * STRIP : (i + 1) * STRIP]
                packed = jnp.where(lane8 // width == g, pltpu.roll(blk, (width * g - coef_lane) % 128, 1), packed)
            dst[pl.ds(h * STRIP, STRIP), :] = packed

    def strip_pair(a, first, keep_low):
        lo = X[a, pl.ds(first, STRIP), :]
        hi = X[a + 1, pl.ds(first, STRIP), :]
        if keep_low:
            return jnp.where(sub8 < 4, lo, pltpu.roll(hi, 4, 0))
        return jnp.where(sub8 < 4, pltpu.roll(lo, 4, 0), hi)

    for dst_b, dst_c, first, keep_low in (
        (send_tb, send_tc, TOP, True),
        (send_bb, send_bc, TOP + height - STRIP, False),
    ):
        for j in range(dst_b.shape[0]):
            both = [strip_pair(4 * j, first, keep_low), strip_pair(4 * j + 2, first, keep_low)]
            dst_b[j] = jnp.concatenate(both, axis=0).astype(jnp.bfloat16)
        dst_c[...] = strip_pair(nfield, first, keep_low)

    def seam_of(t3, t0):
        lane_x = lax.broadcasted_iota(jnp.int32, t3.shape, 1)
        return jnp.where(lane_x < SPLIT, pltpu.roll(t3, SPLIT, 1), pltpu.roll(t0, SPLIT, 1))

    for a in range(count):
        SX[a] = seam_of(X[a, :, pl.ds(384, 128)], X[a, :, pl.ds(0, 128)])

    def derive(first, size):
        ca[pl.ds(first, size), :] = cn[pl.ds(first - 1, size), :]
        cw[pl.ds(first, size), :] = pltpu.roll(ce[pl.ds(first, size), :], 1, 1)
        cd[pl.ds(first, size), :] = 2.0 - (
            cn[pl.ds(first, size), :] + ca[pl.ds(first, size), :] + ce[pl.ds(first, size), :] + cw[pl.ds(first, size), :]
        )

    derive(8, rows - 16)
    acc[...] = jnp.zeros_like(acc)
    src_tiles[:, :, 0] = jnp.zeros((2, steps, STRIP, COLS), jnp.float32)
    seam_src[:, :, 0] = jnp.zeros((2, steps, STRIP, 128), jnp.float32)
    lane_s8 = lax.broadcasted_iota(jnp.int32, (STRIP, 128), 1)
    sub_s8 = lax.broadcasted_iota(jnp.int32, (STRIP, 128), 0)
    keep = jnp.logical_not((lane_w < HALO) | ((lane_w >= breadth - HALO) & (lane_w < breadth)))

    def slot_places(s, seam):
        slot = member * slots + s
        act = jnp.where(s < pc_ref[member], jnp.float32(1.0), jnp.float32(0.0))
        row_first = me_lat * height
        col_first = me_lon * breadth
        places = []
        for comp in range(2):
            cell = sc_ref[pl_ref[comp, slot]]
            r = lax.div(cell, nlon_cells)
            c = cell - r * nlon_cells
            rb = r - row_first + TOP
            d = c - col_first
            d = jnp.where(d < 0, d + nlon_cells, d)
            near = d < breadth + HALO
            wrap = d >= nlon_cells - HALO
            cb = jnp.where(near, d, d - nlon_cells + COLS)
            valid = (rb >= TOP - HALO) & (rb < TOP + height + HALO) & (near | wrap)
            row8 = lax.rem(jnp.maximum(rb, 0), 8)
            if seam:
                in_seam = (cb >= 384 + 128 - SPLIT) | (cb < 128 - SPLIT)
                valid = valid & in_seam
                lane_at = jnp.where(cb >= 384 + 128 - SPLIT, cb - 384 - (128 - SPLIT), cb + SPLIT)
                hit = (sub_s8 == row8) & (lane_s8 == lane_at)
                tiles = seam_src
            else:
                hit = (sub8 == row8) & (lane_w == cb)
                tiles = src_tiles
            for t in range(steps):
                amp = wav_ref[t] if comp == 0 else res_ref[steps - 1 - t, slot]
                tiles[comp, t, 1] = jnp.where(hit, amp, jnp.float32(0.0))
            places.append((rb, valid))
        return act, places

    def run_blocks(s, t, block_list, act, places, seam):
        if seam:
            bufs = [(SX.at[s * fields + comp], SX.at[s * fields + 2 + comp], swork.at[s, comp]) for comp in range(2)]
            coefs = (sd, SX.at[nfield], sa, SX.at[nfield + 1], sw)
            span, tiles = 128, seam_src
        else:
            bufs = [(X.at[s * fields + comp], X.at[s * fields + 2 + comp], work.at[s, comp]) for comp in range(2)]
            coefs = (cd, cn, ca, ce, cw)
            span, tiles = COLS, src_tiles
        ei, ci, ni = t % 3, (t + 1) % 3, (t + 2) % 3
        for k in block_list:
            r0 = 8 * k
            dd, nn, aa, ee, ww = (ref[pl.ds(r0, 8), :] for ref in coefs)
            outs = []
            for comp in range(2):
                rb, valid = places[comp]
                pick = (valid & (rb >= r0) & (rb < r0 + 8)).astype(jnp.int32)
                cur_ref, ear_ref, nxt_ref = bufs[comp][ci], bufs[comp][ei], bufs[comp][ni]
                cur = cur_ref[pl.ds(r0, 8), :]
                above = cur_ref[pl.ds(r0 - 1, 8), :]
                below = cur_ref[pl.ds(r0 + 1, 8), :]
                ear = ear_ref[pl.ds(r0, 8), :]
                west = pltpu.roll(cur, 1, 1)
                east = pltpu.roll(cur, span - 1, 1)
                nxt = dd * cur + nn * below + aa * above + ee * east + ww * west - ear
                nxt = nxt + tiles[comp, t, pick]
                nxt_ref[pl.ds(r0, 8), :] = nxt
                outs.append(nxt)
            if 2 <= k < blocks - 2:
                prod = (outs[0] * act) * outs[1]
                out_rows = pl.ds(r0 - TOP, 8)
                if seam:
                    back = pltpu.roll(prod, 128 - SPLIT, 1)
                    acc[out_rows, pl.ds(0, 128)] += jnp.where(lane_s8 < HALO, back, jnp.float32(0.0))
                    east_edge = (lane_s8 >= breadth - 384 - HALO) & (lane_s8 < breadth - 384)
                    acc[out_rows, pl.ds(384, 128)] += jnp.where(east_edge, back, jnp.float32(0.0))
                else:
                    acc[out_rows, :] += jnp.where(keep, prod, jnp.float32(0.0))

    def phase(ranges, seam=False):
        def body(s, carry):
            act, places = slot_places(s, seam)
            for t in range(steps):
                run_blocks(s, t, ranges(t), act, places, seam)
            return carry

        lax.fori_loop(0, slots, body, 0)

    inner = lambda t: list(range(3 + t, blocks - 3 - t))
    phase(inner)

    pl.semaphore_wait(barrier, 3 + 3 * has_up.astype(jnp.int32) + 3 * has_down.astype(jnp.int32))

    last8 = pl.ds(height - STRIP, STRIP)
    first8 = pl.ds(0, STRIP)
    copies = [
        (send_rb, rlb, me_lat, right, None),
        (send_rc, rlc, me_lat, right, None),
        (send_lb, rrb, me_lat, left, None),
        (send_lc, rrc, me_lat, left, None),
        (send_tb, rbb, up, me_lon, "up"),
        (send_tc, rbc, up, me_lon, "up"),
        (send_bb, rab, down, me_lon, "down"),
        (send_bc, rac, down, me_lon, "down"),
        (pack_r.at[last8], rc.at[TL], down, right, "down"),
        (pack_l.at[last8], rc.at[TR], down, left, "down"),
        (pack_r.at[first8], rc.at[BL], up, right, "up"),
        (pack_l.at[first8], rc.at[BR], up, left, "up"),
    ]

    def descriptor(i):
        src, dst, lat_to, lon_to, _ = copies[i]
        return pltpu.make_async_remote_copy(
            src, dst, send_sem.at[i], recv_sem.at[i], device_id={"lat": lat_to, "lon": lon_to}, device_id_type=MESH
        )

    def when(cond, fn):
        if cond is None:
            fn()
        else:
            pl.when(has_up if cond == "up" else has_down)(fn)

    def finish(i):
        cond = copies[i][4]
        when(cond, lambda: descriptor(i).wait_send())
        mirror = {None: None, "up": "down", "down": "up"}[cond]
        when(mirror, lambda: descriptor(i).wait_recv())

    for i, copy in enumerate(copies):
        when(copy[4], lambda i=i: descriptor(i).start())

    for i in range(len(copies)):
        finish(i)

    @pl.when(jnp.logical_not(has_up))
    def _():
        rab[...] = jnp.zeros_like(rab)
        rac[...] = jnp.zeros_like(rac)
        rc[TL] = jnp.zeros((STRIP, 128), jnp.float32)
        rc[TR] = jnp.zeros((STRIP, 128), jnp.float32)

    @pl.when(jnp.logical_not(has_down))
    def _():
        rbb[...] = jnp.zeros_like(rbb)
        rbc[...] = jnp.zeros_like(rbc)
        rc[BL] = jnp.zeros((STRIP, 128), jnp.float32)
        rc[BR] = jnp.zeros((STRIP, 128), jnp.float32)

    east_gap = (lane >= breadth - 384) & (lane < breadth - 384 + HALO)
    west_gap = lane >= 128 - HALO
    unpacked = []
    for src_b, src_c in ((rlb, rlc), (rrb, rrc)):
        fields_part = src_b[...].astype(jnp.float32)
        parts = []
        for i in range(height // STRIP):
            h, g = divmod(i, per_row)
            blk_c = pltpu.roll(src_c[pl.ds(h * STRIP, STRIP), :], (coef_lane - width * g) % 128, 1)
            blk_f = fields_part[i * STRIP : (i + 1) * STRIP]
            parts.append(jnp.where(lane8 < coef_lane, blk_f, blk_c))
        unpacked.append(jnp.concatenate(parts, axis=0))
    from_l, from_r = unpacked
    east_s = (lane >= breadth - 384 - (128 - SPLIT)) & (lane < breadth - 384 - (128 - SPLIT) + HALO)
    west_s = (lane >= SPLIT - HALO) & (lane < SPLIT)
    for a in range(count):
        east_shift = (breadth - 384 - (128 - SPLIT) - HALO * a) % 128
        west_shift = (SPLIT - HALO - HALO * a) % 128
        mid = SX[a, pl.ds(TOP, height), :]
        mid = jnp.where(east_s, pltpu.roll(from_r, east_shift, 1), mid)
        mid = jnp.where(west_s, pltpu.roll(from_l, west_shift, 1), mid)
        SX[a, pl.ds(TOP, height), :] = mid

    east_c = (lane8 >= breadth - 384) & (lane8 < breadth - 384 + HALO)
    west_c = lane8 >= 128 - HALO
    for src_b, src_c, first, low_half, (c_east, c_west) in (
        (rab, rac, TOP - STRIP, False, (TR, TL)),
        (rbb, rbc, TOP + height, True, (BR, BL)),
    ):
        for a in range(count):
            b = a // 2
            if a < nfield:
                both = src_b[b // 2].astype(jnp.float32)
                blk = both[STRIP * (b % 2) : STRIP * (b % 2 + 1)]
            else:
                blk = src_c[...]
            even = a % 2 == 0
            if low_half:
                blk = blk if even else pltpu.roll(blk, 4, 0)
                blk = jnp.where(sub8 < 4, blk, jnp.float32(0.0))
                band = sub_c < 4
            else:
                blk = pltpu.roll(blk, 4, 0) if even else blk
                blk = jnp.where(sub8 >= 4, blk, jnp.float32(0.0))
                band = sub_c >= 4
            X[a, pl.ds(first, STRIP), :] = blk
            east_shift = (breadth - 384 - HALO * a) % 128
            west_shift = (128 - HALO - HALO * a) % 128
            tail = X[a, pl.ds(first, STRIP), pl.ds(384, 128)]
            tail = jnp.where(band & east_c, pltpu.roll(rc[c_east], east_shift, 1), tail)
            tail = jnp.where(band & west_c, pltpu.roll(rc[c_west], west_shift, 1), tail)
            X[a, pl.ds(first, STRIP), pl.ds(384, 128)] = tail
            SX[a, pl.ds(first, STRIP), :] = seam_of(tail, blk[:, 0:128])

    derive(8, 24)
    derive(rows - 32, 24)
    sn = SX.at[nfield]
    se = SX.at[nfield + 1]
    sa[pl.ds(8, rows - 16), :] = sn[pl.ds(7, rows - 16), :]
    sw[pl.ds(8, rows - 16), :] = pltpu.roll(se[pl.ds(8, rows - 16), :], 1, 1)
    sd[pl.ds(8, rows - 16), :] = 2.0 - (
        sn[pl.ds(8, rows - 16), :] + sa[pl.ds(8, rows - 16), :] + se[pl.ds(8, rows - 16), :] + sw[pl.ds(8, rows - 16), :]
    )

    def outer(t):
        if t < steps - 1:
            return list(range(1, 3 + t)) + list(range(blocks - 3 - t, blocks - 1))
        return list(range(2, 3 + t)) + list(range(blocks - 3 - t, blocks - 2))

    phase(outer)

    def full(t):
        return list(range(1, blocks - 1)) if t < steps - 1 else list(range(2, blocks - 2))

    phase(full, seam=True)

    to_partner = pltpu.make_async_remote_copy(
        acc, pacc, send_sem.at[len(copies)], recv_sem.at[len(copies)], device_id={"pair": partner}, device_id_type=MESH
    )
    to_partner.start()
    to_partner.wait()
    o_ref[...] = (acc[...] + pacc[...])[:, 0:breadth]


def fused(wave_states, lat_faces, lon_faces, scalars, nlon_cells):
    slots, fields, height, breadth = wave_states.shape
    nfield = slots * fields
    count = nfield + 2
    rows = height + 2 * TOP
    smem = pl.BlockSpec(memory_space=pltpu.SMEM)
    vmem = pl.BlockSpec(memory_space=pltpu.VMEM)
    per_row = 128 // (2 * HALO)
    coef_rows = STRIP * ((height // STRIP + per_row - 1) // per_row)
    packed_b = pltpu.VMEM((height, 128), jnp.bfloat16)
    packed_c = pltpu.VMEM((coef_rows, 128), jnp.float32)
    strip_b16 = pltpu.VMEM((nfield // 4, 2 * STRIP, COLS), jnp.bfloat16)
    strip_c = pltpu.VMEM((STRIP, COLS), jnp.float32)
    plane = pltpu.VMEM((rows, COLS), jnp.float32)
    return pl.pallas_call(
        functools.partial(fused_kernel, nlon_cells),
        out_shape=jax.ShapeDtypeStruct((height, breadth), jnp.float32),
        in_specs=[smem] * 5 + [pl.BlockSpec(memory_space=pl.ANY)] * 3,
        out_specs=vmem,
        scratch_shapes=[
            pltpu.VMEM(wave_states.shape, wave_states.dtype),
            pltpu.VMEM(lat_faces.shape, jnp.float32),
            pltpu.VMEM(lon_faces.shape, jnp.float32),
            pltpu.SemaphoreType.DMA((slots + 2,)),
            pltpu.VMEM((2, 4, 2, STRIP, COLS), jnp.float32),
            pltpu.VMEM((count, rows, COLS), jnp.float32),
            pltpu.VMEM((slots, 2, rows, COLS), jnp.float32),
            plane,
            plane,
            plane,
            pltpu.VMEM((height, COLS), jnp.float32),
            pltpu.VMEM((height, COLS), jnp.float32),
            pltpu.VMEM((count, rows, 128), jnp.float32),
            pltpu.VMEM((slots, 2, rows, 128), jnp.float32),
            pltpu.VMEM((rows, 128), jnp.float32),
            pltpu.VMEM((rows, 128), jnp.float32),
            pltpu.VMEM((rows, 128), jnp.float32),
            pltpu.VMEM((2, 4, 2, STRIP, 128), jnp.float32),
            pltpu.VMEM((height, 128), jnp.float32),
            pltpu.VMEM((height, 128), jnp.float32),
        ]
        + [packed_b, packed_b, packed_c, packed_c, strip_b16, strip_b16, strip_c, strip_c] * 2
        + [
            pltpu.VMEM((4, STRIP, 128), jnp.float32),
            pltpu.SemaphoreType.DMA((13,)),
            pltpu.SemaphoreType.DMA((13,)),
        ],
        compiler_params=pltpu.CompilerParams(collective_id=0, has_side_effects=True, vmem_limit_bytes=60 * 1024 * 1024),
    )(*scalars, wave_states, lat_faces, lon_faces)


def body(
    wave_states,
    pair_list,
    pair_counts,
    residuals,
    station_cell,
    source_wavelet,
    lat_faces,
    lon_faces,
):
    height, breadth = lat_faces.shape
    nlon_cells = breadth * lax.axis_size("lon")
    scalars = (pair_list.T, pair_counts, residuals.T, station_cell, source_wavelet)
    return fused(wave_states, lat_faces, lon_faces, scalars, nlon_cells)


def solution(mesh):
    in_specs = (
        P("pair", None, "lat", "lon"),
        P(),
        P(),
        P(),
        P(),
        P(),
        P("lat", "lon"),
        P("lat", "lon"),
    )
    out_specs = P("lat", "lon")
    return jax.shard_map(body, mesh=mesh, in_specs=in_specs, out_specs=out_specs, check_vma=False)
```

```python
import functools

import jax
import jax.numpy as jnp
from jax import lax
from jax.experimental import pallas as pl
from jax.experimental.pallas import tpu as pltpu
from jax.sharding import PartitionSpec as P

HALO = 4
TOP = 16
COLS = 512
STRIP = 8
MESH = pl.DeviceIdType.MESH
TL, TR, BL, BR = 0, 1, 2, 3
MID_FIRST = 32


def fused_kernel(
    nlon_cells,
    pl_ref, pc_ref, res_ref, sc_ref, wav_ref,
    f_hbm, lat_hbm, lon_hbm,
    o_ref,
    f_ref, lat_ref, lon_ref, in_sem, src_tiles,
    X, work, ca, cw, cd, acc, pacc, acc_mid, pacc_mid,
    pack_l, pack_r,
    send_lb, send_rb, send_lc, send_rc, send_tb, send_bb, send_tc, send_bc,
    rlb, rrb, rlc, rrc, rab, rbb, rac, rbc, rc,
    send_sem, recv_sem,
):
    slots, fields, height, breadth = f_ref.shape
    nfield = slots * fields
    count = nfield + 2
    rows = X.shape[1]
    blocks = rows // 8
    steps = wav_ref.shape[0]
    nlon = lax.axis_size("lon")
    nlat = lax.axis_size("lat")
    me_lat = lax.axis_index("lat")
    me_lon = lax.axis_index("lon")
    member = lax.axis_index("pair")
    partner = 1 - member
    right = lax.rem(me_lon + 1, nlon)
    left = lax.rem(me_lon + nlon - 1, nlon)
    has_up = me_lat > 0
    has_down = me_lat < nlat - 1
    up = jnp.maximum(me_lat - 1, 0)
    down = jnp.minimum(me_lat + 1, nlat - 1)
    cn = X.at[nfield]
    ce = X.at[nfield + 1]

    barrier = pltpu.get_barrier_semaphore()
    pl.semaphore_signal(barrier, 1, device_id={"pair": partner}, device_id_type=MESH)
    for lon_to in (left, right):
        pl.semaphore_signal(barrier, 1, device_id={"lon": lon_to}, device_id_type=MESH)

    @pl.when(has_up)
    def _():
        for lon_to in (me_lon, left, right):
            pl.semaphore_signal(barrier, 1, device_id={"lat": up, "lon": lon_to}, device_id_type=MESH)

    @pl.when(has_down)
    def _():
        for lon_to in (me_lon, left, right):
            pl.semaphore_signal(barrier, 1, device_id={"lat": down, "lon": lon_to}, device_id_type=MESH)

    loads = [pltpu.make_async_copy(f_hbm.at[i], f_ref.at[i], in_sem.at[i]) for i in range(slots)]
    loads.append(pltpu.make_async_copy(lat_hbm, lat_ref, in_sem.at[slots]))
    loads.append(pltpu.make_async_copy(lon_hbm, lon_ref, in_sem.at[slots + 1]))
    for copy in loads:
        copy.start()

    lane = lax.broadcasted_iota(jnp.int32, (height, 128), 1)
    quad = lane // HALO
    sub8 = lax.broadcasted_iota(jnp.int32, (STRIP, COLS), 0)
    lane8 = lax.broadcasted_iota(jnp.int32, (STRIP, 128), 1)
    sub_c = lax.broadcasted_iota(jnp.int32, (STRIP, 128), 0)
    lane_w = lax.broadcasted_iota(jnp.int32, (STRIP, COLS), 1)
    zero_rows = jnp.zeros((TOP, COLS), jnp.float32)

    for a in range(count):
        if a % fields == 0 and a < nfield:
            loads[a // fields].wait()
        if a == nfield:
            loads[slots].wait()
            loads[slots + 1].wait()
        if a < nfield:
            raw = f_ref[a // fields, a % fields].astype(jnp.float32)
        else:
            raw = (lat_ref if a == nfield else lon_ref)[...]
        X[a, pl.ds(TOP, height), pl.ds(0, breadth)] = raw
        tail = X[a, pl.ds(TOP, height), pl.ds(384, 128)]
        X[a, pl.ds(TOP, height), pl.ds(384, 128)] = jnp.where(lane < breadth - 384, tail, jnp.float32(0.0))
        X[a, pl.ds(0, TOP), :] = zero_rows
        X[a, pl.ds(TOP + height, rows - TOP - height), :] = zero_rows

    @pl.when(me_lat == nlat - 1)
    def _():
        last = TOP + height - 8
        cn[pl.ds(last, 8), :] = jnp.where(sub8 == 7, jnp.float32(0.0), cn[pl.ds(last, 8), :])

    pl_acc = jnp.zeros((height, 128), jnp.float32)
    pr_acc = jnp.zeros((height, 128), jnp.float32)
    for a in range(count):
        head = X[a, pl.ds(TOP, height), pl.ds(0, 128)]
        tail = X[a, pl.ds(TOP, height), pl.ds(384, 128)]
        pl_acc = jnp.where(quad == a, pltpu.roll(head, (HALO * a) % 128, 1), pl_acc)
        pr_acc = jnp.where(quad == a, pltpu.roll(tail, (HALO * a - (breadth - 384 - HALO)) % 128, 1), pr_acc)
    pack_l[...] = pl_acc
    pack_r[...] = pr_acc

    coef_lane = HALO * nfield
    width = 2 * HALO
    per_row = 128 // width
    send_lb[...] = pl_acc.astype(jnp.bfloat16)
    send_rb[...] = pr_acc.astype(jnp.bfloat16)
    for src, dst in ((pl_acc, send_lc), (pr_acc, send_rc)):
        for h in range(dst.shape[0] // STRIP):
            packed = jnp.zeros((STRIP, 128), jnp.float32)
            for g in range(per_row):
                i = h * per_row + g
                if i * STRIP >= height:
                    break
                blk = src[i * STRIP : (i + 1) * STRIP]
                packed = jnp.where(lane8 // width == g, pltpu.roll(blk, (width * g - coef_lane) % 128, 1), packed)
            dst[pl.ds(h * STRIP, STRIP), :] = packed

    def strip_pair(a, first, keep_low):
        lo = X[a, pl.ds(first, STRIP), :]
        hi = X[a + 1, pl.ds(first, STRIP), :]
        if keep_low:
            return jnp.where(sub8 < 4, lo, pltpu.roll(hi, 4, 0))
        return jnp.where(sub8 < 4, pltpu.roll(lo, 4, 0), hi)

    for dst_b, dst_c, first, keep_low in (
        (send_tb, send_tc, TOP, True),
        (send_bb, send_bc, TOP + height - STRIP, False),
    ):
        for j in range(dst_b.shape[0]):
            both = [strip_pair(4 * j, first, keep_low), strip_pair(4 * j + 2, first, keep_low)]
            dst_b[j] = jnp.concatenate(both, axis=0).astype(jnp.bfloat16)
        dst_c[...] = strip_pair(nfield, first, keep_low)

    pl.semaphore_wait(barrier, 3 + 3 * has_up.astype(jnp.int32) + 3 * has_down.astype(jnp.int32))

    last8 = pl.ds(height - STRIP, STRIP)
    first8 = pl.ds(0, STRIP)
    copies = [
        (send_rb, rlb, me_lat, right, None),
        (send_rc, rlc, me_lat, right, None),
        (send_lb, rrb, me_lat, left, None),
        (send_lc, rrc, me_lat, left, None),
        (send_tb, rbb, up, me_lon, "up"),
        (send_tc, rbc, up, me_lon, "up"),
        (send_bb, rab, down, me_lon, "down"),
        (send_bc, rac, down, me_lon, "down"),
        (pack_r.at[last8], rc.at[TL], down, right, "down"),
        (pack_l.at[last8], rc.at[TR], down, left, "down"),
        (pack_r.at[first8], rc.at[BL], up, right, "up"),
        (pack_l.at[first8], rc.at[BR], up, left, "up"),
    ]

    def descriptor(i):
        src, dst, lat_to, lon_to, _ = copies[i]
        return pltpu.make_async_remote_copy(
            src, dst, send_sem.at[i], recv_sem.at[i], device_id={"lat": lat_to, "lon": lon_to}, device_id_type=MESH
        )

    def when(cond, fn):
        if cond is None:
            fn()
        else:
            pl.when(has_up if cond == "up" else has_down)(fn)

    def finish(i):
        cond = copies[i][4]
        when(cond, lambda: descriptor(i).wait_send())
        mirror = {None: None, "up": "down", "down": "up"}[cond]
        when(mirror, lambda: descriptor(i).wait_recv())

    for i, copy in enumerate(copies):
        when(copy[4], lambda i=i: descriptor(i).start())

    for i in range(4):
        finish(i)
    east_gap = (lane >= breadth - 384) & (lane < breadth - 384 + HALO)
    west_gap = lane >= 128 - HALO
    unpacked = []
    for src_b, src_c in ((rlb, rlc), (rrb, rrc)):
        fields_part = src_b[...].astype(jnp.float32)
        parts = []
        for i in range(height // STRIP):
            h, g = divmod(i, per_row)
            blk_c = pltpu.roll(src_c[pl.ds(h * STRIP, STRIP), :], (coef_lane - width * g) % 128, 1)
            blk_f = fields_part[i * STRIP : (i + 1) * STRIP]
            parts.append(jnp.where(lane8 < coef_lane, blk_f, blk_c))
        unpacked.append(jnp.concatenate(parts, axis=0))
    from_l, from_r = unpacked
    for a in range(count):
        east_shift = (breadth - 384 - HALO * a) % 128
        west_shift = (128 - HALO - HALO * a) % 128
        tail = X[a, pl.ds(TOP, height), pl.ds(384, 128)]
        tail = jnp.where(east_gap, pltpu.roll(from_r, east_shift, 1), tail)
        tail = jnp.where(west_gap, pltpu.roll(from_l, west_shift, 1), tail)
        X[a, pl.ds(TOP, height), pl.ds(384, 128)] = tail

    def derive(first, size):
        ca[pl.ds(first, size), :] = cn[pl.ds(first - 1, size), :]
        cw[pl.ds(first, size), :] = pltpu.roll(ce[pl.ds(first, size), :], 1, 1)
        cd[pl.ds(first, size), :] = 2.0 - (
            cn[pl.ds(first, size), :] + ca[pl.ds(first, size), :] + ce[pl.ds(first, size), :] + cw[pl.ds(first, size), :]
        )

    derive(8, rows - 16)
    acc[...] = jnp.zeros_like(acc)
    acc_mid[...] = jnp.zeros_like(acc_mid)
    src_tiles[:, :, 0] = jnp.zeros((2, steps, STRIP, COLS), jnp.float32)

    def slot_places(s):
        slot = member * slots + s
        act = jnp.where(s < pc_ref[member], jnp.float32(1.0), jnp.float32(0.0))
        row_first = me_lat * height
        col_first = me_lon * breadth
        places = []
        for comp in range(2):
            cell = sc_ref[pl_ref[comp, slot]]
            r = lax.div(cell, nlon_cells)
            c = cell - r * nlon_cells
            rb = r - row_first + TOP
            d = c - col_first
            d = jnp.where(d < 0, d + nlon_cells, d)
            near = d < breadth + HALO
            wrap = d >= nlon_cells - HALO
            cb = jnp.where(near, d, d - nlon_cells + COLS)
            valid = (rb >= TOP - HALO) & (rb < TOP + height + HALO) & (near | wrap)
            hit = (sub8 == lax.rem(jnp.maximum(rb, 0), 8)) & (lane_w == cb)
            for t in range(steps):
                amp = wav_ref[t] if comp == 0 else res_ref[steps - 1 - t, slot]
                src_tiles[comp, t, 1] = jnp.where(hit, amp, jnp.float32(0.0))
            places.append((rb, valid))
        return act, places

    def run_blocks(s, t, block_list, act, places):
        bufs = [(X.at[s * fields + comp], X.at[s * fields + 2 + comp], work.at[s, comp]) for comp in range(2)]
        ei, ci, ni = t % 3, (t + 1) % 3, (t + 2) % 3
        for k in block_list:
            r0 = 8 * k
            dd = cd[pl.ds(r0, 8), :]
            nn = cn[pl.ds(r0, 8), :]
            aa = ca[pl.ds(r0, 8), :]
            ee = ce[pl.ds(r0, 8), :]
            ww = cw[pl.ds(r0, 8), :]
            outs = []
            for comp in range(2):
                rb, valid = places[comp]
                pick = (valid & (rb >= r0) & (rb < r0 + 8)).astype(jnp.int32)
                cur_ref, ear_ref, nxt_ref = bufs[comp][ci], bufs[comp][ei], bufs[comp][ni]
                cur = cur_ref[pl.ds(r0, 8), :]
                above = cur_ref[pl.ds(r0 - 1, 8), :]
                below = cur_ref[pl.ds(r0 + 1, 8), :]
                ear = ear_ref[pl.ds(r0, 8), :]
                west = pltpu.roll(cur, 1, 1)
                east = pltpu.roll(cur, COLS - 1, 1)
                nxt = dd * cur + nn * below + aa * above + ee * east + ww * west - ear
                nxt = nxt + src_tiles[comp, t, pick]
                nxt_ref[pl.ds(r0, 8), :] = nxt
                outs.append(nxt)
            if 2 <= k < blocks - 2:
                row = r0 - TOP
                if MID_FIRST <= row < MID_FIRST + acc_mid.shape[0]:
                    dst, row = acc_mid, row - MID_FIRST
                else:
                    dst, row = acc, (row if row < MID_FIRST else row - acc_mid.shape[0])
                dst[pl.ds(row, 8), :] += (outs[0] * act) * outs[1]

    def phase(ranges):
        def body(s, carry):
            act, places = slot_places(s)
            for t in range(steps):
                run_blocks(s, t, ranges(t), act, places)
            return carry

        lax.fori_loop(0, slots, body, 0)

    inner = lambda t: list(range(3 + t, blocks - 3 - t))
    phase(inner)

    mid_out = pltpu.make_async_remote_copy(
        acc_mid, pacc_mid, send_sem.at[len(copies) + 1], recv_sem.at[len(copies) + 1],
        device_id={"pair": partner}, device_id_type=MESH,
    )
    mid_out.start()

    for i in range(4, len(copies)):
        finish(i)

    @pl.when(jnp.logical_not(has_up))
    def _():
        rab[...] = jnp.zeros_like(rab)
        rac[...] = jnp.zeros_like(rac)
        rc[TL] = jnp.zeros((STRIP, 128), jnp.float32)
        rc[TR] = jnp.zeros((STRIP, 128), jnp.float32)

    @pl.when(jnp.logical_not(has_down))
    def _():
        rbb[...] = jnp.zeros_like(rbb)
        rbc[...] = jnp.zeros_like(rbc)
        rc[BL] = jnp.zeros((STRIP, 128), jnp.float32)
        rc[BR] = jnp.zeros((STRIP, 128), jnp.float32)

    east_c = (lane8 >= breadth - 384) & (lane8 < breadth - 384 + HALO)
    west_c = lane8 >= 128 - HALO
    for src_b, src_c, first, low_half, (c_east, c_west) in (
        (rab, rac, TOP - STRIP, False, (TR, TL)),
        (rbb, rbc, TOP + height, True, (BR, BL)),
    ):
        for a in range(count):
            b = a // 2
            if a < nfield:
                both = src_b[b // 2].astype(jnp.float32)
                blk = both[STRIP * (b % 2) : STRIP * (b % 2 + 1)]
            else:
                blk = src_c[...]
            even = a % 2 == 0
            if low_half:
                blk = blk if even else pltpu.roll(blk, 4, 0)
                blk = jnp.where(sub8 < 4, blk, jnp.float32(0.0))
                band = sub_c < 4
            else:
                blk = pltpu.roll(blk, 4, 0) if even else blk
                blk = jnp.where(sub8 >= 4, blk, jnp.float32(0.0))
                band = sub_c >= 4
            X[a, pl.ds(first, STRIP), :] = blk
            east_shift = (breadth - 384 - HALO * a) % 128
            west_shift = (128 - HALO - HALO * a) % 128
            tail = X[a, pl.ds(first, STRIP), pl.ds(384, 128)]
            tail = jnp.where(band & east_c, pltpu.roll(rc[c_east], east_shift, 1), tail)
            tail = jnp.where(band & west_c, pltpu.roll(rc[c_west], west_shift, 1), tail)
            X[a, pl.ds(first, STRIP), pl.ds(384, 128)] = tail

    derive(8, 24)
    derive(rows - 32, 24)

    def outer(t):
        if t < steps - 1:
            return list(range(1, 3 + t)) + list(range(blocks - 3 - t, blocks - 1))
        return list(range(2, 3 + t)) + list(range(blocks - 3 - t, blocks - 2))

    phase(outer)

    to_partner = pltpu.make_async_remote_copy(
        acc, pacc, send_sem.at[len(copies)], recv_sem.at[len(copies)], device_id={"pair": partner}, device_id_type=MESH
    )
    to_partner.start()
    to_partner.wait()
    mid_out.wait()
    edge = acc[...] + pacc[...]
    mids = acc_mid.shape[0]
    o_ref[pl.ds(0, MID_FIRST), :] = edge[0:MID_FIRST, 0:breadth]
    o_ref[pl.ds(MID_FIRST, mids), :] = (acc_mid[...] + pacc_mid[...])[:, 0:breadth]
    o_ref[pl.ds(MID_FIRST + mids, height - MID_FIRST - mids), :] = edge[MID_FIRST:, 0:breadth]


def fused(wave_states, lat_faces, lon_faces, scalars, nlon_cells):
    slots, fields, height, breadth = wave_states.shape
    nfield = slots * fields
    count = nfield + 2
    rows = height + 2 * TOP
    smem = pl.BlockSpec(memory_space=pltpu.SMEM)
    vmem = pl.BlockSpec(memory_space=pltpu.VMEM)
    per_row = 128 // (2 * HALO)
    coef_rows = STRIP * ((height // STRIP + per_row - 1) // per_row)
    packed_b = pltpu.VMEM((height, 128), jnp.bfloat16)
    packed_c = pltpu.VMEM((coef_rows, 128), jnp.float32)
    strip_b16 = pltpu.VMEM((nfield // 4, 2 * STRIP, COLS), jnp.bfloat16)
    strip_c = pltpu.VMEM((STRIP, COLS), jnp.float32)
    plane = pltpu.VMEM((rows, COLS), jnp.float32)
    return pl.pallas_call(
        functools.partial(fused_kernel, nlon_cells),
        out_shape=jax.ShapeDtypeStruct((height, breadth), jnp.float32),
        in_specs=[smem] * 5 + [pl.BlockSpec(memory_space=pl.ANY)] * 3,
        out_specs=vmem,
        scratch_shapes=[
            pltpu.VMEM(wave_states.shape, wave_states.dtype),
            pltpu.VMEM(lat_faces.shape, jnp.float32),
            pltpu.VMEM(lon_faces.shape, jnp.float32),
            pltpu.SemaphoreType.DMA((slots + 2,)),
            pltpu.VMEM((2, 4, 2, STRIP, COLS), jnp.float32),
            pltpu.VMEM((count, rows, COLS), jnp.float32),
            pltpu.VMEM((slots, 2, rows, COLS), jnp.float32),
            plane,
            plane,
            plane,
            pltpu.VMEM((2 * MID_FIRST, COLS), jnp.float32),
            pltpu.VMEM((2 * MID_FIRST, COLS), jnp.float32),
            pltpu.VMEM((height - 2 * MID_FIRST, COLS), jnp.float32),
            pltpu.VMEM((height - 2 * MID_FIRST, COLS), jnp.float32),
            pltpu.VMEM((height, 128), jnp.float32),
            pltpu.VMEM((height, 128), jnp.float32),
        ]
        + [packed_b, packed_b, packed_c, packed_c, strip_b16, strip_b16, strip_c, strip_c] * 2
        + [
            pltpu.VMEM((4, STRIP, 128), jnp.float32),
            pltpu.SemaphoreType.DMA((14,)),
            pltpu.SemaphoreType.DMA((14,)),
        ],
        compiler_params=pltpu.CompilerParams(collective_id=0, has_side_effects=True, vmem_limit_bytes=60 * 1024 * 1024),
    )(*scalars, wave_states, lat_faces, lon_faces)


def body(
    wave_states,
    pair_list,
    pair_counts,
    residuals,
    station_cell,
    source_wavelet,
    lat_faces,
    lon_faces,
):
    height, breadth = lat_faces.shape
    nlon_cells = breadth * lax.axis_size("lon")
    scalars = (pair_list.T, pair_counts, residuals.T, station_cell, source_wavelet)
    return fused(wave_states, lat_faces, lon_faces, scalars, nlon_cells)


def solution(mesh):
    in_specs = (
        P("pair", None, "lat", "lon"),
        P(),
        P(),
        P(),
        P(),
        P(),
        P("lat", "lon"),
        P("lat", "lon"),
    )
    out_specs = P("lat", "lon")
    return jax.shard_map(body, mesh=mesh, in_specs=in_specs, out_specs=out_specs, check_vma=False)
```

```python
import functools

import jax
import jax.numpy as jnp
from jax import lax
from jax.experimental import pallas as pl
from jax.experimental.pallas import tpu as pltpu
from jax.sharding import PartitionSpec as P

HALO = 4
TOP = 16
COLS = 512
STRIP = 8
MESH = pl.DeviceIdType.MESH
TL, TR, BL, BR = 0, 1, 2, 3
MID_FIRST = 32


def fused_kernel(
    nlon_cells,
    pl_ref, pc_ref, res_ref, sc_ref, wav_ref,
    f_hbm, lat_hbm, lon_hbm,
    o_ref,
    f_ref, lat_ref, lon_ref, in_sem, src_tiles,
    X, work, ca, cw, cd, acc, pacc, acc_mid, pacc_mid,
    pack_l, pack_r,
    send_lb, send_rb, send_lc, send_rc, send_tb, send_bb, send_tc, send_bc,
    rlb, rrb, rlc, rrc, rab, rbb, rac, rbc, rc,
    send_sem, recv_sem,
):
    slots, fields, height, breadth = f_ref.shape
    nfield = slots * fields
    count = nfield + 2
    rows = X.shape[1]
    blocks = rows // 8
    steps = wav_ref.shape[0]
    nlon = lax.axis_size("lon")
    nlat = lax.axis_size("lat")
    me_lat = lax.axis_index("lat")
    me_lon = lax.axis_index("lon")
    member = lax.axis_index("pair")
    partner = 1 - member
    right = lax.rem(me_lon + 1, nlon)
    left = lax.rem(me_lon + nlon - 1, nlon)
    has_up = me_lat > 0
    has_down = me_lat < nlat - 1
    up = jnp.maximum(me_lat - 1, 0)
    down = jnp.minimum(me_lat + 1, nlat - 1)
    cn = X.at[nfield]
    ce = X.at[nfield + 1]

    barrier = pltpu.get_barrier_semaphore()
    pl.semaphore_signal(barrier, 1, device_id={"pair": partner}, device_id_type=MESH)
    for lon_to in (left, right):
        pl.semaphore_signal(barrier, 1, device_id={"lon": lon_to}, device_id_type=MESH)

    @pl.when(has_up)
    def _():
        for lon_to in (me_lon, left, right):
            pl.semaphore_signal(barrier, 1, device_id={"lat": up, "lon": lon_to}, device_id_type=MESH)

    @pl.when(has_down)
    def _():
        for lon_to in (me_lon, left, right):
            pl.semaphore_signal(barrier, 1, device_id={"lat": down, "lon": lon_to}, device_id_type=MESH)

    loads = [pltpu.make_async_copy(f_hbm.at[i], f_ref.at[i], in_sem.at[i]) for i in range(slots)]
    loads.append(pltpu.make_async_copy(lat_hbm, lat_ref, in_sem.at[slots]))
    loads.append(pltpu.make_async_copy(lon_hbm, lon_ref, in_sem.at[slots + 1]))
    for copy in loads:
        copy.start()

    lane = lax.broadcasted_iota(jnp.int32, (height, 128), 1)
    quad = lane // HALO
    sub8 = lax.broadcasted_iota(jnp.int32, (STRIP, COLS), 0)
    lane8 = lax.broadcasted_iota(jnp.int32, (STRIP, 128), 1)
    sub_c = lax.broadcasted_iota(jnp.int32, (STRIP, 128), 0)
    lane_w = lax.broadcasted_iota(jnp.int32, (STRIP, COLS), 1)
    zero_rows = jnp.zeros((TOP, COLS), jnp.float32)

    for a in range(count):
        if a % fields == 0 and a < nfield:
            loads[a // fields].wait()
        if a == nfield:
            loads[slots].wait()
            loads[slots + 1].wait()
        if a < nfield:
            raw = f_ref[a // fields, a % fields].astype(jnp.float32)
        else:
            raw = (lat_ref if a == nfield else lon_ref)[...]
        X[a, pl.ds(TOP, height), pl.ds(0, breadth)] = raw
        tail = X[a, pl.ds(TOP, height), pl.ds(384, 128)]
        X[a, pl.ds(TOP, height), pl.ds(384, 128)] = jnp.where(lane < breadth - 384, tail, jnp.float32(0.0))
        X[a, pl.ds(0, TOP), :] = zero_rows
        X[a, pl.ds(TOP + height, rows - TOP - height), :] = zero_rows

    @pl.when(me_lat == nlat - 1)
    def _():
        last = TOP + height - 8
        cn[pl.ds(last, 8), :] = jnp.where(sub8 == 7, jnp.float32(0.0), cn[pl.ds(last, 8), :])

    pl_acc = jnp.zeros((height, 128), jnp.float32)
    pr_acc = jnp.zeros((height, 128), jnp.float32)
    for a in range(count):
        head = X[a, pl.ds(TOP, height), pl.ds(0, 128)]
        tail = X[a, pl.ds(TOP, height), pl.ds(384, 128)]
        pl_acc = jnp.where(quad == a, pltpu.roll(head, (HALO * a) % 128, 1), pl_acc)
        pr_acc = jnp.where(quad == a, pltpu.roll(tail, (HALO * a - (breadth - 384 - HALO)) % 128, 1), pr_acc)
    pack_l[...] = pl_acc
    pack_r[...] = pr_acc

    coef_lane = HALO * nfield
    width = 2 * HALO
    per_row = 128 // width
    send_lb[...] = pl_acc.astype(jnp.bfloat16)
    send_rb[...] = pr_acc.astype(jnp.bfloat16)
    for src, dst in ((pl_acc, send_lc), (pr_acc, send_rc)):
        for h in range(dst.shape[0] // STRIP):
            packed = jnp.zeros((STRIP, 128), jnp.float32)
            for g in range(per_row):
                i = h * per_row + g
                if i * STRIP >= height:
                    break
                blk = src[i * STRIP : (i + 1) * STRIP]
                packed = jnp.where(lane8 // width == g, pltpu.roll(blk, (width * g - coef_lane) % 128, 1), packed)
            dst[pl.ds(h * STRIP, STRIP), :] = packed

    def strip_pair(a, first, keep_low):
        lo = X[a, pl.ds(first, STRIP), :]
        hi = X[a + 1, pl.ds(first, STRIP), :]
        if keep_low:
            return jnp.where(sub8 < 4, lo, pltpu.roll(hi, 4, 0))
        return jnp.where(sub8 < 4, pltpu.roll(lo, 4, 0), hi)

    for dst_b, dst_c, first, keep_low in (
        (send_tb, send_tc, TOP, True),
        (send_bb, send_bc, TOP + height - STRIP, False),
    ):
        for j in range(dst_b.shape[0]):
            both = [strip_pair(4 * j, first, keep_low), strip_pair(4 * j + 2, first, keep_low)]
            dst_b[j] = jnp.concatenate(both, axis=0).astype(jnp.bfloat16)
        dst_c[...] = strip_pair(nfield, first, keep_low)

    pl.semaphore_wait(barrier, 3 + 3 * has_up.astype(jnp.int32) + 3 * has_down.astype(jnp.int32))

    last8 = pl.ds(height - STRIP, STRIP)
    first8 = pl.ds(0, STRIP)
    copies = [
        (send_rb, rlb, me_lat, right, None),
        (send_rc, rlc, me_lat, right, None),
        (send_lb, rrb, me_lat, left, None),
        (send_lc, rrc, me_lat, left, None),
        (send_tb, rbb, up, me_lon, "up"),
        (send_tc, rbc, up, me_lon, "up"),
        (send_bb, rab, down, me_lon, "down"),
        (send_bc, rac, down, me_lon, "down"),
        (pack_r.at[last8], rc.at[TL], down, right, "down"),
        (pack_l.at[last8], rc.at[TR], down, left, "down"),
        (pack_r.at[first8], rc.at[BL], up, right, "up"),
        (pack_l.at[first8], rc.at[BR], up, left, "up"),
    ]

    def descriptor(i):
        src, dst, lat_to, lon_to, _ = copies[i]
        return pltpu.make_async_remote_copy(
            src, dst, send_sem.at[i], recv_sem.at[i], device_id={"lat": lat_to, "lon": lon_to}, device_id_type=MESH
        )

    def when(cond, fn):
        if cond is None:
            fn()
        else:
            pl.when(has_up if cond == "up" else has_down)(fn)

    def finish(i):
        cond = copies[i][4]
        when(cond, lambda: descriptor(i).wait_send())
        mirror = {None: None, "up": "down", "down": "up"}[cond]
        when(mirror, lambda: descriptor(i).wait_recv())

    for i, copy in enumerate(copies):
        when(copy[4], lambda i=i: descriptor(i).start())

    for i in range(4):
        finish(i)
    east_gap = (lane >= breadth - 384) & (lane < breadth - 384 + HALO)
    west_gap = lane >= 128 - HALO
    unpacked = []
    for src_b, src_c in ((rlb, rlc), (rrb, rrc)):
        fields_part = src_b[...].astype(jnp.float32)
        parts = []
        for i in range(height // STRIP):
            h, g = divmod(i, per_row)
            blk_c = pltpu.roll(src_c[pl.ds(h * STRIP, STRIP), :], (coef_lane - width * g) % 128, 1)
            blk_f = fields_part[i * STRIP : (i + 1) * STRIP]
            parts.append(jnp.where(lane8 < coef_lane, blk_f, blk_c))
        unpacked.append(jnp.concatenate(parts, axis=0))
    from_l, from_r = unpacked
    for a in range(count):
        east_shift = (breadth - 384 - HALO * a) % 128
        west_shift = (128 - HALO - HALO * a) % 128
        tail = X[a, pl.ds(TOP, height), pl.ds(384, 128)]
        tail = jnp.where(east_gap, pltpu.roll(from_r, east_shift, 1), tail)
        tail = jnp.where(west_gap, pltpu.roll(from_l, west_shift, 1), tail)
        X[a, pl.ds(TOP, height), pl.ds(384, 128)] = tail

    def derive(first, size):
        ca[pl.ds(first, size), :] = cn[pl.ds(first - 1, size), :]
        cw[pl.ds(first, size), :] = pltpu.roll(ce[pl.ds(first, size), :], 1, 1)
        cd[pl.ds(first, size), :] = 2.0 - (
            cn[pl.ds(first, size), :] + ca[pl.ds(first, size), :] + ce[pl.ds(first, size), :] + cw[pl.ds(first, size), :]
        )

    derive(8, rows - 16)
    acc[...] = jnp.zeros_like(acc)
    acc_mid[...] = jnp.zeros_like(acc_mid)
    src_tiles[:, :, 0] = jnp.zeros((2, steps, STRIP, COLS), jnp.float32)

    def slot_places(s):
        slot = member * slots + s
        act = jnp.where(s < pc_ref[member], jnp.float32(1.0), jnp.float32(0.0))
        row_first = me_lat * height
        col_first = me_lon * breadth
        places = []
        for comp in range(2):
            cell = sc_ref[pl_ref[comp, slot]]
            r = lax.div(cell, nlon_cells)
            c = cell - r * nlon_cells
            rb = r - row_first + TOP
            d = c - col_first
            d = jnp.where(d < 0, d + nlon_cells, d)
            near = d < breadth + HALO
            wrap = d >= nlon_cells - HALO
            cb = jnp.where(near, d, d - nlon_cells + COLS)
            valid = (rb >= TOP - HALO) & (rb < TOP + height + HALO) & (near | wrap)
            hit = (sub8 == lax.rem(jnp.maximum(rb, 0), 8)) & (lane_w == cb)
            for t in range(steps):
                amp = wav_ref[t] if comp == 0 else res_ref[steps - 1 - t, slot]
                src_tiles[comp, t, 1] = jnp.where(hit, amp, jnp.float32(0.0))
            places.append((rb, valid))
        return act, places

    def run_blocks(s, t, block_list, act, places):
        bufs = [(X.at[s * fields + comp], X.at[s * fields + 2 + comp], work.at[s, comp]) for comp in range(2)]
        ei, ci, ni = t % 3, (t + 1) % 3, (t + 2) % 3
        for k in block_list:
            r0 = 8 * k
            dd = cd[pl.ds(r0, 8), :]
            nn = cn[pl.ds(r0, 8), :]
            aa = ca[pl.ds(r0, 8), :]
            ee = ce[pl.ds(r0, 8), :]
            ww = cw[pl.ds(r0, 8), :]
            outs = []
            for comp in range(2):
                rb, valid = places[comp]
                pick = (valid & (rb >= r0) & (rb < r0 + 8)).astype(jnp.int32)
                cur_ref, ear_ref, nxt_ref = bufs[comp][ci], bufs[comp][ei], bufs[comp][ni]
                cur = cur_ref[pl.ds(r0, 8), :]
                above = cur_ref[pl.ds(r0 - 1, 8), :]
                below = cur_ref[pl.ds(r0 + 1, 8), :]
                ear = ear_ref[pl.ds(r0, 8), :]
                west = pltpu.roll(cur, 1, 1)
                east = pltpu.roll(cur, COLS - 1, 1)
                nxt = dd * cur + nn * below + aa * above + ee * east + ww * west - ear
                nxt = nxt + src_tiles[comp, t, pick]
                nxt_ref[pl.ds(r0, 8), :] = nxt
                outs.append(nxt)
            if 2 <= k < blocks - 2:
                row = r0 - TOP
                if MID_FIRST <= row < MID_FIRST + acc_mid.shape[0]:
                    dst, row = acc_mid, row - MID_FIRST
                else:
                    dst, row = acc, (row if row < MID_FIRST else row - acc_mid.shape[0])
                dst[pl.ds(row, 8), :] += (outs[0] * act) * outs[1]

    def phase(ranges):
        def body(s, carry):
            act, places = slot_places(s)
            for t in range(steps):
                run_blocks(s, t, ranges(t), act, places)
            return carry

        lax.fori_loop(0, slots, body, 0)

    inner = lambda t: list(range(3 + t, blocks - 3 - t))
    phase(inner)

    mid_out = pltpu.make_async_remote_copy(
        acc_mid, pacc_mid, send_sem.at[len(copies) + 1], recv_sem.at[len(copies) + 1],
        device_id={"pair": partner}, device_id_type=MESH,
    )
    mid_out.start()

    for i in range(4, len(copies)):
        finish(i)

    @pl.when(jnp.logical_not(has_up))
    def _():
        rab[...] = jnp.zeros_like(rab)
        rac[...] = jnp.zeros_like(rac)
        rc[TL] = jnp.zeros((STRIP, 128), jnp.float32)
        rc[TR] = jnp.zeros((STRIP, 128), jnp.float32)

    @pl.when(jnp.logical_not(has_down))
    def _():
        rbb[...] = jnp.zeros_like(rbb)
        rbc[...] = jnp.zeros_like(rbc)
        rc[BL] = jnp.zeros((STRIP, 128), jnp.float32)
        rc[BR] = jnp.zeros((STRIP, 128), jnp.float32)

    east_c = (lane8 >= breadth - 384) & (lane8 < breadth - 384 + HALO)
    west_c = lane8 >= 128 - HALO
    for src_b, src_c, first, low_half, (c_east, c_west) in (
        (rab, rac, TOP - STRIP, False, (TR, TL)),
        (rbb, rbc, TOP + height, True, (BR, BL)),
    ):
        for a in range(count):
            b = a // 2
            if a < nfield:
                both = src_b[b // 2].astype(jnp.float32)
                blk = both[STRIP * (b % 2) : STRIP * (b % 2 + 1)]
            else:
                blk = src_c[...]
            even = a % 2 == 0
            if low_half:
                blk = blk if even else pltpu.roll(blk, 4, 0)
                blk = jnp.where(sub8 < 4, blk, jnp.float32(0.0))
                band = sub_c < 4
            else:
                blk = pltpu.roll(blk, 4, 0) if even else blk
                blk = jnp.where(sub8 >= 4, blk, jnp.float32(0.0))
                band = sub_c >= 4
            X[a, pl.ds(first, STRIP), :] = blk
            east_shift = (breadth - 384 - HALO * a) % 128
            west_shift = (128 - HALO - HALO * a) % 128
            tail = X[a, pl.ds(first, STRIP), pl.ds(384, 128)]
            tail = jnp.where(band & east_c, pltpu.roll(rc[c_east], east_shift, 1), tail)
            tail = jnp.where(band & west_c, pltpu.roll(rc[c_west], west_shift, 1), tail)
            X[a, pl.ds(first, STRIP), pl.ds(384, 128)] = tail

    derive(8, 24)
    derive(rows - 32, 24)

    def outer(t):
        if t < steps - 1:
            return list(range(1, 3 + t)) + list(range(blocks - 3 - t, blocks - 1))
        return list(range(2, 3 + t)) + list(range(blocks - 3 - t, blocks - 2))

    phase(outer)

    to_partner = pltpu.make_async_remote_copy(
        acc, pacc, send_sem.at[len(copies)], recv_sem.at[len(copies)], device_id={"pair": partner}, device_id_type=MESH
    )
    to_partner.start()
    to_partner.wait()
    mid_out.wait()
    mids = acc_mid.shape[0]
    for side, (edge_ref, mid_ref) in enumerate(((acc, acc_mid), (pacc, pacc_mid))):
        o_ref[side, pl.ds(0, MID_FIRST), :] = edge_ref[pl.ds(0, MID_FIRST), pl.ds(0, breadth)]
        o_ref[side, pl.ds(MID_FIRST, mids), :] = mid_ref[:, pl.ds(0, breadth)]
        o_ref[side, pl.ds(MID_FIRST + mids, height - MID_FIRST - mids), :] = edge_ref[
            pl.ds(MID_FIRST, height - MID_FIRST - mids), pl.ds(0, breadth)
        ]


def add_kernel(parts_ref, o_ref):
    o_ref[...] = parts_ref[0] + parts_ref[1]


def add_parts(parts):
    vmem = pl.BlockSpec(memory_space=pltpu.VMEM)
    return pl.pallas_call(
        add_kernel,
        out_shape=jax.ShapeDtypeStruct(parts.shape[1:], parts.dtype),
        in_specs=[vmem],
        out_specs=vmem,
    )(parts)


def fused(wave_states, lat_faces, lon_faces, scalars, nlon_cells):
    slots, fields, height, breadth = wave_states.shape
    nfield = slots * fields
    count = nfield + 2
    rows = height + 2 * TOP
    smem = pl.BlockSpec(memory_space=pltpu.SMEM)
    vmem = pl.BlockSpec(memory_space=pltpu.VMEM)
    per_row = 128 // (2 * HALO)
    coef_rows = STRIP * ((height // STRIP + per_row - 1) // per_row)
    packed_b = pltpu.VMEM((height, 128), jnp.bfloat16)
    packed_c = pltpu.VMEM((coef_rows, 128), jnp.float32)
    strip_b16 = pltpu.VMEM((nfield // 4, 2 * STRIP, COLS), jnp.bfloat16)
    strip_c = pltpu.VMEM((STRIP, COLS), jnp.float32)
    plane = pltpu.VMEM((rows, COLS), jnp.float32)
    return pl.pallas_call(
        functools.partial(fused_kernel, nlon_cells),
        out_shape=jax.ShapeDtypeStruct((2, height, breadth), jnp.float32),
        in_specs=[smem] * 5 + [pl.BlockSpec(memory_space=pl.ANY)] * 3,
        out_specs=vmem,
        scratch_shapes=[
            pltpu.VMEM(wave_states.shape, wave_states.dtype),
            pltpu.VMEM(lat_faces.shape, jnp.float32),
            pltpu.VMEM(lon_faces.shape, jnp.float32),
            pltpu.SemaphoreType.DMA((slots + 2,)),
            pltpu.VMEM((2, 4, 2, STRIP, COLS), jnp.float32),
            pltpu.VMEM((count, rows, COLS), jnp.float32),
            pltpu.VMEM((slots, 2, rows, COLS), jnp.float32),
            plane,
            plane,
            plane,
            pltpu.VMEM((2 * MID_FIRST, COLS), jnp.float32),
            pltpu.VMEM((2 * MID_FIRST, COLS), jnp.float32),
            pltpu.VMEM((height - 2 * MID_FIRST, COLS), jnp.float32),
            pltpu.VMEM((height - 2 * MID_FIRST, COLS), jnp.float32),
            pltpu.VMEM((height, 128), jnp.float32),
            pltpu.VMEM((height, 128), jnp.float32),
        ]
        + [packed_b, packed_b, packed_c, packed_c, strip_b16, strip_b16, strip_c, strip_c] * 2
        + [
            pltpu.VMEM((4, STRIP, 128), jnp.float32),
            pltpu.SemaphoreType.DMA((14,)),
            pltpu.SemaphoreType.DMA((14,)),
        ],
        compiler_params=pltpu.CompilerParams(collective_id=0, has_side_effects=True, vmem_limit_bytes=60 * 1024 * 1024),
    )(*scalars, wave_states, lat_faces, lon_faces)


def body(
    wave_states,
    pair_list,
    pair_counts,
    residuals,
    station_cell,
    source_wavelet,
    lat_faces,
    lon_faces,
):
    height, breadth = lat_faces.shape
    nlon_cells = breadth * lax.axis_size("lon")
    scalars = (pair_list.T, pair_counts, residuals.T, station_cell, source_wavelet)
    return add_parts(fused(wave_states, lat_faces, lon_faces, scalars, nlon_cells))


def solution(mesh):
    in_specs = (
        P("pair", None, "lat", "lon"),
        P(),
        P(),
        P(),
        P(),
        P(),
        P("lat", "lon"),
        P("lat", "lon"),
    )
    out_specs = P("lat", "lon")
    return jax.shard_map(body, mesh=mesh, in_specs=in_specs, out_specs=out_specs, check_vma=False)
```

```python
import functools

import jax
import jax.numpy as jnp
from jax import lax
from jax.experimental import pallas as pl
from jax.experimental.pallas import tpu as pltpu
from jax.sharding import PartitionSpec as P

HALO = 4
TOP = 16
COLS = 512
STRIP = 8
MESH = pl.DeviceIdType.MESH
TL, TR, BL, BR = 0, 1, 2, 3
MID_FIRST = 32


def fused_kernel(
    nlon_cells,
    pl_ref, pc_ref, res_ref, sc_ref, wav_ref,
    f_hbm, lat_hbm, lon_hbm,
    o_ref,
    f_ref, lat_ref, lon_ref, in_sem, src_tiles,
    X, work, ca, cw, cd, acc, pacc, acc_mid, pacc_mid,
    pack_l, pack_r,
    send_lb, send_rb, send_lc, send_rc, send_tb, send_bb, send_tc, send_bc,
    rlb, rrb, rlc, rrc, rab, rbb, rac, rbc, rc,
    send_sem, recv_sem,
):
    slots, fields, height, breadth = f_ref.shape
    nfield = slots * fields
    count = nfield + 2
    rows = X.shape[1]
    blocks = rows // 8
    steps = wav_ref.shape[0]
    nlon = lax.axis_size("lon")
    nlat = lax.axis_size("lat")
    me_lat = lax.axis_index("lat")
    me_lon = lax.axis_index("lon")
    member = lax.axis_index("pair")
    partner = 1 - member
    right = lax.rem(me_lon + 1, nlon)
    left = lax.rem(me_lon + nlon - 1, nlon)
    has_up = me_lat > 0
    has_down = me_lat < nlat - 1
    up = jnp.maximum(me_lat - 1, 0)
    down = jnp.minimum(me_lat + 1, nlat - 1)
    cn = X.at[nfield]
    ce = X.at[nfield + 1]

    barrier = pltpu.get_barrier_semaphore()
    pl.semaphore_signal(barrier, 1, device_id={"pair": partner}, device_id_type=MESH)
    for lon_to in (left, right):
        pl.semaphore_signal(barrier, 1, device_id={"lon": lon_to}, device_id_type=MESH)

    @pl.when(has_up)
    def _():
        for lon_to in (me_lon, left, right):
            pl.semaphore_signal(barrier, 1, device_id={"lat": up, "lon": lon_to}, device_id_type=MESH)

    @pl.when(has_down)
    def _():
        for lon_to in (me_lon, left, right):
            pl.semaphore_signal(barrier, 1, device_id={"lat": down, "lon": lon_to}, device_id_type=MESH)

    loads = [pltpu.make_async_copy(f_hbm.at[i], f_ref.at[i], in_sem.at[i]) for i in range(slots)]
    loads.append(pltpu.make_async_copy(lat_hbm, lat_ref, in_sem.at[slots]))
    loads.append(pltpu.make_async_copy(lon_hbm, lon_ref, in_sem.at[slots + 1]))
    for copy in loads:
        copy.start()

    lane = lax.broadcasted_iota(jnp.int32, (height, 128), 1)
    quad = lane // HALO
    sub8 = lax.broadcasted_iota(jnp.int32, (STRIP, COLS), 0)
    lane8 = lax.broadcasted_iota(jnp.int32, (STRIP, 128), 1)
    sub_c = lax.broadcasted_iota(jnp.int32, (STRIP, 128), 0)
    lane_w = lax.broadcasted_iota(jnp.int32, (STRIP, COLS), 1)
    zero_rows = jnp.zeros((TOP, COLS), jnp.float32)

    for a in range(count):
        if a % fields == 0 and a < nfield:
            loads[a // fields].wait()
        if a == nfield:
            loads[slots].wait()
            loads[slots + 1].wait()
        if a < nfield:
            raw = f_ref[a // fields, a % fields].astype(jnp.float32)
            if a % 2 == 0:
                live = a // fields < pc_ref[member]
                raw = raw * jnp.where(live, jnp.float32(1.0), jnp.float32(0.0))
        else:
            raw = (lat_ref if a == nfield else lon_ref)[...]
        X[a, pl.ds(TOP, height), pl.ds(0, breadth)] = raw
        tail = X[a, pl.ds(TOP, height), pl.ds(384, 128)]
        X[a, pl.ds(TOP, height), pl.ds(384, 128)] = jnp.where(lane < breadth - 384, tail, jnp.float32(0.0))
        X[a, pl.ds(0, TOP), :] = zero_rows
        X[a, pl.ds(TOP + height, rows - TOP - height), :] = zero_rows

    @pl.when(me_lat == nlat - 1)
    def _():
        last = TOP + height - 8
        cn[pl.ds(last, 8), :] = jnp.where(sub8 == 7, jnp.float32(0.0), cn[pl.ds(last, 8), :])

    pl_acc = jnp.zeros((height, 128), jnp.float32)
    pr_acc = jnp.zeros((height, 128), jnp.float32)
    for a in range(count):
        head = X[a, pl.ds(TOP, height), pl.ds(0, 128)]
        tail = X[a, pl.ds(TOP, height), pl.ds(384, 128)]
        pl_acc = jnp.where(quad == a, pltpu.roll(head, (HALO * a) % 128, 1), pl_acc)
        pr_acc = jnp.where(quad == a, pltpu.roll(tail, (HALO * a - (breadth - 384 - HALO)) % 128, 1), pr_acc)
    pack_l[...] = pl_acc
    pack_r[...] = pr_acc

    coef_lane = HALO * nfield
    width = 2 * HALO
    per_row = 128 // width
    send_lb[...] = pl_acc.astype(jnp.bfloat16)
    send_rb[...] = pr_acc.astype(jnp.bfloat16)
    for src, dst in ((pl_acc, send_lc), (pr_acc, send_rc)):
        for h in range(dst.shape[0] // STRIP):
            packed = jnp.zeros((STRIP, 128), jnp.float32)
            for g in range(per_row):
                i = h * per_row + g
                if i * STRIP >= height:
                    break
                blk = src[i * STRIP : (i + 1) * STRIP]
                packed = jnp.where(lane8 // width == g, pltpu.roll(blk, (width * g - coef_lane) % 128, 1), packed)
            dst[pl.ds(h * STRIP, STRIP), :] = packed

    def strip_pair(a, first, keep_low):
        lo = X[a, pl.ds(first, STRIP), :]
        hi = X[a + 1, pl.ds(first, STRIP), :]
        if keep_low:
            return jnp.where(sub8 < 4, lo, pltpu.roll(hi, 4, 0))
        return jnp.where(sub8 < 4, pltpu.roll(lo, 4, 0), hi)

    for dst_b, dst_c, first, keep_low in (
        (send_tb, send_tc, TOP, True),
        (send_bb, send_bc, TOP + height - STRIP, False),
    ):
        for j in range(dst_b.shape[0]):
            both = [strip_pair(4 * j, first, keep_low), strip_pair(4 * j + 2, first, keep_low)]
            dst_b[j] = jnp.concatenate(both, axis=0).astype(jnp.bfloat16)
        dst_c[...] = strip_pair(nfield, first, keep_low)

    pl.semaphore_wait(barrier, 3 + 3 * has_up.astype(jnp.int32) + 3 * has_down.astype(jnp.int32))

    last8 = pl.ds(height - STRIP, STRIP)
    first8 = pl.ds(0, STRIP)
    copies = [
        (send_rb, rlb, me_lat, right, None),
        (send_rc, rlc, me_lat, right, None),
        (send_lb, rrb, me_lat, left, None),
        (send_lc, rrc, me_lat, left, None),
        (send_tb, rbb, up, me_lon, "up"),
        (send_tc, rbc, up, me_lon, "up"),
        (send_bb, rab, down, me_lon, "down"),
        (send_bc, rac, down, me_lon, "down"),
        (pack_r.at[last8], rc.at[TL], down, right, "down"),
        (pack_l.at[last8], rc.at[TR], down, left, "down"),
        (pack_r.at[first8], rc.at[BL], up, right, "up"),
        (pack_l.at[first8], rc.at[BR], up, left, "up"),
    ]

    def descriptor(i):
        src, dst, lat_to, lon_to, _ = copies[i]
        return pltpu.make_async_remote_copy(
            src, dst, send_sem.at[i], recv_sem.at[i], device_id={"lat": lat_to, "lon": lon_to}, device_id_type=MESH
        )

    def when(cond, fn):
        if cond is None:
            fn()
        else:
            pl.when(has_up if cond == "up" else has_down)(fn)

    def finish(i):
        cond = copies[i][4]
        when(cond, lambda: descriptor(i).wait_send())
        mirror = {None: None, "up": "down", "down": "up"}[cond]
        when(mirror, lambda: descriptor(i).wait_recv())

    for i, copy in enumerate(copies):
        when(copy[4], lambda i=i: descriptor(i).start())

    for i in range(4):
        finish(i)
    east_gap = (lane >= breadth - 384) & (lane < breadth - 384 + HALO)
    west_gap = lane >= 128 - HALO
    unpacked = []
    for src_b, src_c in ((rlb, rlc), (rrb, rrc)):
        fields_part = src_b[...].astype(jnp.float32)
        parts = []
        for i in range(height // STRIP):
            h, g = divmod(i, per_row)
            blk_c = pltpu.roll(src_c[pl.ds(h * STRIP, STRIP), :], (coef_lane - width * g) % 128, 1)
            blk_f = fields_part[i * STRIP : (i + 1) * STRIP]
            parts.append(jnp.where(lane8 < coef_lane, blk_f, blk_c))
        unpacked.append(jnp.concatenate(parts, axis=0))
    from_l, from_r = unpacked
    for a in range(count):
        east_shift = (breadth - 384 - HALO * a) % 128
        west_shift = (128 - HALO - HALO * a) % 128
        tail = X[a, pl.ds(TOP, height), pl.ds(384, 128)]
        tail = jnp.where(east_gap, pltpu.roll(from_r, east_shift, 1), tail)
        tail = jnp.where(west_gap, pltpu.roll(from_l, west_shift, 1), tail)
        X[a, pl.ds(TOP, height), pl.ds(384, 128)] = tail

    def derive(first, size):
        ca[pl.ds(first, size), :] = cn[pl.ds(first - 1, size), :]
        cw[pl.ds(first, size), :] = pltpu.roll(ce[pl.ds(first, size), :], 1, 1)
        cd[pl.ds(first, size), :] = 2.0 - (
            cn[pl.ds(first, size), :] + ca[pl.ds(first, size), :] + ce[pl.ds(first, size), :] + cw[pl.ds(first, size), :]
        )

    derive(8, rows - 16)
    acc[...] = jnp.zeros_like(acc)
    acc_mid[...] = jnp.zeros_like(acc_mid)
    src_tiles[:, :, 0] = jnp.zeros((2, steps, STRIP, COLS), jnp.float32)

    def slot_places(s):
        slot = member * slots + s
        act = jnp.where(s < pc_ref[member], jnp.float32(1.0), jnp.float32(0.0))
        row_first = me_lat * height
        col_first = me_lon * breadth
        places = []
        for comp in range(2):
            cell = sc_ref[pl_ref[comp, slot]]
            r = lax.div(cell, nlon_cells)
            c = cell - r * nlon_cells
            rb = r - row_first + TOP
            d = c - col_first
            d = jnp.where(d < 0, d + nlon_cells, d)
            near = d < breadth + HALO
            wrap = d >= nlon_cells - HALO
            cb = jnp.where(near, d, d - nlon_cells + COLS)
            valid = (rb >= TOP - HALO) & (rb < TOP + height + HALO) & (near | wrap)
            hit = (sub8 == lax.rem(jnp.maximum(rb, 0), 8)) & (lane_w == cb)
            for t in range(steps):
                amp = wav_ref[t] * act if comp == 0 else res_ref[steps - 1 - t, slot]
                src_tiles[comp, t, 1] = jnp.where(hit, amp, jnp.float32(0.0))
            places.append((rb, valid))
        return act, places

    def run_blocks(s, t, block_list, act, places):
        bufs = [(X.at[s * fields + comp], X.at[s * fields + 2 + comp], work.at[s, comp]) for comp in range(2)]
        ei, ci, ni = t % 3, (t + 1) % 3, (t + 2) % 3
        for k in block_list:
            r0 = 8 * k
            dd = cd[pl.ds(r0, 8), :]
            nn = cn[pl.ds(r0, 8), :]
            aa = ca[pl.ds(r0, 8), :]
            ee = ce[pl.ds(r0, 8), :]
            ww = cw[pl.ds(r0, 8), :]
            outs = []
            for comp in range(2):
                rb, valid = places[comp]
                pick = (valid & (rb >= r0) & (rb < r0 + 8)).astype(jnp.int32)
                cur_ref, ear_ref, nxt_ref = bufs[comp][ci], bufs[comp][ei], bufs[comp][ni]
                cur = cur_ref[pl.ds(r0, 8), :]
                above = cur_ref[pl.ds(r0 - 1, 8), :]
                below = cur_ref[pl.ds(r0 + 1, 8), :]
                ear = ear_ref[pl.ds(r0, 8), :]
                west = pltpu.roll(cur, 1, 1)
                east = pltpu.roll(cur, COLS - 1, 1)
                nxt = dd * cur + nn * below + aa * above + ee * east + ww * west - ear
                nxt = nxt + src_tiles[comp, t, pick]
                nxt_ref[pl.ds(r0, 8), :] = nxt
                outs.append(nxt)
            if 2 <= k < blocks - 2:
                row = r0 - TOP
                if MID_FIRST <= row < MID_FIRST + acc_mid.shape[0]:
                    dst, row = acc_mid, row - MID_FIRST
                else:
                    dst, row = acc, (row if row < MID_FIRST else row - acc_mid.shape[0])
                dst[pl.ds(row, 8), :] += outs[0] * outs[1]

    def phase(ranges):
        def body(s, carry):
            act, places = slot_places(s)
            for t in range(steps):
                run_blocks(s, t, ranges(t), act, places)
            return carry

        lax.fori_loop(0, slots, body, 0)

    inner = lambda t: list(range(3 + t, blocks - 3 - t))
    phase(inner)

    mid_out = pltpu.make_async_remote_copy(
        acc_mid, pacc_mid, send_sem.at[len(copies) + 1], recv_sem.at[len(copies) + 1],
        device_id={"pair": partner}, device_id_type=MESH,
    )
    mid_out.start()

    for i in range(4, len(copies)):
        finish(i)

    @pl.when(jnp.logical_not(has_up))
    def _():
        rab[...] = jnp.zeros_like(rab)
        rac[...] = jnp.zeros_like(rac)
        rc[TL] = jnp.zeros((STRIP, 128), jnp.float32)
        rc[TR] = jnp.zeros((STRIP, 128), jnp.float32)

    @pl.when(jnp.logical_not(has_down))
    def _():
        rbb[...] = jnp.zeros_like(rbb)
        rbc[...] = jnp.zeros_like(rbc)
        rc[BL] = jnp.zeros((STRIP, 128), jnp.float32)
        rc[BR] = jnp.zeros((STRIP, 128), jnp.float32)

    east_c = (lane8 >= breadth - 384) & (lane8 < breadth - 384 + HALO)
    west_c = lane8 >= 128 - HALO
    for src_b, src_c, first, low_half, (c_east, c_west) in (
        (rab, rac, TOP - STRIP, False, (TR, TL)),
        (rbb, rbc, TOP + height, True, (BR, BL)),
    ):
        for a in range(count):
            b = a // 2
            if a < nfield:
                both = src_b[b // 2].astype(jnp.float32)
                blk = both[STRIP * (b % 2) : STRIP * (b % 2 + 1)]
            else:
                blk = src_c[...]
            even = a % 2 == 0
            if low_half:
                blk = blk if even else pltpu.roll(blk, 4, 0)
                blk = jnp.where(sub8 < 4, blk, jnp.float32(0.0))
                band = sub_c < 4
            else:
                blk = pltpu.roll(blk, 4, 0) if even else blk
                blk = jnp.where(sub8 >= 4, blk, jnp.float32(0.0))
                band = sub_c >= 4
            X[a, pl.ds(first, STRIP), :] = blk
            east_shift = (breadth - 384 - HALO * a) % 128
            west_shift = (128 - HALO - HALO * a) % 128
            tail = X[a, pl.ds(first, STRIP), pl.ds(384, 128)]
            tail = jnp.where(band & east_c, pltpu.roll(rc[c_east], east_shift, 1), tail)
            tail = jnp.where(band & west_c, pltpu.roll(rc[c_west], west_shift, 1), tail)
            X[a, pl.ds(first, STRIP), pl.ds(384, 128)] = tail

    derive(8, 24)
    derive(rows - 32, 24)

    def outer(t):
        if t < steps - 1:
            return list(range(1, 3 + t)) + list(range(blocks - 3 - t, blocks - 1))
        return list(range(2, 3 + t)) + list(range(blocks - 3 - t, blocks - 2))

    phase(outer)

    to_partner = pltpu.make_async_remote_copy(
        acc, pacc, send_sem.at[len(copies)], recv_sem.at[len(copies)], device_id={"pair": partner}, device_id_type=MESH
    )
    to_partner.start()
    to_partner.wait()
    mid_out.wait()
    edge = acc[...] + pacc[...]
    mids = acc_mid.shape[0]
    o_ref[pl.ds(0, MID_FIRST), :] = edge[0:MID_FIRST, 0:breadth]
    o_ref[pl.ds(MID_FIRST, mids), :] = (acc_mid[...] + pacc_mid[...])[:, 0:breadth]
    o_ref[pl.ds(MID_FIRST + mids, height - MID_FIRST - mids), :] = edge[MID_FIRST:, 0:breadth]


def fused(wave_states, lat_faces, lon_faces, scalars, nlon_cells):
    slots, fields, height, breadth = wave_states.shape
    nfield = slots * fields
    count = nfield + 2
    rows = height + 2 * TOP
    smem = pl.BlockSpec(memory_space=pltpu.SMEM)
    vmem = pl.BlockSpec(memory_space=pltpu.VMEM)
    per_row = 128 // (2 * HALO)
    coef_rows = STRIP * ((height // STRIP + per_row - 1) // per_row)
    packed_b = pltpu.VMEM((height, 128), jnp.bfloat16)
    packed_c = pltpu.VMEM((coef_rows, 128), jnp.float32)
    strip_b16 = pltpu.VMEM((nfield // 4, 2 * STRIP, COLS), jnp.bfloat16)
    strip_c = pltpu.VMEM((STRIP, COLS), jnp.float32)
    plane = pltpu.VMEM((rows, COLS), jnp.float32)
    return pl.pallas_call(
        functools.partial(fused_kernel, nlon_cells),
        out_shape=jax.ShapeDtypeStruct((height, breadth), jnp.float32),
        in_specs=[smem] * 5 + [pl.BlockSpec(memory_space=pl.ANY)] * 3,
        out_specs=vmem,
        scratch_shapes=[
            pltpu.VMEM(wave_states.shape, wave_states.dtype),
            pltpu.VMEM(lat_faces.shape, jnp.float32),
            pltpu.VMEM(lon_faces.shape, jnp.float32),
            pltpu.SemaphoreType.DMA((slots + 2,)),
            pltpu.VMEM((2, 4, 2, STRIP, COLS), jnp.float32),
            pltpu.VMEM((count, rows, COLS), jnp.float32),
            pltpu.VMEM((slots, 2, rows, COLS), jnp.float32),
            plane,
            plane,
            plane,
            pltpu.VMEM((2 * MID_FIRST, COLS), jnp.float32),
            pltpu.VMEM((2 * MID_FIRST, COLS), jnp.float32),
            pltpu.VMEM((height - 2 * MID_FIRST, COLS), jnp.float32),
            pltpu.VMEM((height - 2 * MID_FIRST, COLS), jnp.float32),
            pltpu.VMEM((height, 128), jnp.float32),
            pltpu.VMEM((height, 128), jnp.float32),
        ]
        + [packed_b, packed_b, packed_c, packed_c, strip_b16, strip_b16, strip_c, strip_c] * 2
        + [
            pltpu.VMEM((4, STRIP, 128), jnp.float32),
            pltpu.SemaphoreType.DMA((14,)),
            pltpu.SemaphoreType.DMA((14,)),
        ],
        compiler_params=pltpu.CompilerParams(collective_id=0, has_side_effects=True, vmem_limit_bytes=60 * 1024 * 1024),
    )(*scalars, wave_states, lat_faces, lon_faces)


def body(
    wave_states,
    pair_list,
    pair_counts,
    residuals,
    station_cell,
    source_wavelet,
    lat_faces,
    lon_faces,
):
    height, breadth = lat_faces.shape
    nlon_cells = breadth * lax.axis_size("lon")
    scalars = (pair_list.T, pair_counts, residuals.T, station_cell, source_wavelet)
    return fused(wave_states, lat_faces, lon_faces, scalars, nlon_cells)


def solution(mesh):
    in_specs = (
        P("pair", None, "lat", "lon"),
        P(),
        P(),
        P(),
        P(),
        P(),
        P("lat", "lon"),
        P("lat", "lon"),
    )
    out_specs = P("lat", "lon")
    return jax.shard_map(body, mesh=mesh, in_specs=in_specs, out_specs=out_specs, check_vma=False)
```

```python
import functools

import jax
import jax.numpy as jnp
from jax import lax
from jax.experimental import pallas as pl
from jax.experimental.pallas import tpu as pltpu
from jax.sharding import PartitionSpec as P

HALO = 4
TOP = 16
COLS = 512
STRIP = 8
MESH = pl.DeviceIdType.MESH
TL, TR, BL, BR = 0, 1, 2, 3
MID_FIRST = 32


def fused_kernel(
    nlon_cells,
    pl_ref, pc_ref, res_ref, sc_ref, wav_ref,
    f_hbm, lat_hbm, lon_hbm,
    o_ref,
    f_ref, lat_ref, lon_ref, in_sem, src_tiles,
    X, work, ca, cw, cd, acc, pacc, acc_mid, pacc_mid,
    pack_l, pack_r,
    send_lb, send_rb, send_lc, send_rc, send_tb, send_bb, send_tc, send_bc,
    rlb, rrb, rlc, rrc, rab, rbb, rac, rbc, rc,
    send_sem, recv_sem,
):
    slots, fields, height, breadth = f_ref.shape
    nfield = slots * fields
    count = nfield + 2
    rows = X.shape[1]
    blocks = rows // 8
    steps = wav_ref.shape[0]
    nlon = lax.axis_size("lon")
    nlat = lax.axis_size("lat")
    me_lat = lax.axis_index("lat")
    me_lon = lax.axis_index("lon")
    member = lax.axis_index("pair")
    partner = 1 - member
    right = lax.rem(me_lon + 1, nlon)
    left = lax.rem(me_lon + nlon - 1, nlon)
    has_up = me_lat > 0
    has_down = me_lat < nlat - 1
    up = jnp.maximum(me_lat - 1, 0)
    down = jnp.minimum(me_lat + 1, nlat - 1)
    cn = X.at[nfield]
    ce = X.at[nfield + 1]

    barrier = pltpu.get_barrier_semaphore()
    pl.semaphore_signal(barrier, 1, device_id={"pair": partner}, device_id_type=MESH)
    for lon_to in (left, right):
        pl.semaphore_signal(barrier, 1, device_id={"lon": lon_to}, device_id_type=MESH)

    @pl.when(has_up)
    def _():
        for lon_to in (me_lon, left, right):
            pl.semaphore_signal(barrier, 1, device_id={"lat": up, "lon": lon_to}, device_id_type=MESH)

    @pl.when(has_down)
    def _():
        for lon_to in (me_lon, left, right):
            pl.semaphore_signal(barrier, 1, device_id={"lat": down, "lon": lon_to}, device_id_type=MESH)

    loads = [pltpu.make_async_copy(f_hbm.at[i], f_ref.at[i], in_sem.at[i]) for i in range(slots)]
    loads.append(pltpu.make_async_copy(lat_hbm, lat_ref, in_sem.at[slots]))
    loads.append(pltpu.make_async_copy(lon_hbm, lon_ref, in_sem.at[slots + 1]))
    for copy in loads:
        copy.start()

    lane = lax.broadcasted_iota(jnp.int32, (height, 128), 1)
    quad = lane // HALO
    sub8 = lax.broadcasted_iota(jnp.int32, (STRIP, COLS), 0)
    lane8 = lax.broadcasted_iota(jnp.int32, (STRIP, 128), 1)
    sub_c = lax.broadcasted_iota(jnp.int32, (STRIP, 128), 0)
    lane_w = lax.broadcasted_iota(jnp.int32, (STRIP, COLS), 1)
    zero_rows = jnp.zeros((TOP, COLS), jnp.float32)

    for a in range(count):
        if a % fields == 0 and a < nfield:
            loads[a // fields].wait()
        if a == nfield:
            loads[slots].wait()
            loads[slots + 1].wait()
        if a < nfield:
            raw = f_ref[a // fields, a % fields].astype(jnp.float32)
            if a % 2 == 0:
                live = a // fields < pc_ref[member]
                raw = raw * jnp.where(live, jnp.float32(1.0), jnp.float32(0.0))
        else:
            raw = (lat_ref if a == nfield else lon_ref)[...]
        X[a, pl.ds(TOP, height), pl.ds(0, breadth)] = raw
        tail = X[a, pl.ds(TOP, height), pl.ds(384, 128)]
        X[a, pl.ds(TOP, height), pl.ds(384, 128)] = jnp.where(lane < breadth - 384, tail, jnp.float32(0.0))
        X[a, pl.ds(0, TOP), :] = zero_rows
        X[a, pl.ds(TOP + height, rows - TOP - height), :] = zero_rows

    @pl.when(me_lat == nlat - 1)
    def _():
        last = TOP + height - 8
        cn[pl.ds(last, 8), :] = jnp.where(sub8 == 7, jnp.float32(0.0), cn[pl.ds(last, 8), :])

    pl_acc = jnp.zeros((height, 128), jnp.float32)
    pr_acc = jnp.zeros((height, 128), jnp.float32)
    for a in range(count):
        head = X[a, pl.ds(TOP, height), pl.ds(0, 128)]
        tail = X[a, pl.ds(TOP, height), pl.ds(384, 128)]
        pl_acc = jnp.where(quad == a, pltpu.roll(head, (HALO * a) % 128, 1), pl_acc)
        pr_acc = jnp.where(quad == a, pltpu.roll(tail, (HALO * a - (breadth - 384 - HALO)) % 128, 1), pr_acc)
    pack_l[...] = pl_acc
    pack_r[...] = pr_acc

    coef_lane = HALO * nfield
    width = 2 * HALO
    per_row = 128 // width
    half = height // 2
    lane_h = lax.broadcasted_iota(jnp.int32, (half, 128), 1)
    for src, dst in ((pl_acc, send_lb), (pr_acc, send_rb)):
        folded = jnp.where(lane_h < coef_lane, src[0:half], pltpu.roll(src[half:height], coef_lane, 1))
        dst[...] = folded.astype(jnp.bfloat16)
    for src, dst in ((pl_acc, send_lc), (pr_acc, send_rc)):
        for h in range(dst.shape[0] // STRIP):
            packed = jnp.zeros((STRIP, 128), jnp.float32)
            for g in range(per_row):
                i = h * per_row + g
                if i * STRIP >= height:
                    break
                blk = src[i * STRIP : (i + 1) * STRIP]
                packed = jnp.where(lane8 // width == g, pltpu.roll(blk, (width * g - coef_lane) % 128, 1), packed)
            dst[pl.ds(h * STRIP, STRIP), :] = packed

    def strip_pair(a, first, keep_low):
        lo = X[a, pl.ds(first, STRIP), :]
        hi = X[a + 1, pl.ds(first, STRIP), :]
        if keep_low:
            return jnp.where(sub8 < 4, lo, pltpu.roll(hi, 4, 0))
        return jnp.where(sub8 < 4, pltpu.roll(lo, 4, 0), hi)

    for dst_b, dst_c, first, keep_low in (
        (send_tb, send_tc, TOP, True),
        (send_bb, send_bc, TOP + height - STRIP, False),
    ):
        for j in range(dst_b.shape[0]):
            both = [strip_pair(4 * j, first, keep_low), strip_pair(4 * j + 2, first, keep_low)]
            dst_b[j] = jnp.concatenate(both, axis=0).astype(jnp.bfloat16)
        dst_c[...] = strip_pair(nfield, first, keep_low)

    pl.semaphore_wait(barrier, 3 + 3 * has_up.astype(jnp.int32) + 3 * has_down.astype(jnp.int32))

    last8 = pl.ds(height - STRIP, STRIP)
    first8 = pl.ds(0, STRIP)
    copies = [
        (send_rb, rlb, me_lat, right, None),
        (send_rc, rlc, me_lat, right, None),
        (send_lb, rrb, me_lat, left, None),
        (send_lc, rrc, me_lat, left, None),
        (send_tb, rbb, up, me_lon, "up"),
        (send_tc, rbc, up, me_lon, "up"),
        (send_bb, rab, down, me_lon, "down"),
        (send_bc, rac, down, me_lon, "down"),
        (pack_r.at[last8], rc.at[TL], down, right, "down"),
        (pack_l.at[last8], rc.at[TR], down, left, "down"),
        (pack_r.at[first8], rc.at[BL], up, right, "up"),
        (pack_l.at[first8], rc.at[BR], up, left, "up"),
    ]

    def descriptor(i):
        src, dst, lat_to, lon_to, _ = copies[i]
        return pltpu.make_async_remote_copy(
            src, dst, send_sem.at[i], recv_sem.at[i], device_id={"lat": lat_to, "lon": lon_to}, device_id_type=MESH
        )

    def when(cond, fn):
        if cond is None:
            fn()
        else:
            pl.when(has_up if cond == "up" else has_down)(fn)

    def finish(i):
        cond = copies[i][4]
        when(cond, lambda: descriptor(i).wait_send())
        mirror = {None: None, "up": "down", "down": "up"}[cond]
        when(mirror, lambda: descriptor(i).wait_recv())

    for i, copy in enumerate(copies):
        when(copy[4], lambda i=i: descriptor(i).start())

    for i in range(4):
        finish(i)
    east_gap = (lane >= breadth - 384) & (lane < breadth - 384 + HALO)
    west_gap = lane >= 128 - HALO
    unpacked = []
    for src_b, src_c in ((rlb, rlc), (rrb, rrc)):
        folded = src_b[...].astype(jnp.float32)
        fields_part = jnp.concatenate([folded, pltpu.roll(folded, 128 - coef_lane, 1)], axis=0)
        parts = []
        for i in range(height // STRIP):
            h, g = divmod(i, per_row)
            blk_c = pltpu.roll(src_c[pl.ds(h * STRIP, STRIP), :], (coef_lane - width * g) % 128, 1)
            blk_f = fields_part[i * STRIP : (i + 1) * STRIP]
            parts.append(jnp.where(lane8 < coef_lane, blk_f, blk_c))
        unpacked.append(jnp.concatenate(parts, axis=0))
    from_l, from_r = unpacked
    for a in range(count):
        east_shift = (breadth - 384 - HALO * a) % 128
        west_shift = (128 - HALO - HALO * a) % 128
        tail = X[a, pl.ds(TOP, height), pl.ds(384, 128)]
        tail = jnp.where(east_gap, pltpu.roll(from_r, east_shift, 1), tail)
        tail = jnp.where(west_gap, pltpu.roll(from_l, west_shift, 1), tail)
        X[a, pl.ds(TOP, height), pl.ds(384, 128)] = tail

    def derive(first, size):
        ca[pl.ds(first, size), :] = cn[pl.ds(first - 1, size), :]
        cw[pl.ds(first, size), :] = pltpu.roll(ce[pl.ds(first, size), :], 1, 1)
        cd[pl.ds(first, size), :] = 2.0 - (
            cn[pl.ds(first, size), :] + ca[pl.ds(first, size), :] + ce[pl.ds(first, size), :] + cw[pl.ds(first, size), :]
        )

    derive(8, rows - 16)
    acc[...] = jnp.zeros_like(acc)
    acc_mid[...] = jnp.zeros_like(acc_mid)
    src_tiles[:, :, 0] = jnp.zeros((2, steps, STRIP, COLS), jnp.float32)

    def slot_places(s):
        slot = member * slots + s
        act = jnp.where(s < pc_ref[member], jnp.float32(1.0), jnp.float32(0.0))
        row_first = me_lat * height
        col_first = me_lon * breadth
        places = []
        for comp in range(2):
            cell = sc_ref[pl_ref[comp, slot]]
            r = lax.div(cell, nlon_cells)
            c = cell - r * nlon_cells
            rb = r - row_first + TOP
            d = c - col_first
            d = jnp.where(d < 0, d + nlon_cells, d)
            near = d < breadth + HALO
            wrap = d >= nlon_cells - HALO
            cb = jnp.where(near, d, d - nlon_cells + COLS)
            valid = (rb >= TOP - HALO) & (rb < TOP + height + HALO) & (near | wrap)
            hit = (sub8 == lax.rem(jnp.maximum(rb, 0), 8)) & (lane_w == cb)
            for t in range(steps):
                amp = wav_ref[t] * act if comp == 0 else res_ref[steps - 1 - t, slot]
                src_tiles[comp, t, 1] = jnp.where(hit, amp, jnp.float32(0.0))
            places.append((rb, valid))
        return act, places

    def run_blocks(s, t, block_list, act, places):
        bufs = [(X.at[s * fields + comp], X.at[s * fields + 2 + comp], work.at[s, comp]) for comp in range(2)]
        ei, ci, ni = t % 3, (t + 1) % 3, (t + 2) % 3
        for k in block_list:
            r0 = 8 * k
            dd = cd[pl.ds(r0, 8), :]
            nn = cn[pl.ds(r0, 8), :]
            aa = ca[pl.ds(r0, 8), :]
            ee = ce[pl.ds(r0, 8), :]
            ww = cw[pl.ds(r0, 8), :]
            outs = []
            for comp in range(2):
                rb, valid = places[comp]
                pick = (valid & (rb >= r0) & (rb < r0 + 8)).astype(jnp.int32)
                cur_ref, ear_ref, nxt_ref = bufs[comp][ci], bufs[comp][ei], bufs[comp][ni]
                cur = cur_ref[pl.ds(r0, 8), :]
                above = cur_ref[pl.ds(r0 - 1, 8), :]
                below = cur_ref[pl.ds(r0 + 1, 8), :]
                ear = ear_ref[pl.ds(r0, 8), :]
                west = pltpu.roll(cur, 1, 1)
                east = pltpu.roll(cur, COLS - 1, 1)
                nxt = dd * cur + nn * below + aa * above + ee * east + ww * west - ear
                nxt = nxt + src_tiles[comp, t, pick]
                nxt_ref[pl.ds(r0, 8), :] = nxt
                outs.append(nxt)
            if 2 <= k < blocks - 2:
                row = r0 - TOP
                if MID_FIRST <= row < MID_FIRST + acc_mid.shape[0]:
                    dst, row = acc_mid, row - MID_FIRST
                else:
                    dst, row = acc, (row if row < MID_FIRST else row - acc_mid.shape[0])
                dst[pl.ds(row, 8), :] += outs[0] * outs[1]

    def phase(ranges):
        def body(s, carry):
            act, places = slot_places(s)
            for t in range(steps):
                run_blocks(s, t, ranges(t), act, places)
            return carry

        lax.fori_loop(0, slots, body, 0)

    inner = lambda t: list(range(3 + t, blocks - 3 - t))
    phase(inner)

    mid_out = pltpu.make_async_remote_copy(
        acc_mid, pacc_mid, send_sem.at[len(copies) + 1], recv_sem.at[len(copies) + 1],
        device_id={"pair": partner}, device_id_type=MESH,
    )
    mid_out.start()

    for i in range(4, len(copies)):
        finish(i)

    @pl.when(jnp.logical_not(has_up))
    def _():
        rab[...] = jnp.zeros_like(rab)
        rac[...] = jnp.zeros_like(rac)
        rc[TL] = jnp.zeros((STRIP, 128), jnp.float32)
        rc[TR] = jnp.zeros((STRIP, 128), jnp.float32)

    @pl.when(jnp.logical_not(has_down))
    def _():
        rbb[...] = jnp.zeros_like(rbb)
        rbc[...] = jnp.zeros_like(rbc)
        rc[BL] = jnp.zeros((STRIP, 128), jnp.float32)
        rc[BR] = jnp.zeros((STRIP, 128), jnp.float32)

    east_c = (lane8 >= breadth - 384) & (lane8 < breadth - 384 + HALO)
    west_c = lane8 >= 128 - HALO
    for src_b, src_c, first, low_half, (c_east, c_west) in (
        (rab, rac, TOP - STRIP, False, (TR, TL)),
        (rbb, rbc, TOP + height, True, (BR, BL)),
    ):
        for a in range(count):
            b = a // 2
            if a < nfield:
                both = src_b[b // 2].astype(jnp.float32)
                blk = both[STRIP * (b % 2) : STRIP * (b % 2 + 1)]
            else:
                blk = src_c[...]
            even = a % 2 == 0
            if low_half:
                blk = blk if even else pltpu.roll(blk, 4, 0)
                blk = jnp.where(sub8 < 4, blk, jnp.float32(0.0))
                band = sub_c < 4
            else:
                blk = pltpu.roll(blk, 4, 0) if even else blk
                blk = jnp.where(sub8 >= 4, blk, jnp.float32(0.0))
                band = sub_c >= 4
            X[a, pl.ds(first, STRIP), :] = blk
            east_shift = (breadth - 384 - HALO * a) % 128
            west_shift = (128 - HALO - HALO * a) % 128
            tail = X[a, pl.ds(first, STRIP), pl.ds(384, 128)]
            tail = jnp.where(band & east_c, pltpu.roll(rc[c_east], east_shift, 1), tail)
            tail = jnp.where(band & west_c, pltpu.roll(rc[c_west], west_shift, 1), tail)
            X[a, pl.ds(first, STRIP), pl.ds(384, 128)] = tail

    derive(8, 24)
    derive(rows - 32, 24)

    def outer(t):
        if t < steps - 1:
            return list(range(1, 3 + t)) + list(range(blocks - 3 - t, blocks - 1))
        return list(range(2, 3 + t)) + list(range(blocks - 3 - t, blocks - 2))

    phase(outer)

    to_partner = pltpu.make_async_remote_copy(
        acc, pacc, send_sem.at[len(copies)], recv_sem.at[len(copies)], device_id={"pair": partner}, device_id_type=MESH
    )
    to_partner.start()
    to_partner.wait()
    mid_out.wait()
    edge = acc[...] + pacc[...]
    mids = acc_mid.shape[0]
    o_ref[pl.ds(0, MID_FIRST), :] = edge[0:MID_FIRST, 0:breadth]
    o_ref[pl.ds(MID_FIRST, mids), :] = (acc_mid[...] + pacc_mid[...])[:, 0:breadth]
    o_ref[pl.ds(MID_FIRST + mids, height - MID_FIRST - mids), :] = edge[MID_FIRST:, 0:breadth]


def fused(wave_states, lat_faces, lon_faces, scalars, nlon_cells):
    slots, fields, height, breadth = wave_states.shape
    nfield = slots * fields
    count = nfield + 2
    rows = height + 2 * TOP
    smem = pl.BlockSpec(memory_space=pltpu.SMEM)
    vmem = pl.BlockSpec(memory_space=pltpu.VMEM)
    per_row = 128 // (2 * HALO)
    coef_rows = STRIP * ((height // STRIP + per_row - 1) // per_row)
    packed_b = pltpu.VMEM((height // 2, 128), jnp.bfloat16)
    packed_c = pltpu.VMEM((coef_rows, 128), jnp.float32)
    strip_b16 = pltpu.VMEM((nfield // 4, 2 * STRIP, COLS), jnp.bfloat16)
    strip_c = pltpu.VMEM((STRIP, COLS), jnp.float32)
    plane = pltpu.VMEM((rows, COLS), jnp.float32)
    return pl.pallas_call(
        functools.partial(fused_kernel, nlon_cells),
        out_shape=jax.ShapeDtypeStruct((height, breadth), jnp.float32),
        in_specs=[smem] * 5 + [pl.BlockSpec(memory_space=pl.ANY)] * 3,
        out_specs=vmem,
        scratch_shapes=[
            pltpu.VMEM(wave_states.shape, wave_states.dtype),
            pltpu.VMEM(lat_faces.shape, jnp.float32),
            pltpu.VMEM(lon_faces.shape, jnp.float32),
            pltpu.SemaphoreType.DMA((slots + 2,)),
            pltpu.VMEM((2, 4, 2, STRIP, COLS), jnp.float32),
            pltpu.VMEM((count, rows, COLS), jnp.float32),
            pltpu.VMEM((slots, 2, rows, COLS), jnp.float32),
            plane,
            plane,
            plane,
            pltpu.VMEM((2 * MID_FIRST, COLS), jnp.float32),
            pltpu.VMEM((2 * MID_FIRST, COLS), jnp.float32),
            pltpu.VMEM((height - 2 * MID_FIRST, COLS), jnp.float32),
            pltpu.VMEM((height - 2 * MID_FIRST, COLS), jnp.float32),
            pltpu.VMEM((height, 128), jnp.float32),
            pltpu.VMEM((height, 128), jnp.float32),
        ]
        + [packed_b, packed_b, packed_c, packed_c, strip_b16, strip_b16, strip_c, strip_c] * 2
        + [
            pltpu.VMEM((4, STRIP, 128), jnp.float32),
            pltpu.SemaphoreType.DMA((14,)),
            pltpu.SemaphoreType.DMA((14,)),
        ],
        compiler_params=pltpu.CompilerParams(collective_id=0, has_side_effects=True, vmem_limit_bytes=60 * 1024 * 1024),
    )(*scalars, wave_states, lat_faces, lon_faces)


def body(
    wave_states,
    pair_list,
    pair_counts,
    residuals,
    station_cell,
    source_wavelet,
    lat_faces,
    lon_faces,
):
    height, breadth = lat_faces.shape
    nlon_cells = breadth * lax.axis_size("lon")
    scalars = (pair_list.T, pair_counts, residuals.T, station_cell, source_wavelet)
    return fused(wave_states, lat_faces, lon_faces, scalars, nlon_cells)


def solution(mesh):
    in_specs = (
        P("pair", None, "lat", "lon"),
        P(),
        P(),
        P(),
        P(),
        P(),
        P("lat", "lon"),
        P("lat", "lon"),
    )
    out_specs = P("lat", "lon")
    return jax.shard_map(body, mesh=mesh, in_specs=in_specs, out_specs=out_specs, check_vma=False)
```

```python
import functools

import jax
import jax.numpy as jnp
from jax import lax
from jax.experimental import pallas as pl
from jax.experimental.pallas import tpu as pltpu
from jax.sharding import PartitionSpec as P

HALO = 4
TOP = 16
COLS = 512
STRIP = 8
MESH = pl.DeviceIdType.MESH
TL, TR, BL, BR = 0, 1, 2, 3
MID_FIRST = 32


def fused_kernel(
    nlon_cells,
    pl_ref, pc_ref, res_ref, sc_ref, wav_ref,
    f_hbm, lat_hbm, lon_hbm,
    o_ref,
    f_ref, lat_ref, lon_ref, in_sem, src_tiles,
    X, work, ca, cw, cd, acc, pacc, acc_mid, pacc_mid, acc_bot, pacc_bot,
    pack_l, pack_r,
    send_lb, send_rb, send_lc, send_rc, send_tb, send_bb, send_tc, send_bc,
    rlb, rrb, rlc, rrc, rab, rbb, rac, rbc, rc,
    send_sem, recv_sem,
):
    slots, fields, height, breadth = f_ref.shape
    nfield = slots * fields
    count = nfield + 2
    rows = X.shape[1]
    blocks = rows // 8
    steps = wav_ref.shape[0]
    nlon = lax.axis_size("lon")
    nlat = lax.axis_size("lat")
    me_lat = lax.axis_index("lat")
    me_lon = lax.axis_index("lon")
    member = lax.axis_index("pair")
    partner = 1 - member
    right = lax.rem(me_lon + 1, nlon)
    left = lax.rem(me_lon + nlon - 1, nlon)
    has_up = me_lat > 0
    has_down = me_lat < nlat - 1
    up = jnp.maximum(me_lat - 1, 0)
    down = jnp.minimum(me_lat + 1, nlat - 1)
    cn = X.at[nfield]
    ce = X.at[nfield + 1]

    barrier = pltpu.get_barrier_semaphore()
    pl.semaphore_signal(barrier, 1, device_id={"pair": partner}, device_id_type=MESH)
    for lon_to in (left, right):
        pl.semaphore_signal(barrier, 1, device_id={"lon": lon_to}, device_id_type=MESH)

    @pl.when(has_up)
    def _():
        for lon_to in (me_lon, left, right):
            pl.semaphore_signal(barrier, 1, device_id={"lat": up, "lon": lon_to}, device_id_type=MESH)

    @pl.when(has_down)
    def _():
        for lon_to in (me_lon, left, right):
            pl.semaphore_signal(barrier, 1, device_id={"lat": down, "lon": lon_to}, device_id_type=MESH)

    loads = [pltpu.make_async_copy(f_hbm.at[i], f_ref.at[i], in_sem.at[i]) for i in range(slots)]
    loads.append(pltpu.make_async_copy(lat_hbm, lat_ref, in_sem.at[slots]))
    loads.append(pltpu.make_async_copy(lon_hbm, lon_ref, in_sem.at[slots + 1]))
    for copy in loads:
        copy.start()

    lane = lax.broadcasted_iota(jnp.int32, (height, 128), 1)
    quad = lane // HALO
    sub8 = lax.broadcasted_iota(jnp.int32, (STRIP, COLS), 0)
    lane8 = lax.broadcasted_iota(jnp.int32, (STRIP, 128), 1)
    sub_c = lax.broadcasted_iota(jnp.int32, (STRIP, 128), 0)
    lane_w = lax.broadcasted_iota(jnp.int32, (STRIP, COLS), 1)
    zero_rows = jnp.zeros((TOP, COLS), jnp.float32)

    for a in range(count):
        if a % fields == 0 and a < nfield:
            loads[a // fields].wait()
        if a == nfield:
            loads[slots].wait()
            loads[slots + 1].wait()
        if a < nfield:
            raw = f_ref[a // fields, a % fields].astype(jnp.float32)
            if a % 2 == 0:
                live = a // fields < pc_ref[member]
                raw = raw * jnp.where(live, jnp.float32(1.0), jnp.float32(0.0))
        else:
            raw = (lat_ref if a == nfield else lon_ref)[...]
        X[a, pl.ds(TOP, height), pl.ds(0, breadth)] = raw
        tail = X[a, pl.ds(TOP, height), pl.ds(384, 128)]
        X[a, pl.ds(TOP, height), pl.ds(384, 128)] = jnp.where(lane < breadth - 384, tail, jnp.float32(0.0))
        X[a, pl.ds(0, TOP), :] = zero_rows
        X[a, pl.ds(TOP + height, rows - TOP - height), :] = zero_rows

    @pl.when(me_lat == nlat - 1)
    def _():
        last = TOP + height - 8
        cn[pl.ds(last, 8), :] = jnp.where(sub8 == 7, jnp.float32(0.0), cn[pl.ds(last, 8), :])

    pl_acc = jnp.zeros((height, 128), jnp.float32)
    pr_acc = jnp.zeros((height, 128), jnp.float32)
    for a in range(count):
        head = X[a, pl.ds(TOP, height), pl.ds(0, 128)]
        tail = X[a, pl.ds(TOP, height), pl.ds(384, 128)]
        pl_acc = jnp.where(quad == a, pltpu.roll(head, (HALO * a) % 128, 1), pl_acc)
        pr_acc = jnp.where(quad == a, pltpu.roll(tail, (HALO * a - (breadth - 384 - HALO)) % 128, 1), pr_acc)
    pack_l[...] = pl_acc
    pack_r[...] = pr_acc

    coef_lane = HALO * nfield
    width = 2 * HALO
    per_row = 128 // width
    half = height // 2
    lane_h = lax.broadcasted_iota(jnp.int32, (half, 128), 1)
    for src, dst in ((pl_acc, send_lb), (pr_acc, send_rb)):
        folded = jnp.where(lane_h < coef_lane, src[0:half], pltpu.roll(src[half:height], coef_lane, 1))
        dst[...] = folded.astype(jnp.bfloat16)
    for src, dst in ((pl_acc, send_lc), (pr_acc, send_rc)):
        for h in range(dst.shape[0] // STRIP):
            packed = jnp.zeros((STRIP, 128), jnp.float32)
            for g in range(per_row):
                i = h * per_row + g
                if i * STRIP >= height:
                    break
                blk = src[i * STRIP : (i + 1) * STRIP]
                packed = jnp.where(lane8 // width == g, pltpu.roll(blk, (width * g - coef_lane) % 128, 1), packed)
            dst[pl.ds(h * STRIP, STRIP), :] = packed

    def strip_pair(a, first, keep_low):
        lo = X[a, pl.ds(first, STRIP), :]
        hi = X[a + 1, pl.ds(first, STRIP), :]
        if keep_low:
            return jnp.where(sub8 < 4, lo, pltpu.roll(hi, 4, 0))
        return jnp.where(sub8 < 4, pltpu.roll(lo, 4, 0), hi)

    for dst_b, dst_c, first, keep_low in (
        (send_tb, send_tc, TOP, True),
        (send_bb, send_bc, TOP + height - STRIP, False),
    ):
        for j in range(dst_b.shape[0]):
            both = [strip_pair(4 * j, first, keep_low), strip_pair(4 * j + 2, first, keep_low)]
            dst_b[j] = jnp.concatenate(both, axis=0).astype(jnp.bfloat16)
        dst_c[...] = strip_pair(nfield, first, keep_low)

    pl.semaphore_wait(barrier, 3 + 3 * has_up.astype(jnp.int32) + 3 * has_down.astype(jnp.int32))

    last8 = pl.ds(height - STRIP, STRIP)
    first8 = pl.ds(0, STRIP)
    copies = [
        (send_rb, rlb, me_lat, right, None),
        (send_rc, rlc, me_lat, right, None),
        (send_lb, rrb, me_lat, left, None),
        (send_lc, rrc, me_lat, left, None),
        (send_tb, rbb, up, me_lon, "up"),
        (send_tc, rbc, up, me_lon, "up"),
        (send_bb, rab, down, me_lon, "down"),
        (send_bc, rac, down, me_lon, "down"),
        (pack_r.at[last8], rc.at[TL], down, right, "down"),
        (pack_l.at[last8], rc.at[TR], down, left, "down"),
        (pack_r.at[first8], rc.at[BL], up, right, "up"),
        (pack_l.at[first8], rc.at[BR], up, left, "up"),
    ]

    def descriptor(i):
        src, dst, lat_to, lon_to, _ = copies[i]
        return pltpu.make_async_remote_copy(
            src, dst, send_sem.at[i], recv_sem.at[i], device_id={"lat": lat_to, "lon": lon_to}, device_id_type=MESH
        )

    def when(cond, fn):
        if cond is None:
            fn()
        else:
            pl.when(has_up if cond == "up" else has_down)(fn)

    def finish(i):
        cond = copies[i][4]
        when(cond, lambda: descriptor(i).wait_send())
        mirror = {None: None, "up": "down", "down": "up"}[cond]
        when(mirror, lambda: descriptor(i).wait_recv())

    for i, copy in enumerate(copies):
        when(copy[4], lambda i=i: descriptor(i).start())

    for i in range(4):
        finish(i)
    east_gap = (lane >= breadth - 384) & (lane < breadth - 384 + HALO)
    west_gap = lane >= 128 - HALO
    unpacked = []
    for src_b, src_c in ((rlb, rlc), (rrb, rrc)):
        folded = src_b[...].astype(jnp.float32)
        fields_part = jnp.concatenate([folded, pltpu.roll(folded, 128 - coef_lane, 1)], axis=0)
        parts = []
        for i in range(height // STRIP):
            h, g = divmod(i, per_row)
            blk_c = pltpu.roll(src_c[pl.ds(h * STRIP, STRIP), :], (coef_lane - width * g) % 128, 1)
            blk_f = fields_part[i * STRIP : (i + 1) * STRIP]
            parts.append(jnp.where(lane8 < coef_lane, blk_f, blk_c))
        unpacked.append(jnp.concatenate(parts, axis=0))
    from_l, from_r = unpacked
    for a in range(count):
        east_shift = (breadth - 384 - HALO * a) % 128
        west_shift = (128 - HALO - HALO * a) % 128
        tail = X[a, pl.ds(TOP, height), pl.ds(384, 128)]
        tail = jnp.where(east_gap, pltpu.roll(from_r, east_shift, 1), tail)
        tail = jnp.where(west_gap, pltpu.roll(from_l, west_shift, 1), tail)
        X[a, pl.ds(TOP, height), pl.ds(384, 128)] = tail

    def derive(first, size):
        ca[pl.ds(first, size), :] = cn[pl.ds(first - 1, size), :]
        cw[pl.ds(first, size), :] = pltpu.roll(ce[pl.ds(first, size), :], 1, 1)
        cd[pl.ds(first, size), :] = 2.0 - (
            cn[pl.ds(first, size), :] + ca[pl.ds(first, size), :] + ce[pl.ds(first, size), :] + cw[pl.ds(first, size), :]
        )

    derive(8, rows - 16)
    acc[...] = jnp.zeros_like(acc)
    acc_bot[...] = jnp.zeros_like(acc_bot)
    acc_mid[...] = jnp.zeros_like(acc_mid)
    src_tiles[:, :, 0] = jnp.zeros((2, steps, STRIP, COLS), jnp.float32)

    def slot_places(s):
        slot = member * slots + s
        act = jnp.where(s < pc_ref[member], jnp.float32(1.0), jnp.float32(0.0))
        row_first = me_lat * height
        col_first = me_lon * breadth
        places = []
        for comp in range(2):
            cell = sc_ref[pl_ref[comp, slot]]
            r = lax.div(cell, nlon_cells)
            c = cell - r * nlon_cells
            rb = r - row_first + TOP
            d = c - col_first
            d = jnp.where(d < 0, d + nlon_cells, d)
            near = d < breadth + HALO
            wrap = d >= nlon_cells - HALO
            cb = jnp.where(near, d, d - nlon_cells + COLS)
            valid = (rb >= TOP - HALO) & (rb < TOP + height + HALO) & (near | wrap)
            hit = (sub8 == lax.rem(jnp.maximum(rb, 0), 8)) & (lane_w == cb)
            for t in range(steps):
                amp = wav_ref[t] * act if comp == 0 else res_ref[steps - 1 - t, slot]
                src_tiles[comp, t, 1] = jnp.where(hit, amp, jnp.float32(0.0))
            places.append((rb, valid))
        return act, places

    def run_blocks(s, t, block_list, act, places):
        bufs = [(X.at[s * fields + comp], X.at[s * fields + 2 + comp], work.at[s, comp]) for comp in range(2)]
        ei, ci, ni = t % 3, (t + 1) % 3, (t + 2) % 3
        for k in block_list:
            r0 = 8 * k
            dd = cd[pl.ds(r0, 8), :]
            nn = cn[pl.ds(r0, 8), :]
            aa = ca[pl.ds(r0, 8), :]
            ee = ce[pl.ds(r0, 8), :]
            ww = cw[pl.ds(r0, 8), :]
            outs = []
            for comp in range(2):
                rb, valid = places[comp]
                pick = (valid & (rb >= r0) & (rb < r0 + 8)).astype(jnp.int32)
                cur_ref, ear_ref, nxt_ref = bufs[comp][ci], bufs[comp][ei], bufs[comp][ni]
                cur = cur_ref[pl.ds(r0, 8), :]
                above = cur_ref[pl.ds(r0 - 1, 8), :]
                below = cur_ref[pl.ds(r0 + 1, 8), :]
                ear = ear_ref[pl.ds(r0, 8), :]
                west = pltpu.roll(cur, 1, 1)
                east = pltpu.roll(cur, COLS - 1, 1)
                nxt = dd * cur + nn * below + aa * above + ee * east + ww * west - ear
                nxt = nxt + src_tiles[comp, t, pick]
                nxt_ref[pl.ds(r0, 8), :] = nxt
                outs.append(nxt)
            if 2 <= k < blocks - 2:
                row = r0 - TOP
                if MID_FIRST <= row < MID_FIRST + acc_mid.shape[0]:
                    dst, row = acc_mid, row - MID_FIRST
                else:
                    dst, row = (acc, row) if row < MID_FIRST else (acc_bot, row - MID_FIRST - acc_mid.shape[0])
                dst[pl.ds(row, 8), :] += outs[0] * outs[1]

    def phase(ranges):
        def body(s, carry):
            act, places = slot_places(s)
            for t in range(steps):
                run_blocks(s, t, ranges(t), act, places)
            return carry

        lax.fori_loop(0, slots, body, 0)

    inner = lambda t: list(range(3 + t, blocks - 3 - t))
    phase(inner)

    mid_out = pltpu.make_async_remote_copy(
        acc_mid, pacc_mid, send_sem.at[len(copies) + 1], recv_sem.at[len(copies) + 1],
        device_id={"pair": partner}, device_id_type=MESH,
    )
    mid_out.start()

    for i in range(4, len(copies)):
        finish(i)

    @pl.when(jnp.logical_not(has_up))
    def _():
        rab[...] = jnp.zeros_like(rab)
        rac[...] = jnp.zeros_like(rac)
        rc[TL] = jnp.zeros((STRIP, 128), jnp.float32)
        rc[TR] = jnp.zeros((STRIP, 128), jnp.float32)

    @pl.when(jnp.logical_not(has_down))
    def _():
        rbb[...] = jnp.zeros_like(rbb)
        rbc[...] = jnp.zeros_like(rbc)
        rc[BL] = jnp.zeros((STRIP, 128), jnp.float32)
        rc[BR] = jnp.zeros((STRIP, 128), jnp.float32)

    east_c = (lane8 >= breadth - 384) & (lane8 < breadth - 384 + HALO)
    west_c = lane8 >= 128 - HALO
    for src_b, src_c, first, low_half, (c_east, c_west) in (
        (rab, rac, TOP - STRIP, False, (TR, TL)),
        (rbb, rbc, TOP + height, True, (BR, BL)),
    ):
        for a in range(count):
            b = a // 2
            if a < nfield:
                both = src_b[b // 2].astype(jnp.float32)
                blk = both[STRIP * (b % 2) : STRIP * (b % 2 + 1)]
            else:
                blk = src_c[...]
            even = a % 2 == 0
            if low_half:
                blk = blk if even else pltpu.roll(blk, 4, 0)
                blk = jnp.where(sub8 < 4, blk, jnp.float32(0.0))
                band = sub_c < 4
            else:
                blk = pltpu.roll(blk, 4, 0) if even else blk
                blk = jnp.where(sub8 >= 4, blk, jnp.float32(0.0))
                band = sub_c >= 4
            X[a, pl.ds(first, STRIP), :] = blk
            east_shift = (breadth - 384 - HALO * a) % 128
            west_shift = (128 - HALO - HALO * a) % 128
            tail = X[a, pl.ds(first, STRIP), pl.ds(384, 128)]
            tail = jnp.where(band & east_c, pltpu.roll(rc[c_east], east_shift, 1), tail)
            tail = jnp.where(band & west_c, pltpu.roll(rc[c_west], west_shift, 1), tail)
            X[a, pl.ds(first, STRIP), pl.ds(384, 128)] = tail

    derive(8, 24)
    derive(rows - 32, 24)

    def outer_top(t):
        return list(range(1, 3 + t)) if t < steps - 1 else list(range(2, 3 + t))

    def outer_bottom(t):
        return list(range(blocks - 3 - t, blocks - 1)) if t < steps - 1 else list(range(blocks - 3 - t, blocks - 2))

    def to_other(i, src, dst):
        return pltpu.make_async_remote_copy(
            src, dst, send_sem.at[len(copies) + i], recv_sem.at[len(copies) + i],
            device_id={"pair": partner}, device_id_type=MESH,
        )

    phase(outer_top)
    top_out = to_other(2, acc, pacc)
    top_out.start()
    phase(outer_bottom)
    bottom_out = to_other(3, acc_bot, pacc_bot)
    bottom_out.start()
    top_out.wait()
    bottom_out.wait()
    mid_out.wait()
    mids = acc_mid.shape[0]
    o_ref[pl.ds(0, MID_FIRST), :] = (acc[...] + pacc[...])[:, 0:breadth]
    o_ref[pl.ds(MID_FIRST, mids), :] = (acc_mid[...] + pacc_mid[...])[:, 0:breadth]
    o_ref[pl.ds(MID_FIRST + mids, height - MID_FIRST - mids), :] = (acc_bot[...] + pacc_bot[...])[:, 0:breadth]


def fused(wave_states, lat_faces, lon_faces, scalars, nlon_cells):
    slots, fields, height, breadth = wave_states.shape
    nfield = slots * fields
    count = nfield + 2
    rows = height + 2 * TOP
    smem = pl.BlockSpec(memory_space=pltpu.SMEM)
    vmem = pl.BlockSpec(memory_space=pltpu.VMEM)
    per_row = 128 // (2 * HALO)
    coef_rows = STRIP * ((height // STRIP + per_row - 1) // per_row)
    packed_b = pltpu.VMEM((height // 2, 128), jnp.bfloat16)
    packed_c = pltpu.VMEM((coef_rows, 128), jnp.float32)
    strip_b16 = pltpu.VMEM((nfield // 4, 2 * STRIP, COLS), jnp.bfloat16)
    strip_c = pltpu.VMEM((STRIP, COLS), jnp.float32)
    plane = pltpu.VMEM((rows, COLS), jnp.float32)
    return pl.pallas_call(
        functools.partial(fused_kernel, nlon_cells),
        out_shape=jax.ShapeDtypeStruct((height, breadth), jnp.float32),
        in_specs=[smem] * 5 + [pl.BlockSpec(memory_space=pl.ANY)] * 3,
        out_specs=vmem,
        scratch_shapes=[
            pltpu.VMEM(wave_states.shape, wave_states.dtype),
            pltpu.VMEM(lat_faces.shape, jnp.float32),
            pltpu.VMEM(lon_faces.shape, jnp.float32),
            pltpu.SemaphoreType.DMA((slots + 2,)),
            pltpu.VMEM((2, 4, 2, STRIP, COLS), jnp.float32),
            pltpu.VMEM((count, rows, COLS), jnp.float32),
            pltpu.VMEM((slots, 2, rows, COLS), jnp.float32),
            plane,
            plane,
            plane,
            pltpu.VMEM((MID_FIRST, COLS), jnp.float32),
            pltpu.VMEM((MID_FIRST, COLS), jnp.float32),
            pltpu.VMEM((height - 2 * MID_FIRST, COLS), jnp.float32),
            pltpu.VMEM((height - 2 * MID_FIRST, COLS), jnp.float32),
            pltpu.VMEM((MID_FIRST, COLS), jnp.float32),
            pltpu.VMEM((MID_FIRST, COLS), jnp.float32),
            pltpu.VMEM((height, 128), jnp.float32),
            pltpu.VMEM((height, 128), jnp.float32),
        ]
        + [packed_b, packed_b, packed_c, packed_c, strip_b16, strip_b16, strip_c, strip_c] * 2
        + [
            pltpu.VMEM((4, STRIP, 128), jnp.float32),
            pltpu.SemaphoreType.DMA((16,)),
            pltpu.SemaphoreType.DMA((16,)),
        ],
        compiler_params=pltpu.CompilerParams(collective_id=0, has_side_effects=True, vmem_limit_bytes=60 * 1024 * 1024),
    )(*scalars, wave_states, lat_faces, lon_faces)


def body(
    wave_states,
    pair_list,
    pair_counts,
    residuals,
    station_cell,
    source_wavelet,
    lat_faces,
    lon_faces,
):
    height, breadth = lat_faces.shape
    nlon_cells = breadth * lax.axis_size("lon")
    scalars = (pair_list.T, pair_counts, residuals.T, station_cell, source_wavelet)
    return fused(wave_states, lat_faces, lon_faces, scalars, nlon_cells)


def solution(mesh):
    in_specs = (
        P("pair", None, "lat", "lon"),
        P(),
        P(),
        P(),
        P(),
        P(),
        P("lat", "lon"),
        P("lat", "lon"),
    )
    out_specs = P("lat", "lon")
    return jax.shard_map(body, mesh=mesh, in_specs=in_specs, out_specs=out_specs, check_vma=False)
```

```python
import functools

import jax
import jax.numpy as jnp
from jax import lax
from jax.experimental import pallas as pl
from jax.experimental.pallas import tpu as pltpu
from jax.sharding import PartitionSpec as P

HALO = 4
TOP = 16
COLS = 512
STRIP = 8
MESH = pl.DeviceIdType.MESH
TL, TR, BL, BR = 0, 1, 2, 3
MID_FIRST = 32


def fused_kernel(
    nlon_cells,
    pl_ref, pc_ref, res_ref, sc_ref, wav_ref,
    f_hbm, lat_hbm, lon_hbm,
    o_ref,
    f_ref, lat_ref, lon_ref, in_sem, src_tiles,
    X, work, ca, cw, cd, acc, pacc, acc_mid, pacc_mid,
    pack_l, pack_r,
    send_lb, send_rb, send_lc, send_rc, send_tb, send_bb, send_tc, send_bc,
    rlb, rrb, rlc, rrc, rab, rbb, rac, rbc, rc,
    send_sem, recv_sem,
):
    slots, fields, height, breadth = f_ref.shape
    nfield = slots * fields
    count = nfield + 2
    rows = X.shape[1]
    blocks = rows // 8
    steps = wav_ref.shape[0]
    nlon = lax.axis_size("lon")
    nlat = lax.axis_size("lat")
    me_lat = lax.axis_index("lat")
    me_lon = lax.axis_index("lon")
    member = lax.axis_index("pair")
    partner = 1 - member
    right = lax.rem(me_lon + 1, nlon)
    left = lax.rem(me_lon + nlon - 1, nlon)
    has_up = me_lat > 0
    has_down = me_lat < nlat - 1
    up = jnp.maximum(me_lat - 1, 0)
    down = jnp.minimum(me_lat + 1, nlat - 1)
    cn = X.at[nfield]
    ce = X.at[nfield + 1]

    barrier = pltpu.get_barrier_semaphore()
    pl.semaphore_signal(barrier, 1, device_id={"pair": partner}, device_id_type=MESH)
    for lon_to in (left, right):
        pl.semaphore_signal(barrier, 1, device_id={"lon": lon_to}, device_id_type=MESH)

    @pl.when(has_up)
    def _():
        for lon_to in (me_lon, left, right):
            pl.semaphore_signal(barrier, 1, device_id={"lat": up, "lon": lon_to}, device_id_type=MESH)

    @pl.when(has_down)
    def _():
        for lon_to in (me_lon, left, right):
            pl.semaphore_signal(barrier, 1, device_id={"lat": down, "lon": lon_to}, device_id_type=MESH)

    loads = [pltpu.make_async_copy(f_hbm.at[i], f_ref.at[i], in_sem.at[i]) for i in range(slots)]
    loads.append(pltpu.make_async_copy(lat_hbm, lat_ref, in_sem.at[slots]))
    loads.append(pltpu.make_async_copy(lon_hbm, lon_ref, in_sem.at[slots + 1]))
    for copy in loads:
        copy.start()

    lane = lax.broadcasted_iota(jnp.int32, (height, 128), 1)
    quad = lane // HALO
    sub8 = lax.broadcasted_iota(jnp.int32, (STRIP, COLS), 0)
    lane8 = lax.broadcasted_iota(jnp.int32, (STRIP, 128), 1)
    sub_c = lax.broadcasted_iota(jnp.int32, (STRIP, 128), 0)
    lane_w = lax.broadcasted_iota(jnp.int32, (STRIP, COLS), 1)
    zero_rows = jnp.zeros((TOP, COLS), jnp.float32)

    for a in range(count):
        if a % fields == 0 and a < nfield:
            loads[a // fields].wait()
        if a == nfield:
            loads[slots].wait()
            loads[slots + 1].wait()
        if a < nfield:
            raw = f_ref[a // fields, a % fields].astype(jnp.float32)
            if a % 2 == 0:
                live = a // fields < pc_ref[member]
                raw = raw * jnp.where(live, jnp.float32(1.0), jnp.float32(0.0))
        else:
            raw = (lat_ref if a == nfield else lon_ref)[...]
        X[a, pl.ds(TOP, height), pl.ds(0, breadth)] = raw
        tail = X[a, pl.ds(TOP, height), pl.ds(384, 128)]
        X[a, pl.ds(TOP, height), pl.ds(384, 128)] = jnp.where(lane < breadth - 384, tail, jnp.float32(0.0))
        X[a, pl.ds(0, TOP), :] = zero_rows
        X[a, pl.ds(TOP + height, rows - TOP - height), :] = zero_rows

    @pl.when(me_lat == nlat - 1)
    def _():
        last = TOP + height - 8
        cn[pl.ds(last, 8), :] = jnp.where(sub8 == 7, jnp.float32(0.0), cn[pl.ds(last, 8), :])

    pl_acc = jnp.zeros((height, 128), jnp.float32)
    pr_acc = jnp.zeros((height, 128), jnp.float32)
    for a in range(count):
        head = X[a, pl.ds(TOP, height), pl.ds(0, 128)]
        tail = X[a, pl.ds(TOP, height), pl.ds(384, 128)]
        pl_acc = jnp.where(quad == a, pltpu.roll(head, (HALO * a) % 128, 1), pl_acc)
        pr_acc = jnp.where(quad == a, pltpu.roll(tail, (HALO * a - (breadth - 384 - HALO)) % 128, 1), pr_acc)
    pack_l[...] = pl_acc
    pack_r[...] = pr_acc

    coef_lane = HALO * nfield
    width = 2 * HALO
    per_row = 128 // width
    half = height // 2
    lane_h = lax.broadcasted_iota(jnp.int32, (half, 128), 1)
    for src, dst in ((pl_acc, send_lb), (pr_acc, send_rb)):
        folded = jnp.where(lane_h < coef_lane, src[0:half], pltpu.roll(src[half:height], coef_lane, 1))
        dst[...] = folded.astype(jnp.bfloat16)
    for src, dst in ((pl_acc, send_lc), (pr_acc, send_rc)):
        for h in range(dst.shape[0] // STRIP):
            packed = jnp.zeros((STRIP, 128), jnp.float32)
            for g in range(per_row):
                i = h * per_row + g
                if i * STRIP >= height:
                    break
                blk = src[i * STRIP : (i + 1) * STRIP]
                packed = jnp.where(lane8 // width == g, pltpu.roll(blk, (width * g - coef_lane) % 128, 1), packed)
            dst[pl.ds(h * STRIP, STRIP), :] = packed

    def strip_pair(a, first, keep_low):
        lo = X[a, pl.ds(first, STRIP), :]
        hi = X[a + 1, pl.ds(first, STRIP), :]
        if keep_low:
            return jnp.where(sub8 < 4, lo, pltpu.roll(hi, 4, 0))
        return jnp.where(sub8 < 4, pltpu.roll(lo, 4, 0), hi)

    for dst_b, dst_c, first, keep_low in (
        (send_tb, send_tc, TOP, True),
        (send_bb, send_bc, TOP + height - STRIP, False),
    ):
        for j in range(dst_b.shape[0]):
            both = [strip_pair(4 * j, first, keep_low), strip_pair(4 * j + 2, first, keep_low)]
            dst_b[j] = jnp.concatenate(both, axis=0).astype(jnp.bfloat16)
        dst_c[...] = strip_pair(nfield, first, keep_low)

    pl.semaphore_wait(barrier, 3 + 3 * has_up.astype(jnp.int32) + 3 * has_down.astype(jnp.int32))

    last8 = pl.ds(height - STRIP, STRIP)
    first8 = pl.ds(0, STRIP)
    copies = [
        (send_rb, rlb, me_lat, right, None),
        (send_rc, rlc, me_lat, right, None),
        (send_lb, rrb, me_lat, left, None),
        (send_lc, rrc, me_lat, left, None),
        (send_tb, rbb, up, me_lon, "up"),
        (send_tc, rbc, up, me_lon, "up"),
        (send_bb, rab, down, me_lon, "down"),
        (send_bc, rac, down, me_lon, "down"),
        (pack_r.at[last8], rc.at[TL], down, right, "down"),
        (pack_l.at[last8], rc.at[TR], down, left, "down"),
        (pack_r.at[first8], rc.at[BL], up, right, "up"),
        (pack_l.at[first8], rc.at[BR], up, left, "up"),
    ]

    def descriptor(i):
        src, dst, lat_to, lon_to, _ = copies[i]
        return pltpu.make_async_remote_copy(
            src, dst, send_sem.at[i], recv_sem.at[i], device_id={"lat": lat_to, "lon": lon_to}, device_id_type=MESH
        )

    def when(cond, fn):
        if cond is None:
            fn()
        else:
            pl.when(has_up if cond == "up" else has_down)(fn)

    def finish(i):
        cond = copies[i][4]
        when(cond, lambda: descriptor(i).wait_send())
        mirror = {None: None, "up": "down", "down": "up"}[cond]
        when(mirror, lambda: descriptor(i).wait_recv())

    for i, copy in enumerate(copies):
        when(copy[4], lambda i=i: descriptor(i).start())

    for i in range(4):
        finish(i)
    east_gap = (lane >= breadth - 384) & (lane < breadth - 384 + HALO)
    west_gap = lane >= 128 - HALO
    unpacked = []
    for src_b, src_c in ((rlb, rlc), (rrb, rrc)):
        folded = src_b[...].astype(jnp.float32)
        fields_part = jnp.concatenate([folded, pltpu.roll(folded, 128 - coef_lane, 1)], axis=0)
        parts = []
        for i in range(height // STRIP):
            h, g = divmod(i, per_row)
            blk_c = pltpu.roll(src_c[pl.ds(h * STRIP, STRIP), :], (coef_lane - width * g) % 128, 1)
            blk_f = fields_part[i * STRIP : (i + 1) * STRIP]
            parts.append(jnp.where(lane8 < coef_lane, blk_f, blk_c))
        unpacked.append(jnp.concatenate(parts, axis=0))
    from_l, from_r = unpacked
    for a in range(count):
        east_shift = (breadth - 384 - HALO * a) % 128
        west_shift = (128 - HALO - HALO * a) % 128
        tail = X[a, pl.ds(TOP, height), pl.ds(384, 128)]
        tail = jnp.where(east_gap, pltpu.roll(from_r, east_shift, 1), tail)
        tail = jnp.where(west_gap, pltpu.roll(from_l, west_shift, 1), tail)
        X[a, pl.ds(TOP, height), pl.ds(384, 128)] = tail

    def derive(first, size):
        ca[pl.ds(first, size), :] = cn[pl.ds(first - 1, size), :]
        cw[pl.ds(first, size), :] = pltpu.roll(ce[pl.ds(first, size), :], 1, 1)
        cd[pl.ds(first, size), :] = 2.0 - (
            cn[pl.ds(first, size), :] + ca[pl.ds(first, size), :] + ce[pl.ds(first, size), :] + cw[pl.ds(first, size), :]
        )

    derive(8, rows - 16)
    acc[...] = jnp.zeros_like(acc)
    acc_mid[...] = jnp.zeros_like(acc_mid)
    src_tiles[:, :, 0] = jnp.zeros((2, steps, STRIP, COLS), jnp.float32)

    def slot_places(s):
        slot = member * slots + s
        act = jnp.where(s < pc_ref[member], jnp.float32(1.0), jnp.float32(0.0))
        row_first = me_lat * height
        col_first = me_lon * breadth
        places = []
        for comp in range(2):
            cell = sc_ref[pl_ref[comp, slot]]
            r = lax.div(cell, nlon_cells)
            c = cell - r * nlon_cells
            rb = r - row_first + TOP
            d = c - col_first
            d = jnp.where(d < 0, d + nlon_cells, d)
            near = d < breadth + HALO
            wrap = d >= nlon_cells - HALO
            cb = jnp.where(near, d, d - nlon_cells + COLS)
            valid = (rb >= TOP - HALO) & (rb < TOP + height + HALO) & (near | wrap)
            hit = (sub8 == lax.rem(jnp.maximum(rb, 0), 8)) & (lane_w == cb)
            for t in range(steps):
                amp = wav_ref[t] * act if comp == 0 else res_ref[steps - 1 - t, slot]
                src_tiles[comp, t, 1] = jnp.where(hit, amp, jnp.float32(0.0))
            places.append((rb, valid))
        return act, places

    def run_blocks(s, t, block_list, act, places):
        bufs = [(X.at[s * fields + comp], X.at[s * fields + 2 + comp], work.at[s, comp]) for comp in range(2)]
        ei, ci, ni = t % 3, (t + 1) % 3, (t + 2) % 3
        for k in block_list:
            r0 = 8 * k
            dd = cd[pl.ds(r0, 8), :]
            nn = cn[pl.ds(r0, 8), :]
            aa = ca[pl.ds(r0, 8), :]
            ee = ce[pl.ds(r0, 8), :]
            ww = cw[pl.ds(r0, 8), :]
            outs = []
            for comp in range(2):
                rb, valid = places[comp]
                pick = (valid & (rb >= r0) & (rb < r0 + 8)).astype(jnp.int32)
                cur_ref, ear_ref, nxt_ref = bufs[comp][ci], bufs[comp][ei], bufs[comp][ni]
                cur = cur_ref[pl.ds(r0, 8), :]
                above = cur_ref[pl.ds(r0 - 1, 8), :]
                below = cur_ref[pl.ds(r0 + 1, 8), :]
                ear = ear_ref[pl.ds(r0, 8), :]
                west = pltpu.roll(cur, 1, 1)
                east = pltpu.roll(cur, COLS - 1, 1)
                nxt = dd * cur + nn * below + aa * above + ee * east + ww * west - ear
                nxt = nxt + src_tiles[comp, t, pick]
                nxt_ref[pl.ds(r0, 8), :] = nxt
                outs.append(nxt)
            if 2 <= k < blocks - 2:
                row = r0 - TOP
                if MID_FIRST <= row < MID_FIRST + acc_mid.shape[0]:
                    dst, row = acc_mid, row - MID_FIRST
                else:
                    dst, row = acc, (row if row < MID_FIRST else row - acc_mid.shape[0])
                dst[pl.ds(row, 8), :] += outs[0] * outs[1]

    def phase(ranges):
        def body(s, carry):
            act, places = slot_places(s)
            for t in range(steps):
                run_blocks(s, t, ranges(t), act, places)
            return carry

        lax.fori_loop(0, slots, body, 0, unroll=True)

    inner = lambda t: list(range(3 + t, blocks - 3 - t))
    phase(inner)

    mid_out = pltpu.make_async_remote_copy(
        acc_mid, pacc_mid, send_sem.at[len(copies) + 1], recv_sem.at[len(copies) + 1],
        device_id={"pair": partner}, device_id_type=MESH,
    )
    mid_out.start()

    for i in range(4, len(copies)):
        finish(i)

    @pl.when(jnp.logical_not(has_up))
    def _():
        rab[...] = jnp.zeros_like(rab)
        rac[...] = jnp.zeros_like(rac)
        rc[TL] = jnp.zeros((STRIP, 128), jnp.float32)
        rc[TR] = jnp.zeros((STRIP, 128), jnp.float32)

    @pl.when(jnp.logical_not(has_down))
    def _():
        rbb[...] = jnp.zeros_like(rbb)
        rbc[...] = jnp.zeros_like(rbc)
        rc[BL] = jnp.zeros((STRIP, 128), jnp.float32)
        rc[BR] = jnp.zeros((STRIP, 128), jnp.float32)

    east_c = (lane8 >= breadth - 384) & (lane8 < breadth - 384 + HALO)
    west_c = lane8 >= 128 - HALO
    for src_b, src_c, first, low_half, (c_east, c_west) in (
        (rab, rac, TOP - STRIP, False, (TR, TL)),
        (rbb, rbc, TOP + height, True, (BR, BL)),
    ):
        for a in range(count):
            b = a // 2
            if a < nfield:
                both = src_b[b // 2].astype(jnp.float32)
                blk = both[STRIP * (b % 2) : STRIP * (b % 2 + 1)]
            else:
                blk = src_c[...]
            even = a % 2 == 0
            if low_half:
                blk = blk if even else pltpu.roll(blk, 4, 0)
                blk = jnp.where(sub8 < 4, blk, jnp.float32(0.0))
                band = sub_c < 4
            else:
                blk = pltpu.roll(blk, 4, 0) if even else blk
                blk = jnp.where(sub8 >= 4, blk, jnp.float32(0.0))
                band = sub_c >= 4
            X[a, pl.ds(first, STRIP), :] = blk
            east_shift = (breadth - 384 - HALO * a) % 128
            west_shift = (128 - HALO - HALO * a) % 128
            tail = X[a, pl.ds(first, STRIP), pl.ds(384, 128)]
            tail = jnp.where(band & east_c, pltpu.roll(rc[c_east], east_shift, 1), tail)
            tail = jnp.where(band & west_c, pltpu.roll(rc[c_west], west_shift, 1), tail)
            X[a, pl.ds(first, STRIP), pl.ds(384, 128)] = tail

    derive(8, 24)
    derive(rows - 32, 24)

    def outer(t):
        if t < steps - 1:
            return list(range(1, 3 + t)) + list(range(blocks - 3 - t, blocks - 1))
        return list(range(2, 3 + t)) + list(range(blocks - 3 - t, blocks - 2))

    phase(outer)

    to_partner = pltpu.make_async_remote_copy(
        acc, pacc, send_sem.at[len(copies)], recv_sem.at[len(copies)], device_id={"pair": partner}, device_id_type=MESH
    )
    to_partner.start()
    to_partner.wait()
    mid_out.wait()
    edge = acc[...] + pacc[...]
    mids = acc_mid.shape[0]
    o_ref[pl.ds(0, MID_FIRST), :] = edge[0:MID_FIRST, 0:breadth]
    o_ref[pl.ds(MID_FIRST, mids), :] = (acc_mid[...] + pacc_mid[...])[:, 0:breadth]
    o_ref[pl.ds(MID_FIRST + mids, height - MID_FIRST - mids), :] = edge[MID_FIRST:, 0:breadth]


def fused(wave_states, lat_faces, lon_faces, scalars, nlon_cells):
    slots, fields, height, breadth = wave_states.shape
    nfield = slots * fields
    count = nfield + 2
    rows = height + 2 * TOP
    smem = pl.BlockSpec(memory_space=pltpu.SMEM)
    vmem = pl.BlockSpec(memory_space=pltpu.VMEM)
    per_row = 128 // (2 * HALO)
    coef_rows = STRIP * ((height // STRIP + per_row - 1) // per_row)
    packed_b = pltpu.VMEM((height // 2, 128), jnp.bfloat16)
    packed_c = pltpu.VMEM((coef_rows, 128), jnp.float32)
    strip_b16 = pltpu.VMEM((nfield // 4, 2 * STRIP, COLS), jnp.bfloat16)
    strip_c = pltpu.VMEM((STRIP, COLS), jnp.float32)
    plane = pltpu.VMEM((rows, COLS), jnp.float32)
    return pl.pallas_call(
        functools.partial(fused_kernel, nlon_cells),
        out_shape=jax.ShapeDtypeStruct((height, breadth), jnp.float32),
        in_specs=[smem] * 5 + [pl.BlockSpec(memory_space=pl.ANY)] * 3,
        out_specs=vmem,
        scratch_shapes=[
            pltpu.VMEM(wave_states.shape, wave_states.dtype),
            pltpu.VMEM(lat_faces.shape, jnp.float32),
            pltpu.VMEM(lon_faces.shape, jnp.float32),
            pltpu.SemaphoreType.DMA((slots + 2,)),
            pltpu.VMEM((2, 4, 2, STRIP, COLS), jnp.float32),
            pltpu.VMEM((count, rows, COLS), jnp.float32),
            pltpu.VMEM((slots, 2, rows, COLS), jnp.float32),
            plane,
            plane,
            plane,
            pltpu.VMEM((2 * MID_FIRST, COLS), jnp.float32),
            pltpu.VMEM((2 * MID_FIRST, COLS), jnp.float32),
            pltpu.VMEM((height - 2 * MID_FIRST, COLS), jnp.float32),
            pltpu.VMEM((height - 2 * MID_FIRST, COLS), jnp.float32),
            pltpu.VMEM((height, 128), jnp.float32),
            pltpu.VMEM((height, 128), jnp.float32),
        ]
        + [packed_b, packed_b, packed_c, packed_c, strip_b16, strip_b16, strip_c, strip_c] * 2
        + [
            pltpu.VMEM((4, STRIP, 128), jnp.float32),
            pltpu.SemaphoreType.DMA((14,)),
            pltpu.SemaphoreType.DMA((14,)),
        ],
        compiler_params=pltpu.CompilerParams(collective_id=0, has_side_effects=True, vmem_limit_bytes=60 * 1024 * 1024),
    )(*scalars, wave_states, lat_faces, lon_faces)


def body(
    wave_states,
    pair_list,
    pair_counts,
    residuals,
    station_cell,
    source_wavelet,
    lat_faces,
    lon_faces,
):
    height, breadth = lat_faces.shape
    nlon_cells = breadth * lax.axis_size("lon")
    scalars = (pair_list.T, pair_counts, residuals.T, station_cell, source_wavelet)
    return fused(wave_states, lat_faces, lon_faces, scalars, nlon_cells)


def solution(mesh):
    in_specs = (
        P("pair", None, "lat", "lon"),
        P(),
        P(),
        P(),
        P(),
        P(),
        P("lat", "lon"),
        P("lat", "lon"),
    )
    out_specs = P("lat", "lon")
    return jax.shard_map(body, mesh=mesh, in_specs=in_specs, out_specs=out_specs, check_vma=False)
```

```python
import functools

import jax
import jax.numpy as jnp
from jax import lax
from jax.experimental import pallas as pl
from jax.experimental.pallas import tpu as pltpu
from jax.sharding import PartitionSpec as P

HALO = 4
TOP = 16
COLS = 512
STRIP = 8
MESH = pl.DeviceIdType.MESH
TL, TR, BL, BR = 0, 1, 2, 3
MID_FIRST = 32


def fused_kernel(
    nlon_cells,
    pl_ref, pc_ref, res_ref, sc_ref, wav_ref,
    f_hbm, lat_hbm, lon_hbm,
    o_ref,
    f_ref, lat_ref, lon_ref, in_sem, src_tiles,
    X, work, ca, cw, cd, acc, pacc, acc_mid, pacc_mid,
    pack_l, pack_r,
    send_lb, send_rb, send_lc, send_rc, send_tb, send_bb, send_tc, send_bc,
    rlb, rrb, rlc, rrc, rab, rbb, rac, rbc, rc,
    send_sem, recv_sem,
):
    slots, fields, height, breadth = f_ref.shape
    nfield = slots * fields
    count = nfield + 2
    rows = X.shape[1]
    blocks = rows // 8
    steps = wav_ref.shape[0]
    nlon = lax.axis_size("lon")
    nlat = lax.axis_size("lat")
    me_lat = lax.axis_index("lat")
    me_lon = lax.axis_index("lon")
    member = lax.axis_index("pair")
    partner = 1 - member
    right = lax.rem(me_lon + 1, nlon)
    left = lax.rem(me_lon + nlon - 1, nlon)
    has_up = me_lat > 0
    has_down = me_lat < nlat - 1
    up = jnp.maximum(me_lat - 1, 0)
    down = jnp.minimum(me_lat + 1, nlat - 1)
    cn = X.at[nfield]
    ce = X.at[nfield + 1]

    barrier = pltpu.get_barrier_semaphore()
    pl.semaphore_signal(barrier, 1, device_id={"pair": partner}, device_id_type=MESH)
    for lon_to in (left, right):
        pl.semaphore_signal(barrier, 1, device_id={"lon": lon_to}, device_id_type=MESH)

    @pl.when(has_up)
    def _():
        for lon_to in (me_lon, left, right):
            pl.semaphore_signal(barrier, 1, device_id={"lat": up, "lon": lon_to}, device_id_type=MESH)

    @pl.when(has_down)
    def _():
        for lon_to in (me_lon, left, right):
            pl.semaphore_signal(barrier, 1, device_id={"lat": down, "lon": lon_to}, device_id_type=MESH)

    loads = [pltpu.make_async_copy(f_hbm.at[i], f_ref.at[i], in_sem.at[i]) for i in range(slots)]
    loads.append(pltpu.make_async_copy(lat_hbm, lat_ref, in_sem.at[slots]))
    loads.append(pltpu.make_async_copy(lon_hbm, lon_ref, in_sem.at[slots + 1]))
    for copy in loads:
        copy.start()

    lane = lax.broadcasted_iota(jnp.int32, (height, 128), 1)
    quad = lane // HALO
    sub8 = lax.broadcasted_iota(jnp.int32, (STRIP, COLS), 0)
    lane8 = lax.broadcasted_iota(jnp.int32, (STRIP, 128), 1)
    sub_c = lax.broadcasted_iota(jnp.int32, (STRIP, 128), 0)
    lane_w = lax.broadcasted_iota(jnp.int32, (STRIP, COLS), 1)
    zero_rows = jnp.zeros((TOP, COLS), jnp.float32)

    for a in range(count):
        if a % fields == 0 and a < nfield:
            loads[a // fields].wait()
        if a == nfield:
            loads[slots].wait()
            loads[slots + 1].wait()
        if a < nfield:
            raw = f_ref[a // fields, a % fields].astype(jnp.float32)
            if a % 2 == 0:
                live = a // fields < pc_ref[member]
                raw = raw * jnp.where(live, jnp.float32(1.0), jnp.float32(0.0))
        else:
            raw = (lat_ref if a == nfield else lon_ref)[...]
        X[a, pl.ds(TOP, height), pl.ds(0, breadth)] = raw
        tail = X[a, pl.ds(TOP, height), pl.ds(384, 128)]
        X[a, pl.ds(TOP, height), pl.ds(384, 128)] = jnp.where(lane < breadth - 384, tail, jnp.float32(0.0))
        X[a, pl.ds(0, TOP), :] = zero_rows
        X[a, pl.ds(TOP + height, rows - TOP - height), :] = zero_rows

    @pl.when(me_lat == nlat - 1)
    def _():
        last = TOP + height - 8
        cn[pl.ds(last, 8), :] = jnp.where(sub8 == 7, jnp.float32(0.0), cn[pl.ds(last, 8), :])

    pl_acc = jnp.zeros((height, 128), jnp.float32)
    pr_acc = jnp.zeros((height, 128), jnp.float32)
    for a in range(count):
        head = X[a, pl.ds(TOP, height), pl.ds(0, 128)]
        tail = X[a, pl.ds(TOP, height), pl.ds(384, 128)]
        pl_acc = jnp.where(quad == a, pltpu.roll(head, (HALO * a) % 128, 1), pl_acc)
        pr_acc = jnp.where(quad == a, pltpu.roll(tail, (HALO * a - (breadth - 384 - HALO)) % 128, 1), pr_acc)
    pack_l[...] = pl_acc
    pack_r[...] = pr_acc

    coef_lane = HALO * nfield
    width = 2 * HALO
    per_row = 128 // width
    half = height // 2
    lane_h = lax.broadcasted_iota(jnp.int32, (half, 128), 1)
    for src, dst in ((pl_acc, send_lb), (pr_acc, send_rb)):
        folded = jnp.where(lane_h < coef_lane, src[0:half], pltpu.roll(src[half:height], coef_lane, 1))
        dst[...] = folded.astype(jnp.bfloat16)
    for src, dst in ((pl_acc, send_lc), (pr_acc, send_rc)):
        for h in range(dst.shape[0] // STRIP):
            packed = jnp.zeros((STRIP, 128), jnp.float32)
            for g in range(per_row):
                i = h * per_row + g
                if i * STRIP >= height:
                    break
                blk = src[i * STRIP : (i + 1) * STRIP]
                packed = jnp.where(lane8 // width == g, pltpu.roll(blk, (width * g - coef_lane) % 128, 1), packed)
            dst[pl.ds(h * STRIP, STRIP), :] = packed

    def strip_pair(a, first, keep_low):
        lo = X[a, pl.ds(first, STRIP), :]
        hi = X[a + 1, pl.ds(first, STRIP), :]
        if keep_low:
            return jnp.where(sub8 < 4, lo, pltpu.roll(hi, 4, 0))
        return jnp.where(sub8 < 4, pltpu.roll(lo, 4, 0), hi)

    for dst_b, dst_c, first, keep_low in (
        (send_tb, send_tc, TOP, True),
        (send_bb, send_bc, TOP + height - STRIP, False),
    ):
        for j in range(dst_b.shape[0]):
            both = [strip_pair(4 * j, first, keep_low), strip_pair(4 * j + 2, first, keep_low)]
            dst_b[j] = jnp.concatenate(both, axis=0).astype(jnp.bfloat16)
        dst_c[...] = strip_pair(nfield, first, keep_low)

    acc[...] = jnp.zeros_like(acc)
    acc_mid[...] = jnp.zeros_like(acc_mid)
    src_tiles[:, :, 0] = jnp.zeros((2, steps, STRIP, COLS), jnp.float32)

    pl.semaphore_wait(barrier, 3 + 3 * has_up.astype(jnp.int32) + 3 * has_down.astype(jnp.int32))

    last8 = pl.ds(height - STRIP, STRIP)
    first8 = pl.ds(0, STRIP)
    copies = [
        (send_rb, rlb, me_lat, right, None),
        (send_rc, rlc, me_lat, right, None),
        (send_lb, rrb, me_lat, left, None),
        (send_lc, rrc, me_lat, left, None),
        (send_tb, rbb, up, me_lon, "up"),
        (send_tc, rbc, up, me_lon, "up"),
        (send_bb, rab, down, me_lon, "down"),
        (send_bc, rac, down, me_lon, "down"),
        (pack_r.at[last8], rc.at[TL], down, right, "down"),
        (pack_l.at[last8], rc.at[TR], down, left, "down"),
        (pack_r.at[first8], rc.at[BL], up, right, "up"),
        (pack_l.at[first8], rc.at[BR], up, left, "up"),
    ]

    def descriptor(i):
        src, dst, lat_to, lon_to, _ = copies[i]
        return pltpu.make_async_remote_copy(
            src, dst, send_sem.at[i], recv_sem.at[i], device_id={"lat": lat_to, "lon": lon_to}, device_id_type=MESH
        )

    def when(cond, fn):
        if cond is None:
            fn()
        else:
            pl.when(has_up if cond == "up" else has_down)(fn)

    def finish(i):
        cond = copies[i][4]
        when(cond, lambda: descriptor(i).wait_send())
        mirror = {None: None, "up": "down", "down": "up"}[cond]
        when(mirror, lambda: descriptor(i).wait_recv())

    for i, copy in enumerate(copies):
        when(copy[4], lambda i=i: descriptor(i).start())

    for i in range(4):
        finish(i)
    east_gap = (lane >= breadth - 384) & (lane < breadth - 384 + HALO)
    west_gap = lane >= 128 - HALO
    unpacked = []
    for src_b, src_c in ((rlb, rlc), (rrb, rrc)):
        folded = src_b[...].astype(jnp.float32)
        fields_part = jnp.concatenate([folded, pltpu.roll(folded, 128 - coef_lane, 1)], axis=0)
        parts = []
        for i in range(height // STRIP):
            h, g = divmod(i, per_row)
            blk_c = pltpu.roll(src_c[pl.ds(h * STRIP, STRIP), :], (coef_lane - width * g) % 128, 1)
            blk_f = fields_part[i * STRIP : (i + 1) * STRIP]
            parts.append(jnp.where(lane8 < coef_lane, blk_f, blk_c))
        unpacked.append(jnp.concatenate(parts, axis=0))
    from_l, from_r = unpacked
    for a in range(count):
        east_shift = (breadth - 384 - HALO * a) % 128
        west_shift = (128 - HALO - HALO * a) % 128
        tail = X[a, pl.ds(TOP, height), pl.ds(384, 128)]
        tail = jnp.where(east_gap, pltpu.roll(from_r, east_shift, 1), tail)
        tail = jnp.where(west_gap, pltpu.roll(from_l, west_shift, 1), tail)
        X[a, pl.ds(TOP, height), pl.ds(384, 128)] = tail

    def derive(first, size):
        ca[pl.ds(first, size), :] = cn[pl.ds(first - 1, size), :]
        cw[pl.ds(first, size), :] = pltpu.roll(ce[pl.ds(first, size), :], 1, 1)
        cd[pl.ds(first, size), :] = 2.0 - (
            cn[pl.ds(first, size), :] + ca[pl.ds(first, size), :] + ce[pl.ds(first, size), :] + cw[pl.ds(first, size), :]
        )

    derive(8, rows - 16)

    def slot_places(s):
        slot = member * slots + s
        act = jnp.where(s < pc_ref[member], jnp.float32(1.0), jnp.float32(0.0))
        row_first = me_lat * height
        col_first = me_lon * breadth
        places = []
        for comp in range(2):
            cell = sc_ref[pl_ref[comp, slot]]
            r = lax.div(cell, nlon_cells)
            c = cell - r * nlon_cells
            rb = r - row_first + TOP
            d = c - col_first
            d = jnp.where(d < 0, d + nlon_cells, d)
            near = d < breadth + HALO
            wrap = d >= nlon_cells - HALO
            cb = jnp.where(near, d, d - nlon_cells + COLS)
            valid = (rb >= TOP - HALO) & (rb < TOP + height + HALO) & (near | wrap)
            hit = (sub8 == lax.rem(jnp.maximum(rb, 0), 8)) & (lane_w == cb)
            for t in range(steps):
                amp = wav_ref[t] * act if comp == 0 else res_ref[steps - 1 - t, slot]
                src_tiles[comp, t, 1] = jnp.where(hit, amp, jnp.float32(0.0))
            places.append((rb, valid))
        return act, places

    def run_blocks(s, t, block_list, act, places):
        bufs = [(X.at[s * fields + comp], X.at[s * fields + 2 + comp], work.at[s, comp]) for comp in range(2)]
        ei, ci, ni = t % 3, (t + 1) % 3, (t + 2) % 3
        for k in block_list:
            r0 = 8 * k
            dd = cd[pl.ds(r0, 8), :]
            nn = cn[pl.ds(r0, 8), :]
            aa = ca[pl.ds(r0, 8), :]
            ee = ce[pl.ds(r0, 8), :]
            ww = cw[pl.ds(r0, 8), :]
            outs = []
            for comp in range(2):
                rb, valid = places[comp]
                pick = (valid & (rb >= r0) & (rb < r0 + 8)).astype(jnp.int32)
                cur_ref, ear_ref, nxt_ref = bufs[comp][ci], bufs[comp][ei], bufs[comp][ni]
                cur = cur_ref[pl.ds(r0, 8), :]
                above = cur_ref[pl.ds(r0 - 1, 8), :]
                below = cur_ref[pl.ds(r0 + 1, 8), :]
                ear = ear_ref[pl.ds(r0, 8), :]
                west = pltpu.roll(cur, 1, 1)
                east = pltpu.roll(cur, COLS - 1, 1)
                nxt = dd * cur + nn * below + aa * above + ee * east + ww * west - ear
                nxt = nxt + src_tiles[comp, t, pick]
                nxt_ref[pl.ds(r0, 8), :] = nxt
                outs.append(nxt)
            if 2 <= k < blocks - 2:
                row = r0 - TOP
                if MID_FIRST <= row < MID_FIRST + acc_mid.shape[0]:
                    dst, row = acc_mid, row - MID_FIRST
                else:
                    dst, row = acc, (row if row < MID_FIRST else row - acc_mid.shape[0])
                dst[pl.ds(row, 8), :] += outs[0] * outs[1]

    def phase(ranges):
        def body(s, carry):
            act, places = slot_places(s)
            for t in range(steps):
                run_blocks(s, t, ranges(t), act, places)
            return carry

        lax.fori_loop(0, slots, body, 0)

    inner = lambda t: list(range(3 + t, blocks - 3 - t))
    phase(inner)

    mid_out = pltpu.make_async_remote_copy(
        acc_mid, pacc_mid, send_sem.at[len(copies) + 1], recv_sem.at[len(copies) + 1],
        device_id={"pair": partner}, device_id_type=MESH,
    )
    mid_out.start()

    for i in range(4, len(copies)):
        finish(i)

    @pl.when(jnp.logical_not(has_up))
    def _():
        rab[...] = jnp.zeros_like(rab)
        rac[...] = jnp.zeros_like(rac)
        rc[TL] = jnp.zeros((STRIP, 128), jnp.float32)
        rc[TR] = jnp.zeros((STRIP, 128), jnp.float32)

    @pl.when(jnp.logical_not(has_down))
    def _():
        rbb[...] = jnp.zeros_like(rbb)
        rbc[...] = jnp.zeros_like(rbc)
        rc[BL] = jnp.zeros((STRIP, 128), jnp.float32)
        rc[BR] = jnp.zeros((STRIP, 128), jnp.float32)

    east_c = (lane8 >= breadth - 384) & (lane8 < breadth - 384 + HALO)
    west_c = lane8 >= 128 - HALO
    for src_b, src_c, first, low_half, (c_east, c_west) in (
        (rab, rac, TOP - STRIP, False, (TR, TL)),
        (rbb, rbc, TOP + height, True, (BR, BL)),
    ):
        for a in range(count):
            b = a // 2
            if a < nfield:
                both = src_b[b // 2].astype(jnp.float32)
                blk = both[STRIP * (b % 2) : STRIP * (b % 2 + 1)]
            else:
                blk = src_c[...]
            even = a % 2 == 0
            if low_half:
                blk = blk if even else pltpu.roll(blk, 4, 0)
                blk = jnp.where(sub8 < 4, blk, jnp.float32(0.0))
                band = sub_c < 4
            else:
                blk = pltpu.roll(blk, 4, 0) if even else blk
                blk = jnp.where(sub8 >= 4, blk, jnp.float32(0.0))
                band = sub_c >= 4
            X[a, pl.ds(first, STRIP), :] = blk
            east_shift = (breadth - 384 - HALO * a) % 128
            west_shift = (128 - HALO - HALO * a) % 128
            tail = X[a, pl.ds(first, STRIP), pl.ds(384, 128)]
            tail = jnp.where(band & east_c, pltpu.roll(rc[c_east], east_shift, 1), tail)
            tail = jnp.where(band & west_c, pltpu.roll(rc[c_west], west_shift, 1), tail)
            X[a, pl.ds(first, STRIP), pl.ds(384, 128)] = tail

    derive(8, 24)
    derive(rows - 32, 24)

    def outer(t):
        if t < steps - 1:
            return list(range(1, 3 + t)) + list(range(blocks - 3 - t, blocks - 1))
        return list(range(2, 3 + t)) + list(range(blocks - 3 - t, blocks - 2))

    phase(outer)

    to_partner = pltpu.make_async_remote_copy(
        acc, pacc, send_sem.at[len(copies)], recv_sem.at[len(copies)], device_id={"pair": partner}, device_id_type=MESH
    )
    to_partner.start()
    to_partner.wait()
    mid_out.wait()
    edge = acc[...] + pacc[...]
    mids = acc_mid.shape[0]
    o_ref[pl.ds(0, MID_FIRST), :] = edge[0:MID_FIRST, 0:breadth]
    o_ref[pl.ds(MID_FIRST, mids), :] = (acc_mid[...] + pacc_mid[...])[:, 0:breadth]
    o_ref[pl.ds(MID_FIRST + mids, height - MID_FIRST - mids), :] = edge[MID_FIRST:, 0:breadth]


def fused(wave_states, lat_faces, lon_faces, scalars, nlon_cells):
    slots, fields, height, breadth = wave_states.shape
    nfield = slots * fields
    count = nfield + 2
    rows = height + 2 * TOP
    smem = pl.BlockSpec(memory_space=pltpu.SMEM)
    vmem = pl.BlockSpec(memory_space=pltpu.VMEM)
    per_row = 128 // (2 * HALO)
    coef_rows = STRIP * ((height // STRIP + per_row - 1) // per_row)
    packed_b = pltpu.VMEM((height // 2, 128), jnp.bfloat16)
    packed_c = pltpu.VMEM((coef_rows, 128), jnp.float32)
    strip_b16 = pltpu.VMEM((nfield // 4, 2 * STRIP, COLS), jnp.bfloat16)
    strip_c = pltpu.VMEM((STRIP, COLS), jnp.float32)
    plane = pltpu.VMEM((rows, COLS), jnp.float32)
    return pl.pallas_call(
        functools.partial(fused_kernel, nlon_cells),
        out_shape=jax.ShapeDtypeStruct((height, breadth), jnp.float32),
        in_specs=[smem] * 5 + [pl.BlockSpec(memory_space=pl.ANY)] * 3,
        out_specs=vmem,
        scratch_shapes=[
            pltpu.VMEM(wave_states.shape, wave_states.dtype),
            pltpu.VMEM(lat_faces.shape, jnp.float32),
            pltpu.VMEM(lon_faces.shape, jnp.float32),
            pltpu.SemaphoreType.DMA((slots + 2,)),
            pltpu.VMEM((2, 4, 2, STRIP, COLS), jnp.float32),
            pltpu.VMEM((count, rows, COLS), jnp.float32),
            pltpu.VMEM((slots, 2, rows, COLS), jnp.float32),
            plane,
            plane,
            plane,
            pltpu.VMEM((2 * MID_FIRST, COLS), jnp.float32),
            pltpu.VMEM((2 * MID_FIRST, COLS), jnp.float32),
            pltpu.VMEM((height - 2 * MID_FIRST, COLS), jnp.float32),
            pltpu.VMEM((height - 2 * MID_FIRST, COLS), jnp.float32),
            pltpu.VMEM((height, 128), jnp.float32),
            pltpu.VMEM((height, 128), jnp.float32),
        ]
        + [packed_b, packed_b, packed_c, packed_c, strip_b16, strip_b16, strip_c, strip_c] * 2
        + [
            pltpu.VMEM((4, STRIP, 128), jnp.float32),
            pltpu.SemaphoreType.DMA((14,)),
            pltpu.SemaphoreType.DMA((14,)),
        ],
        compiler_params=pltpu.CompilerParams(collective_id=0, has_side_effects=True, vmem_limit_bytes=60 * 1024 * 1024),
    )(*scalars, wave_states, lat_faces, lon_faces)


def body(
    wave_states,
    pair_list,
    pair_counts,
    residuals,
    station_cell,
    source_wavelet,
    lat_faces,
    lon_faces,
):
    height, breadth = lat_faces.shape
    nlon_cells = breadth * lax.axis_size("lon")
    scalars = (pair_list.T, pair_counts, residuals.T, station_cell, source_wavelet)
    return fused(wave_states, lat_faces, lon_faces, scalars, nlon_cells)


def solution(mesh):
    in_specs = (
        P("pair", None, "lat", "lon"),
        P(),
        P(),
        P(),
        P(),
        P(),
        P("lat", "lon"),
        P("lat", "lon"),
    )
    out_specs = P("lat", "lon")
    return jax.shard_map(body, mesh=mesh, in_specs=in_specs, out_specs=out_specs, check_vma=False)
```

```python
import functools

import jax
import jax.numpy as jnp
from jax import lax
from jax.experimental import pallas as pl
from jax.experimental.pallas import tpu as pltpu
from jax.sharding import PartitionSpec as P

HALO = 4
TOP = 16
COLS = 512
STRIP = 8
MESH = pl.DeviceIdType.MESH
TL, TR, BL, BR = 0, 1, 2, 3
MID_FIRST = 32


def fused_kernel(
    nlon_cells,
    pl_ref, pc_ref, res_ref, sc_ref, wav_ref,
    f_hbm, lat_hbm, lon_hbm,
    o_ref,
    f_ref, lat_ref, lon_ref, in_sem, src_tiles,
    X, work, ca, cw, cd, acc, pacc, acc_mid, pacc_mid,
    pack_l, pack_r,
    send_lb, send_rb, send_lc, send_rc, send_tb, send_bb, send_tc, send_bc,
    rlb, rrb, rlc, rrc, rab, rbb, rac, rbc, rc,
    send_sem, recv_sem,
):
    slots, fields, height, breadth = f_ref.shape
    nfield = slots * fields
    count = nfield + 2
    rows = X.shape[1]
    blocks = rows // 8
    steps = wav_ref.shape[0]
    nlon = lax.axis_size("lon")
    nlat = lax.axis_size("lat")
    me_lat = lax.axis_index("lat")
    me_lon = lax.axis_index("lon")
    member = lax.axis_index("pair")
    partner = 1 - member
    right = lax.rem(me_lon + 1, nlon)
    left = lax.rem(me_lon + nlon - 1, nlon)
    has_up = me_lat > 0
    has_down = me_lat < nlat - 1
    up = jnp.maximum(me_lat - 1, 0)
    down = jnp.minimum(me_lat + 1, nlat - 1)
    cn = X.at[nfield]
    ce = X.at[nfield + 1]

    barrier = pltpu.get_barrier_semaphore()
    pl.semaphore_signal(barrier, 1, device_id={"pair": partner}, device_id_type=MESH)
    for lon_to in (left, right):
        pl.semaphore_signal(barrier, 1, device_id={"lon": lon_to}, device_id_type=MESH)

    @pl.when(has_up)
    def _():
        for lon_to in (me_lon, left, right):
            pl.semaphore_signal(barrier, 1, device_id={"lat": up, "lon": lon_to}, device_id_type=MESH)

    @pl.when(has_down)
    def _():
        for lon_to in (me_lon, left, right):
            pl.semaphore_signal(barrier, 1, device_id={"lat": down, "lon": lon_to}, device_id_type=MESH)

    loads = [pltpu.make_async_copy(f_hbm.at[i], f_ref.at[i], in_sem.at[i]) for i in range(slots)]
    loads.append(pltpu.make_async_copy(lat_hbm, lat_ref, in_sem.at[slots]))
    loads.append(pltpu.make_async_copy(lon_hbm, lon_ref, in_sem.at[slots + 1]))
    for copy in loads:
        copy.start()

    lane = lax.broadcasted_iota(jnp.int32, (height, 128), 1)
    quad = lane // HALO
    sub8 = lax.broadcasted_iota(jnp.int32, (STRIP, COLS), 0)
    lane8 = lax.broadcasted_iota(jnp.int32, (STRIP, 128), 1)
    sub_c = lax.broadcasted_iota(jnp.int32, (STRIP, 128), 0)
    lane_w = lax.broadcasted_iota(jnp.int32, (STRIP, COLS), 1)
    zero_rows = jnp.zeros((TOP, COLS), jnp.float32)

    for a in range(count):
        if a % fields == 0 and a < nfield:
            loads[a // fields].wait()
        if a == nfield:
            loads[slots].wait()
            loads[slots + 1].wait()
        if a < nfield:
            raw = f_ref[a // fields, a % fields].astype(jnp.float32)
            if a % 2 == 0:
                live = a // fields < pc_ref[member]
                raw = raw * jnp.where(live, jnp.float32(1.0), jnp.float32(0.0))
        else:
            raw = (lat_ref if a == nfield else lon_ref)[...]
        X[a, pl.ds(TOP, height), pl.ds(0, breadth)] = raw
        tail = X[a, pl.ds(TOP, height), pl.ds(384, 128)]
        X[a, pl.ds(TOP, height), pl.ds(384, 128)] = jnp.where(lane < breadth - 384, tail, jnp.float32(0.0))
        X[a, pl.ds(0, TOP), :] = zero_rows
        X[a, pl.ds(TOP + height, rows - TOP - height), :] = zero_rows

    @pl.when(me_lat == nlat - 1)
    def _():
        last = TOP + height - 8
        cn[pl.ds(last, 8), :] = jnp.where(sub8 == 7, jnp.float32(0.0), cn[pl.ds(last, 8), :])

    pl_acc = jnp.zeros((height, 128), jnp.float32)
    pr_acc = jnp.zeros((height, 128), jnp.float32)
    for a in range(count):
        head = X[a, pl.ds(TOP, height), pl.ds(0, 128)]
        tail = X[a, pl.ds(TOP, height), pl.ds(384, 128)]
        pl_acc = jnp.where(quad == a, pltpu.roll(head, (HALO * a) % 128, 1), pl_acc)
        pr_acc = jnp.where(quad == a, pltpu.roll(tail, (HALO * a - (breadth - 384 - HALO)) % 128, 1), pr_acc)
    pack_l[...] = pl_acc
    pack_r[...] = pr_acc

    coef_lane = HALO * nfield
    width = 2 * HALO
    per_row = 128 // width
    half = height // 2
    lane_h = lax.broadcasted_iota(jnp.int32, (half, 128), 1)
    for src, dst in ((pl_acc, send_lb), (pr_acc, send_rb)):
        folded = jnp.where(lane_h < coef_lane, src[0:half], pltpu.roll(src[half:height], coef_lane, 1))
        dst[...] = folded.astype(jnp.bfloat16)
    for src, dst in ((pl_acc, send_lc), (pr_acc, send_rc)):
        for h in range(dst.shape[0] // STRIP):
            packed = jnp.zeros((STRIP, 128), jnp.float32)
            for g in range(per_row):
                i = h * per_row + g
                if i * STRIP >= height:
                    break
                blk = src[i * STRIP : (i + 1) * STRIP]
                packed = jnp.where(lane8 // width == g, pltpu.roll(blk, (width * g - coef_lane) % 128, 1), packed)
            dst[pl.ds(h * STRIP, STRIP), :] = packed

    def strip_pair(a, first, keep_low):
        lo = X[a, pl.ds(first, STRIP), :]
        hi = X[a + 1, pl.ds(first, STRIP), :]
        if keep_low:
            return jnp.where(sub8 < 4, lo, pltpu.roll(hi, 4, 0))
        return jnp.where(sub8 < 4, pltpu.roll(lo, 4, 0), hi)

    for dst_b, dst_c, first, keep_low in (
        (send_tb, send_tc, TOP, True),
        (send_bb, send_bc, TOP + height - STRIP, False),
    ):
        for j in range(dst_b.shape[0]):
            both = [strip_pair(4 * j, first, keep_low), strip_pair(4 * j + 2, first, keep_low)]
            dst_b[j] = jnp.concatenate(both, axis=0).astype(jnp.bfloat16)
        dst_c[...] = strip_pair(nfield, first, keep_low)

    acc[...] = jnp.zeros_like(acc)
    acc_mid[...] = jnp.zeros_like(acc_mid)
    src_tiles[:, :, 0] = jnp.zeros((2, steps, STRIP, COLS), jnp.float32)

    pl.semaphore_wait(barrier, 3 + 3 * has_up.astype(jnp.int32) + 3 * has_down.astype(jnp.int32))

    last8 = pl.ds(height - STRIP, STRIP)
    first8 = pl.ds(0, STRIP)
    copies = [
        (send_rb, rlb, me_lat, right, None),
        (send_rc, rlc, me_lat, right, None),
        (send_lb, rrb, me_lat, left, None),
        (send_lc, rrc, me_lat, left, None),
        (send_tb, rbb, up, me_lon, "up"),
        (send_tc, rbc, up, me_lon, "up"),
        (send_bb, rab, down, me_lon, "down"),
        (send_bc, rac, down, me_lon, "down"),
        (pack_r.at[last8], rc.at[TL], down, right, "down"),
        (pack_l.at[last8], rc.at[TR], down, left, "down"),
        (pack_r.at[first8], rc.at[BL], up, right, "up"),
        (pack_l.at[first8], rc.at[BR], up, left, "up"),
    ]

    def descriptor(i):
        src, dst, lat_to, lon_to, _ = copies[i]
        return pltpu.make_async_remote_copy(
            src, dst, send_sem.at[i], recv_sem.at[i], device_id={"lat": lat_to, "lon": lon_to}, device_id_type=MESH
        )

    def when(cond, fn):
        if cond is None:
            fn()
        else:
            pl.when(has_up if cond == "up" else has_down)(fn)

    def finish(i):
        cond = copies[i][4]
        when(cond, lambda: descriptor(i).wait_send())
        mirror = {None: None, "up": "down", "down": "up"}[cond]
        when(mirror, lambda: descriptor(i).wait_recv())

    for i in list(range(4, len(copies))) + list(range(4)):
        when(copies[i][4], lambda i=i: descriptor(i).start())

    for i in range(4):
        finish(i)
    east_gap = (lane >= breadth - 384) & (lane < breadth - 384 + HALO)
    west_gap = lane >= 128 - HALO
    unpacked = []
    for src_b, src_c in ((rlb, rlc), (rrb, rrc)):
        folded = src_b[...].astype(jnp.float32)
        fields_part = jnp.concatenate([folded, pltpu.roll(folded, 128 - coef_lane, 1)], axis=0)
        parts = []
        for i in range(height // STRIP):
            h, g = divmod(i, per_row)
            blk_c = pltpu.roll(src_c[pl.ds(h * STRIP, STRIP), :], (coef_lane - width * g) % 128, 1)
            blk_f = fields_part[i * STRIP : (i + 1) * STRIP]
            parts.append(jnp.where(lane8 < coef_lane, blk_f, blk_c))
        unpacked.append(jnp.concatenate(parts, axis=0))
    from_l, from_r = unpacked
    for a in range(count):
        east_shift = (breadth - 384 - HALO * a) % 128
        west_shift = (128 - HALO - HALO * a) % 128
        tail = X[a, pl.ds(TOP, height), pl.ds(384, 128)]
        tail = jnp.where(east_gap, pltpu.roll(from_r, east_shift, 1), tail)
        tail = jnp.where(west_gap, pltpu.roll(from_l, west_shift, 1), tail)
        X[a, pl.ds(TOP, height), pl.ds(384, 128)] = tail

    def derive(first, size):
        ca[pl.ds(first, size), :] = cn[pl.ds(first - 1, size), :]
        cw[pl.ds(first, size), :] = pltpu.roll(ce[pl.ds(first, size), :], 1, 1)
        cd[pl.ds(first, size), :] = 2.0 - (
            cn[pl.ds(first, size), :] + ca[pl.ds(first, size), :] + ce[pl.ds(first, size), :] + cw[pl.ds(first, size), :]
        )

    derive(8, rows - 16)

    def slot_places(s):
        slot = member * slots + s
        act = jnp.where(s < pc_ref[member], jnp.float32(1.0), jnp.float32(0.0))
        row_first = me_lat * height
        col_first = me_lon * breadth
        places = []
        for comp in range(2):
            cell = sc_ref[pl_ref[comp, slot]]
            r = lax.div(cell, nlon_cells)
            c = cell - r * nlon_cells
            rb = r - row_first + TOP
            d = c - col_first
            d = jnp.where(d < 0, d + nlon_cells, d)
            near = d < breadth + HALO
            wrap = d >= nlon_cells - HALO
            cb = jnp.where(near, d, d - nlon_cells + COLS)
            valid = (rb >= TOP - HALO) & (rb < TOP + height + HALO) & (near | wrap)
            hit = (sub8 == lax.rem(jnp.maximum(rb, 0), 8)) & (lane_w == cb)
            for t in range(steps):
                amp = wav_ref[t] * act if comp == 0 else res_ref[steps - 1 - t, slot]
                src_tiles[comp, t, 1] = jnp.where(hit, amp, jnp.float32(0.0))
            places.append((rb, valid))
        return act, places

    def run_blocks(s, t, block_list, act, places):
        bufs = [(X.at[s * fields + comp], X.at[s * fields + 2 + comp], work.at[s, comp]) for comp in range(2)]
        ei, ci, ni = t % 3, (t + 1) % 3, (t + 2) % 3
        for k in block_list:
            r0 = 8 * k
            dd = cd[pl.ds(r0, 8), :]
            nn = cn[pl.ds(r0, 8), :]
            aa = ca[pl.ds(r0, 8), :]
            ee = ce[pl.ds(r0, 8), :]
            ww = cw[pl.ds(r0, 8), :]
            outs = []
            for comp in range(2):
                rb, valid = places[comp]
                pick = (valid & (rb >= r0) & (rb < r0 + 8)).astype(jnp.int32)
                cur_ref, ear_ref, nxt_ref = bufs[comp][ci], bufs[comp][ei], bufs[comp][ni]
                cur = cur_ref[pl.ds(r0, 8), :]
                above = cur_ref[pl.ds(r0 - 1, 8), :]
                below = cur_ref[pl.ds(r0 + 1, 8), :]
                ear = ear_ref[pl.ds(r0, 8), :]
                west = pltpu.roll(cur, 1, 1)
                east = pltpu.roll(cur, COLS - 1, 1)
                nxt = dd * cur + nn * below + aa * above + ee * east + ww * west - ear
                nxt = nxt + src_tiles[comp, t, pick]
                nxt_ref[pl.ds(r0, 8), :] = nxt
                outs.append(nxt)
            if 2 <= k < blocks - 2:
                row = r0 - TOP
                if MID_FIRST <= row < MID_FIRST + acc_mid.shape[0]:
                    dst, row = acc_mid, row - MID_FIRST
                else:
                    dst, row = acc, (row if row < MID_FIRST else row - acc_mid.shape[0])
                dst[pl.ds(row, 8), :] += outs[0] * outs[1]

    def phase(ranges):
        def body(s, carry):
            act, places = slot_places(s)
            for t in range(steps):
                run_blocks(s, t, ranges(t), act, places)
            return carry

        lax.fori_loop(0, slots, body, 0)

    inner = lambda t: list(range(3 + t, blocks - 3 - t))
    phase(inner)

    mid_out = pltpu.make_async_remote_copy(
        acc_mid, pacc_mid, send_sem.at[len(copies) + 1], recv_sem.at[len(copies) + 1],
        device_id={"pair": partner}, device_id_type=MESH,
    )
    mid_out.start()

    for i in range(4, len(copies)):
        finish(i)

    @pl.when(jnp.logical_not(has_up))
    def _():
        rab[...] = jnp.zeros_like(rab)
        rac[...] = jnp.zeros_like(rac)
        rc[TL] = jnp.zeros((STRIP, 128), jnp.float32)
        rc[TR] = jnp.zeros((STRIP, 128), jnp.float32)

    @pl.when(jnp.logical_not(has_down))
    def _():
        rbb[...] = jnp.zeros_like(rbb)
        rbc[...] = jnp.zeros_like(rbc)
        rc[BL] = jnp.zeros((STRIP, 128), jnp.float32)
        rc[BR] = jnp.zeros((STRIP, 128), jnp.float32)

    east_c = (lane8 >= breadth - 384) & (lane8 < breadth - 384 + HALO)
    west_c = lane8 >= 128 - HALO
    for src_b, src_c, first, low_half, (c_east, c_west) in (
        (rab, rac, TOP - STRIP, False, (TR, TL)),
        (rbb, rbc, TOP + height, True, (BR, BL)),
    ):
        for a in range(count):
            b = a // 2
            if a < nfield:
                both = src_b[b // 2].astype(jnp.float32)
                blk = both[STRIP * (b % 2) : STRIP * (b % 2 + 1)]
            else:
                blk = src_c[...]
            even = a % 2 == 0
            if low_half:
                blk = blk if even else pltpu.roll(blk, 4, 0)
                blk = jnp.where(sub8 < 4, blk, jnp.float32(0.0))
                band = sub_c < 4
            else:
                blk = pltpu.roll(blk, 4, 0) if even else blk
                blk = jnp.where(sub8 >= 4, blk, jnp.float32(0.0))
                band = sub_c >= 4
            X[a, pl.ds(first, STRIP), :] = blk
            east_shift = (breadth - 384 - HALO * a) % 128
            west_shift = (128 - HALO - HALO * a) % 128
            tail = X[a, pl.ds(first, STRIP), pl.ds(384, 128)]
            tail = jnp.where(band & east_c, pltpu.roll(rc[c_east], east_shift, 1), tail)
            tail = jnp.where(band & west_c, pltpu.roll(rc[c_west], west_shift, 1), tail)
            X[a, pl.ds(first, STRIP), pl.ds(384, 128)] = tail

    derive(8, 24)
    derive(rows - 32, 24)

    def outer(t):
        if t < steps - 1:
            return list(range(1, 3 + t)) + list(range(blocks - 3 - t, blocks - 1))
        return list(range(2, 3 + t)) + list(range(blocks - 3 - t, blocks - 2))

    phase(outer)

    to_partner = pltpu.make_async_remote_copy(
        acc, pacc, send_sem.at[len(copies)], recv_sem.at[len(copies)], device_id={"pair": partner}, device_id_type=MESH
    )
    to_partner.start()
    to_partner.wait()
    mid_out.wait()
    edge = acc[...] + pacc[...]
    mids = acc_mid.shape[0]
    o_ref[pl.ds(0, MID_FIRST), :] = edge[0:MID_FIRST, 0:breadth]
    o_ref[pl.ds(MID_FIRST, mids), :] = (acc_mid[...] + pacc_mid[...])[:, 0:breadth]
    o_ref[pl.ds(MID_FIRST + mids, height - MID_FIRST - mids), :] = edge[MID_FIRST:, 0:breadth]


def fused(wave_states, lat_faces, lon_faces, scalars, nlon_cells):
    slots, fields, height, breadth = wave_states.shape
    nfield = slots * fields
    count = nfield + 2
    rows = height + 2 * TOP
    smem = pl.BlockSpec(memory_space=pltpu.SMEM)
    vmem = pl.BlockSpec(memory_space=pltpu.VMEM)
    per_row = 128 // (2 * HALO)
    coef_rows = STRIP * ((height // STRIP + per_row - 1) // per_row)
    packed_b = pltpu.VMEM((height // 2, 128), jnp.bfloat16)
    packed_c = pltpu.VMEM((coef_rows, 128), jnp.float32)
    strip_b16 = pltpu.VMEM((nfield // 4, 2 * STRIP, COLS), jnp.bfloat16)
    strip_c = pltpu.VMEM((STRIP, COLS), jnp.float32)
    plane = pltpu.VMEM((rows, COLS), jnp.float32)
    return pl.pallas_call(
        functools.partial(fused_kernel, nlon_cells),
        out_shape=jax.ShapeDtypeStruct((height, breadth), jnp.float32),
        in_specs=[smem] * 5 + [pl.BlockSpec(memory_space=pl.ANY)] * 3,
        out_specs=vmem,
        scratch_shapes=[
            pltpu.VMEM(wave_states.shape, wave_states.dtype),
            pltpu.VMEM(lat_faces.shape, jnp.float32),
            pltpu.VMEM(lon_faces.shape, jnp.float32),
            pltpu.SemaphoreType.DMA((slots + 2,)),
            pltpu.VMEM((2, 4, 2, STRIP, COLS), jnp.float32),
            pltpu.VMEM((count, rows, COLS), jnp.float32),
            pltpu.VMEM((slots, 2, rows, COLS), jnp.float32),
            plane,
            plane,
            plane,
            pltpu.VMEM((2 * MID_FIRST, COLS), jnp.float32),
            pltpu.VMEM((2 * MID_FIRST, COLS), jnp.float32),
            pltpu.VMEM((height - 2 * MID_FIRST, COLS), jnp.float32),
            pltpu.VMEM((height - 2 * MID_FIRST, COLS), jnp.float32),
            pltpu.VMEM((height, 128), jnp.float32),
            pltpu.VMEM((height, 128), jnp.float32),
        ]
        + [packed_b, packed_b, packed_c, packed_c, strip_b16, strip_b16, strip_c, strip_c] * 2
        + [
            pltpu.VMEM((4, STRIP, 128), jnp.float32),
            pltpu.SemaphoreType.DMA((14,)),
            pltpu.SemaphoreType.DMA((14,)),
        ],
        compiler_params=pltpu.CompilerParams(collective_id=0, has_side_effects=True, vmem_limit_bytes=60 * 1024 * 1024),
    )(*scalars, wave_states, lat_faces, lon_faces)


def body(
    wave_states,
    pair_list,
    pair_counts,
    residuals,
    station_cell,
    source_wavelet,
    lat_faces,
    lon_faces,
):
    height, breadth = lat_faces.shape
    nlon_cells = breadth * lax.axis_size("lon")
    scalars = (pair_list.T, pair_counts, residuals.T, station_cell, source_wavelet)
    return fused(wave_states, lat_faces, lon_faces, scalars, nlon_cells)


def solution(mesh):
    in_specs = (
        P("pair", None, "lat", "lon"),
        P(),
        P(),
        P(),
        P(),
        P(),
        P("lat", "lon"),
        P("lat", "lon"),
    )
    out_specs = P("lat", "lon")
    return jax.shard_map(body, mesh=mesh, in_specs=in_specs, out_specs=out_specs, check_vma=False)
```
